32 devices in a mesh: dp: 8 (over z, x), tensor: 4 (over y, core).
Axes of the slice: x: 2, y: 2, z: 4, core: 2. Of those that a mesh axis runs over, the one named last changes fastest.
Arguments:
- hidden_in: bfloat16 [10240, 2048], P(('dp', 'tensor')), may hold values from -6 to 6
- cotangent: bfloat16 [10240, 2048], P(('dp', 'tensor')), may hold values from -6 to 6
- gain_attn: float32 [2048], replicated, may hold values from 0.1 to 1.9
- w_query: bfloat16 [2048, 2048], P(None, 'tensor'), may hold values from -0.125 to 0.125
- w_key: bfloat16 [2048, 2048], P(None, 'tensor'), may hold values from -0.125 to 0.125
- w_value: bfloat16 [2048, 2048], P(None, 'tensor'), may hold values from -0.125 to 0.125
- w_out: bfloat16 [2048, 2048], P('tensor'), may hold values from -1 to 1
- gain_mlp: float32 [2048], replicated, may hold values from 0.1 to 1.9
- w_gate: bfloat16 [2048, 5632], P(None, 'tensor'), may hold values from -0.125 to 0.125
- w_up: bfloat16 [2048, 5632], P(None, 'tensor'), may hold values from -0.125 to 0.125
- w_down: bfloat16 [5632, 2048], P('tensor'), may hold values from -0.078125 to 0.078125
- doc_lengths: int32 [8, 3], P('dp'), may hold values from 1 to 1024, as said below
- doc_groups: int32 [8, 3], P('dp'), may hold values from 0 to 7
- pad_mask: int32 [8, 1280], P('dp'), may hold values from 0 to 1, as said below
Outputs:
- output: bfloat16 [10240, 2048], P(('dp', 'tensor'))
- grad_input: float32 [10240, 2048], P(('dp', 'tensor'))
- grad_gain_attn: float32 [2048], P('dp')
- grad_w_query: float32 [2048, 2048], P('dp', 'tensor')
- grad_w_key: float32 [2048, 2048], P('dp', 'tensor')
- grad_w_value: float32 [2048, 2048], P('dp', 'tensor')
- grad_w_out: float32 [2048, 2048], P('tensor', 'dp')
- grad_gain_mlp: float32 [2048], P('dp')
- grad_w_gate: float32 [2048, 5632], P('dp', 'tensor')
- grad_w_up: float32 [2048, 5632], P('dp', 'tensor')
- grad_w_down: float32 [5632, 2048], P('tensor', 'dp')
The draws below stay inside these ranges and needn't reach their ends.
Inputs may be any that keep to these rules, and one draw needn't show every extreme that they name: `doc_lengths`: A row's document lengths sum to 1280; every row holds one document of exactly 1024 tokens and the others are shorter. `pad_mask`: the first token of every document is real; padding lies only at a document's end, fewer than half of its tokens.
All inputs are finite; a program needn't handle non-finite values.
Results may differ from the reference program's by a relative error of at most 0.015.
Values may be sent and summed in bfloat16 or wider, within the bound.
A program may use at most 320 MiB of HBM per device.

```python
import math
import jax
import jax.numpy as jnp
import numpy as np
from jax import lax

D = 2048
HEADS = 16
HEAD_DIM = 128
FF = 5632
ROWS = 1280
QBLOCK = 640
DOCS = 3
GROUPS = 8
BATCH = 8
TOKENS = 10240
LONGEST = 1024


def layout_row(row_key):
    key_cuts, key_slot, key_pads = jax.random.split(row_key, 3)
    spare = ROWS // 5
    cuts = jnp.sort(jax.random.permutation(key_cuts, spare - 1)[:DOCS - 2].astype(jnp.int32) + 1)
    edges = jnp.concatenate([jnp.zeros((1,), jnp.int32), cuts, jnp.full((1,), spare, jnp.int32)])
    others = edges[1:] - edges[:-1]
    chosen = jax.random.randint(key_slot, (), 0, DOCS)
    places = jnp.arange(DOCS, dtype=jnp.int32)
    source = jnp.clip(places - (places > chosen).astype(jnp.int32), 0, DOCS - 2)
    lengths = jnp.where(places == chosen, LONGEST, others[source]).astype(jnp.int32)
    pad_draws = jax.random.randint(key_pads, (DOCS,), 0, 65536)
    padding = pad_draws * lengths // 131072
    starts = jnp.cumsum(lengths) - lengths
    token_idx = jnp.arange(ROWS, dtype=jnp.int32)
    doc_index = jnp.sum((token_idx[:, None] >= starts[None, 1:]).astype(jnp.int32), axis=1)
    onehot = doc_index[:, None] == places[None, :]
    inside = token_idx - jnp.sum(jnp.where(onehot, starts[None, :], 0), axis=1)
    keep_len = jnp.sum(jnp.where(onehot, (lengths - padding)[None, :], 0), axis=1)
    return (lengths, (inside < keep_len).astype(jnp.int32))


def doc_layout(key):
    base_key = jax.random.fold_in(key, 11)
    row_keys = jax.random.split(base_key, BATCH)
    return jax.vmap(layout_row)(row_keys)


def draw_doc_lengths(key, part):
    return doc_layout(key)[0]


def draw_pad_mask(key, part):
    return doc_layout(key)[1]


def with_ends(array, rng, smallest, largest):
    shape = array.shape
    place = [jax.random.randint(jax.random.fold_in(rng, axis), (), 0, shape[axis]) for axis in range(len(shape))]
    array = array.at[tuple(place)].set(smallest)
    longest = shape.index(max(shape))
    place[longest] = (place[longest] + 1) % shape[longest]
    return array.at[tuple(place)].set(largest)


def with_spikes(values, key, source, target, parts, factor):
    owner, partner = [(jnp.arange(values.shape[axis_at]) // (values.shape[axis_at] // parts)).reshape([-1 if axis == axis_at else 1 for axis in range(values.ndim)]) for axis_at in (source, target)]
    chosen = jax.random.permutation(key, parts)[partner]
    strong = (owner == chosen) | (owner == (partner + parts // 2) % parts)
    return jnp.where(strong, factor * values, values)


def shard_levels(rng, dims, shards, least, largest):
    level, own = 1.0, jax.random.fold_in(rng, 6)
    for dim, blocks in shards:
        steps = jnp.exp(jax.random.uniform(jax.random.fold_in(own, dim), (blocks,), jnp.float32, least / len(shards), largest / len(shards)))
        level = level * jnp.repeat(steps, dims[dim] // blocks).reshape([-1 if axis == dim else 1 for axis in range(len(dims))])
    return level


def rank_table(amount, lean):
    loads = [(1 << 20) // math.isqrt(standing ** lean) + 1 for standing in range(1, amount + 1)]
    scale = 1 + sum(loads) // (1 << 30)
    return np.cumsum(np.array([max(1, weight // scale) for weight in loads]))


def skewed_ids(rng, extent, number_of, slope):
    grid = rank_table(number_of, slope)
    ticket = jax.random.randint(jax.random.fold_in(rng, 1), extent, 0, int(grid[number_of - 1]))
    rank = jnp.searchsorted(jnp.asarray(grid, jnp.int32), ticket, side="right")
    return jax.random.permutation(jax.random.fold_in(rng, 2), number_of)[rank].astype(jnp.int32)


def gaussian(rng, extent, width, reach, pieces=(), held_as=jnp.bfloat16):
    loudness = shard_levels(rng, extent, pieces, -0.22, 0.18) if pieces else 1.0
    drawn = jax.random.normal(rng, extent, jnp.float32) * width * loudness
    return jnp.minimum(jnp.maximum(drawn, -reach), reach).astype(held_as)


def noise_with(rng, dims, deviation, limit, pieces, heavy, held_as=jnp.bfloat16):
    drawn = deviation * jax.random.normal(rng, dims, jnp.float32)
    if pieces:
        drawn = drawn * shard_levels(rng, dims, pieces, -0.22, 0.18)
    return jnp.clip(with_spikes(drawn, jax.random.fold_in(rng, 3), *heavy), -limit, limit).astype(held_as)


def setup_inputs(seed: int = 0) -> dict:
    key_list = jax.random.split(jax.random.key(seed), 15)
    hidden_in = noise_with(key_list[0], (TOKENS, D), 1.0, 6.0, ((0, 32),), (0, 1, 32, 2.75))
    cotangent = noise_with(key_list[1], (TOKENS, D), 1.0, 6.0, ((0, 32),), (0, 1, 32, 2.75))
    gain_attn = jnp.clip(1.0 + 0.18 * jax.random.normal(key_list[2], (D,), jnp.float32), 0.1, 1.9)
    w_query = gaussian(key_list[3], (D, D), D ** -0.5, 0.125, ((1, 4),))
    w_key = gaussian(key_list[4], (D, D), D ** -0.5, 0.125, ((1, 4),))
    w_value = gaussian(key_list[5], (D, D), D ** -0.5, 0.125, ((1, 4),))
    w_out = gaussian(key_list[6], (D, D), (D // 64) ** -0.5, 1.0, ((0, 4),))
    gain_mlp = jnp.clip(1.0 + 0.18 * jax.random.normal(key_list[7], (D,), jnp.float32), 0.1, 1.9)
    w_gate = gaussian(key_list[8], (D, FF), D ** -0.5, 0.125, ((1, 4),))
    w_up = gaussian(key_list[9], (D, FF), D ** -0.5, 0.125, ((1, 4),))
    w_down = gaussian(key_list[10], (FF, D), FF ** -0.5, 0.078125, ((0, 4),))
    doc_lengths = draw_doc_lengths(jax.random.fold_in(key_list[14], 71), 0)
    doc_groups = with_ends(skewed_ids(key_list[12], (BATCH, DOCS), GROUPS, 1), jax.random.fold_in(key_list[12], 3), 0, GROUPS - 1).astype(jnp.int32)
    pad_mask = draw_pad_mask(jax.random.fold_in(key_list[14], 71), 0)
    return dict(hidden_in=hidden_in, cotangent=cotangent, gain_attn=gain_attn, w_query=w_query, w_key=w_key, w_value=w_value, w_out=w_out, gain_mlp=gain_mlp, w_gate=w_gate, w_up=w_up, w_down=w_down, doc_lengths=doc_lengths, doc_groups=doc_groups, pad_mask=pad_mask)


epsilon = 1e-05
masked_score = -1e+30
rope_base = 10000.0

@jax.custom_vjp
def low(v):
    return lax.optimization_barrier(v.astype(jnp.bfloat16)).astype(jnp.float32)

@jax.custom_vjp
def low_back(v):
    return v

def low_keep(v):
    return (low(v), None)

def low_pass(kept, grad):
    return (grad,)

def back_keep(v):
    return (v, None)

def back_low(kept, grad):
    return (low(grad),)
low.defvjp(low_keep, low_pass)
low_back.defvjp(back_keep, back_low)

def matmul_hi(left, right):
    return jnp.dot(left, right, precision=lax.Precision.HIGHEST, preferred_element_type=jnp.float32)

def row_tables(length_row, group_row):
    length_row = length_row.astype(jnp.int32)
    starts = (jnp.cumsum(length_row) - length_row).astype(jnp.int32)
    token_idx = jnp.arange(ROWS, dtype=jnp.int32)
    doc_index = lax.optimization_barrier(jnp.sum((token_idx[:, None] >= starts[None, 1:]).astype(jnp.int32), axis=1)).astype(jnp.int32)
    onehot = doc_index[:, None] == jnp.arange(DOCS, dtype=jnp.int32)[None, :]
    inside = (token_idx - lax.optimization_barrier(jnp.sum(jnp.where(onehot, starts[None, :], 0), axis=1))).astype(jnp.int32)
    group_tok = lax.optimization_barrier(jnp.sum(jnp.where(onehot, group_row.astype(jnp.int32)[None, :], 0), axis=1)).astype(jnp.int32)
    return (doc_index, inside, group_tok)

def rope_tables(inside):
    freq = rope_base ** (-jnp.arange(0, HEAD_DIM // 2, dtype=jnp.float32) * 2.0 / HEAD_DIM)
    angle = inside.astype(jnp.float32)[:, None] * freq[None, :]
    return (jnp.cos(angle)[:, None, :], jnp.sin(angle)[:, None, :])

def rotate(values, cosine, sine):
    half = values.shape[-1] // 2
    first, second = (values[..., :half], values[..., half:])
    return jnp.concatenate([first * cosine - second * sine, second * cosine + first * sine], axis=-1)

def block_row(xrow, params, doc_index, inside, keymask):
    gain_a, wq_f, wk_f, wv_f, wo_f, gain_m, wg_f, wu_f, wd_f = params
    score_scale = HEAD_DIM ** (-0.5)
    inv_a = lax.rsqrt(lax.optimization_barrier(jnp.mean(xrow * xrow, axis=-1, keepdims=True)) + epsilon)
    normed_a = low(xrow * inv_a * gain_a)
    cosine, sine = rope_tables(inside)
    query = low(rotate(low_back(matmul_hi(normed_a, wq_f)).reshape(ROWS, HEADS, HEAD_DIM), cosine, sine))
    key_vec = low(rotate(low_back(matmul_hi(normed_a, wk_f)).reshape(ROWS, HEADS, HEAD_DIM), cosine, sine))
    value = low(low_back(matmul_hi(normed_a, wv_f))).reshape(ROWS, HEADS, HEAD_DIM)
    token_idx = jnp.arange(ROWS, dtype=jnp.int32)
    num_blocks = ROWS // QBLOCK

    def attend(inputs):
        query_blk, query_doc, query_tok = inputs
        raw = low_back(jnp.einsum('qhd,khd->hqk', query_blk, key_vec, precision=lax.Precision.HIGHEST))
        allowed = (query_doc[:, None] == doc_index[None, :]) & (query_tok[:, None] >= token_idx[None, :]) & (keymask[None, :] > 0.5)
        scores = jnp.where(allowed[None], raw * score_scale, masked_score)
        top_val = lax.optimization_barrier(jnp.max(scores, axis=-1, keepdims=True))
        log_total = top_val + jnp.log(lax.optimization_barrier(jnp.sum(jnp.exp(scores - top_val), axis=-1, keepdims=True)))
        prob = jnp.exp(scores - log_total)
        heads_out = jnp.einsum('hqk,khd->qhd', low(prob), value, precision=lax.Precision.HIGHEST)
        return low(low_back(heads_out))
    attn_heads = lax.map(jax.checkpoint(attend), (query.reshape(num_blocks, QBLOCK, HEADS, HEAD_DIM), doc_index.reshape(num_blocks, QBLOCK), token_idx.reshape(num_blocks, QBLOCK))).reshape(ROWS, D)
    mid_h = xrow + low_back(matmul_hi(attn_heads, wo_f))
    inv_b = lax.rsqrt(lax.optimization_barrier(jnp.mean(mid_h * mid_h, axis=-1, keepdims=True)) + epsilon)
    normed_b = low(mid_h * inv_b * gain_m)
    gate = low_back(matmul_hi(normed_b, wg_f))
    up_val = low_back(matmul_hi(normed_b, wu_f))
    mlp_mid = low(jax.nn.silu(gate) * up_val)
    return mid_h + low_back(matmul_hi(mlp_mid, wd_f))

def reference(hidden_in, cotangent, gain_attn, w_query, w_key, w_value, w_out, gain_mlp, w_gate, w_up, w_down, doc_lengths, doc_groups, pad_mask):
    doc_index, inside, group_tok = jax.vmap(row_tables)(doc_lengths, doc_groups)
    real_tok = pad_mask.astype(jnp.float32)
    onehot_g = group_tok[..., None] == jnp.arange(GROUPS, dtype=jnp.int32)
    counts = lax.optimization_barrier(jnp.sum(jnp.where(onehot_g, real_tok[..., None], 0.0), axis=(0, 1)))
    live = jnp.sum(counts)
    group_scale = jnp.sqrt(live / (GROUPS * jnp.maximum(counts, 1.0)))
    token_weight = real_tok * lax.optimization_barrier(jnp.sum(jnp.where(onehot_g, group_scale, 0.0), axis=-1))
    weighted = cotangent.astype(jnp.float32) * token_weight.reshape(TOKENS)[:, None]

    def forward(x_f, gain_a, wq_f, wk_f, wv_f, wo_f, gain_m, wg_f, wu_f, wd_f):
        params = (gain_a, wq_f, wk_f, wv_f, wo_f, gain_m, wg_f, wu_f, wd_f)

        def one_row(inputs):
            xrow, doc_row, inside_row, mask_row = inputs
            return block_row(xrow, params, doc_row, inside_row, mask_row)
        result = lax.map(jax.checkpoint(one_row), (x_f.reshape(BATCH, ROWS, D), doc_index, inside, real_tok))
        return result.reshape(TOKENS, D)
    primals = (hidden_in.astype(jnp.float32), gain_attn.astype(jnp.float32), w_query.astype(jnp.float32), w_key.astype(jnp.float32), w_value.astype(jnp.float32), w_out.astype(jnp.float32), gain_mlp.astype(jnp.float32), w_gate.astype(jnp.float32), w_up.astype(jnp.float32), w_down.astype(jnp.float32))
    output, backward = jax.vjp(forward, *primals)
    grads = backward(weighted)
    return (output.astype(jnp.bfloat16), grads[0], grads[1], grads[2], grads[3], grads[4], grads[5], grads[6], grads[7], grads[8], grads[9])
```

```python
import jax
import jax.numpy as jnp
from jax import lax
from jax.sharding import PartitionSpec as P

HEAD_DIM = 128
ROWS = 1280
QBLOCK = 640
DOCS = 3
GROUPS = 8


epsilon = 1e-05
masked_score = -1e30
rope_base = 10000.0


def row_tables(length_row, group_row):
    starts = jnp.cumsum(length_row) - length_row
    token_idx = jnp.arange(ROWS, dtype=jnp.int32)
    doc_index = jnp.sum((token_idx[:, None] >= starts[None, 1:]).astype(jnp.int32), axis=1)
    onehot = doc_index[:, None] == jnp.arange(DOCS, dtype=jnp.int32)[None, :]
    inside = token_idx - jnp.sum(jnp.where(onehot, starts[None, :], 0), axis=1)
    group_tok = jnp.sum(jnp.where(onehot, group_row[None, :], 0), axis=1)
    return (doc_index, inside, group_tok)


def rope_tables(inside):
    freq = rope_base ** (-jnp.arange(0, HEAD_DIM // 2, dtype=jnp.float32) * 2.0 / HEAD_DIM)
    angle = inside.astype(jnp.float32)[:, None] * freq[None, :]
    return (jnp.cos(angle)[:, None, :], jnp.sin(angle)[:, None, :])


def rotate(values, cosine, sine):
    half = values.shape[-1] // 2
    first, second = (values[..., :half], values[..., half:])
    return jnp.concatenate(
        [first * cosine - second * sine, second * cosine + first * sine], axis=-1
    )


def rotate_back(values, cosine, sine):
    half = values.shape[-1] // 2
    first, second = (values[..., :half], values[..., half:])
    return jnp.concatenate(
        [first * cosine + second * sine, second * cosine - first * sine], axis=-1
    )


def rows_dot(left, right):
    return jnp.dot(left, right, preferred_element_type=jnp.float32)


def rows_dot_t(left, right):
    return lax.dot_general(
        left, right, (((1,), (1,)), ((), ())), preferred_element_type=jnp.float32
    )


def cross_rows(left, right):
    return lax.dot_general(
        left, right, (((0,), (0,)), ((), ())), preferred_element_type=jnp.float32
    )


def block_scores(query_blk, key_part, query_doc, key_doc, key_mask, row_first):
    score_scale = HEAD_DIM ** (-0.5)
    raw = jnp.einsum("qhd,khd->hqk", query_blk, key_part, preferred_element_type=jnp.float32)
    query_tok = row_first + jnp.arange(query_blk.shape[0], dtype=jnp.int32)
    key_tok = jnp.arange(key_part.shape[0], dtype=jnp.int32)
    allowed = (
        (query_doc[:, None] == key_doc[None, :])
        & (query_tok[:, None] >= key_tok[None, :])
        & (key_mask[None, :] > 0.5)
    )
    return jnp.where(allowed[None], raw * score_scale, masked_score)


def exchange(values, axis, bit):
    size = lax.axis_size(axis)
    return lax.ppermute(values, axis, [(rank, rank ^ bit) for rank in range(size)])


def halve(values, axis_rank, bit):
    pairs = values.reshape((values.shape[0] // 2, 2) + values.shape[1:])
    own = lax.dynamic_index_in_dim(pairs, axis_rank, axis=1, keepdims=False)
    other = lax.dynamic_index_in_dim(pairs, 1 - axis_rank, axis=1, keepdims=False)
    return own, other


def scatter_sum(values, axis, link_dtype):
    size = lax.axis_size(axis)
    rank = lax.axis_index(axis)
    kept = values.reshape((size, values.shape[0] // size) + values.shape[1:])
    bit = 1
    while bit < size:
        own, other = halve(kept, (rank // bit) % 2, bit)
        received = exchange(other.astype(link_dtype), axis, bit)
        kept = own.astype(jnp.float32) + received.astype(jnp.float32)
        bit *= 2
    return kept[0]


def butterfly_sum(values, axis):
    size = lax.axis_size(axis)
    bit = 1
    while bit < size:
        values = values + exchange(values, axis, bit)
        bit *= 2
    return values


def shards(
    hidden_in,
    cotangent,
    gain_attn,
    w_query,
    w_key,
    w_value,
    w_out,
    gain_mlp,
    w_gate,
    w_up,
    w_down,
    doc_lengths,
    doc_groups,
    pad_mask,
):
    rows_local = hidden_in.shape[0]
    heads_local = w_query.shape[1] // HEAD_DIM
    width_local = w_query.shape[1]
    row_offset = lax.axis_index("tensor") * rows_local
    score_scale = HEAD_DIM ** (-0.5)
    doc_index, inside, group_tok = row_tables(doc_lengths[0], doc_groups[0])
    real_tok = pad_mask[0].astype(jnp.float32)
    onehot_g = group_tok[:, None] == jnp.arange(GROUPS, dtype=jnp.int32)[None, :]
    counts_local = jnp.sum(jnp.where(onehot_g, real_tok[:, None], 0.0), axis=0)
    counts = butterfly_sum(counts_local, "dp")
    live = jnp.sum(counts)
    group_scale = jnp.sqrt(live / (GROUPS * jnp.maximum(counts, 1.0)))
    token_weight = real_tok * jnp.sum(jnp.where(onehot_g, group_scale[None, :], 0.0), axis=-1)
    weight_local = lax.dynamic_slice_in_dim(token_weight, row_offset, rows_local)
    x_f = hidden_in.astype(jnp.float32)
    inv_a = lax.rsqrt(jnp.mean(x_f * x_f, axis=-1, keepdims=True) + epsilon)
    scaled_a = x_f * inv_a
    normed_a = (scaled_a * gain_attn).astype(jnp.bfloat16)
    gathered_a = lax.all_gather(normed_a, "tensor", axis=0, tiled=True)
    cosine, sine = rope_tables(inside)
    query = rotate(
        rows_dot(gathered_a, w_query).reshape(ROWS, heads_local, HEAD_DIM), cosine, sine
    ).astype(jnp.bfloat16)
    key_vec = rotate(
        rows_dot(gathered_a, w_key).reshape(ROWS, heads_local, HEAD_DIM), cosine, sine
    ).astype(jnp.bfloat16)
    value = rows_dot(gathered_a, w_value).astype(jnp.bfloat16).reshape(ROWS, heads_local, HEAD_DIM)
    num_blocks = ROWS // QBLOCK
    head_blocks = []
    log_totals = []
    for block_idx in range(num_blocks):
        row_first = block_idx * QBLOCK
        row_end = row_first + QBLOCK
        scores = block_scores(
            query[row_first:row_end],
            key_vec[:row_end],
            doc_index[row_first:row_end],
            doc_index[:row_end],
            real_tok[:row_end],
            row_first,
        )
        top_val = jnp.max(scores, axis=-1, keepdims=True)
        log_total = top_val + jnp.log(jnp.sum(jnp.exp(scores - top_val), axis=-1, keepdims=True))
        prob = jnp.exp(scores - log_total).astype(jnp.bfloat16)
        heads_out = jnp.einsum(
            "hqk,khd->qhd", prob, value[:row_end], preferred_element_type=jnp.float32
        )
        head_blocks.append(heads_out.astype(jnp.bfloat16))
        log_totals.append(log_total)
    attn_heads = jnp.concatenate(head_blocks, axis=0).reshape(ROWS, width_local)
    mid_h = x_f + lax.psum_scatter(
        rows_dot(attn_heads, w_out).astype(jnp.bfloat16),
        "tensor",
        scatter_dimension=0,
        tiled=True,
    ).astype(jnp.float32)
    inv_b = lax.rsqrt(jnp.mean(mid_h * mid_h, axis=-1, keepdims=True) + epsilon)
    scaled_b = mid_h * inv_b
    normed_b = (scaled_b * gain_mlp).astype(jnp.bfloat16)
    gathered_b = lax.all_gather(normed_b, "tensor", axis=0, tiled=True)
    gate = rows_dot(gathered_b, w_gate)
    up_val = rows_dot(gathered_b, w_up)
    sigma = jax.nn.sigmoid(gate)
    activated = gate * sigma
    mlp_mid = (activated * up_val).astype(jnp.bfloat16)
    output = (
        mid_h
        + lax.psum_scatter(
            rows_dot(mlp_mid, w_down).astype(jnp.bfloat16),
            "tensor",
            scatter_dimension=0,
            tiled=True,
        ).astype(jnp.float32)
    ).astype(jnp.bfloat16)
    weighted = cotangent.astype(jnp.float32) * weight_local[:, None]
    grad_rows = lax.all_gather(weighted.astype(jnp.bfloat16), "tensor", axis=0, tiled=True)
    grad_down_t = cross_rows(grad_rows, mlp_mid)
    d_mid = rows_dot_t(grad_rows, w_down)
    d_gate = (d_mid * up_val * sigma * (1.0 + gate * (1.0 - sigma))).astype(jnp.bfloat16)
    d_up = (d_mid * activated).astype(jnp.bfloat16)
    d_normed_b = lax.psum_scatter(
        (rows_dot_t(d_gate, w_gate) + rows_dot_t(d_up, w_up)).astype(jnp.bfloat16),
        "tensor",
        scatter_dimension=0,
        tiled=True,
    ).astype(jnp.float32)
    grad_gate = cross_rows(gathered_b, d_gate)
    grad_upw = cross_rows(gathered_b, d_up)
    gain_mlp_part = jnp.sum(d_normed_b * scaled_b, axis=0)
    e_term = d_normed_b * gain_mlp
    d_hidden = weighted + inv_b * (
        e_term - scaled_b * jnp.mean(e_term * scaled_b, axis=-1, keepdims=True)
    )
    grad_attn_rows = lax.all_gather(d_hidden.astype(jnp.bfloat16), "tensor", axis=0, tiled=True)
    grad_out_t = cross_rows(grad_attn_rows, attn_heads)
    d_heads = (
        rows_dot_t(grad_attn_rows, w_out).astype(jnp.bfloat16).reshape(ROWS, heads_local, HEAD_DIM)
    )
    query_grads = []
    key_grad = jnp.zeros((ROWS, heads_local, HEAD_DIM), jnp.float32)
    value_grad = jnp.zeros((ROWS, heads_local, HEAD_DIM), jnp.float32)
    for block_idx in range(num_blocks):
        row_first = block_idx * QBLOCK
        row_end = row_first + QBLOCK
        scores = block_scores(
            query[row_first:row_end],
            key_vec[:row_end],
            doc_index[row_first:row_end],
            doc_index[:row_end],
            real_tok[:row_end],
            row_first,
        )
        prob = jnp.exp(scores - log_totals[block_idx])
        d_prob = jnp.einsum(
            "qhd,khd->hqk",
            d_heads[row_first:row_end],
            value[:row_end],
            preferred_element_type=jnp.float32,
        )
        row_dot = jnp.sum(prob * d_prob, axis=-1, keepdims=True)
        d_score = (prob * (d_prob - row_dot) * score_scale).astype(jnp.bfloat16)
        query_grads.append(
            jnp.einsum(
                "hqk,khd->qhd", d_score, key_vec[:row_end], preferred_element_type=jnp.float32
            )
        )
        key_grad = key_grad.at[:row_end].add(
            jnp.einsum(
                "hqk,qhd->khd",
                d_score,
                query[row_first:row_end],
                preferred_element_type=jnp.float32,
            )
        )
        value_grad = value_grad.at[:row_end].add(
            jnp.einsum(
                "hqk,qhd->khd",
                prob.astype(jnp.bfloat16),
                d_heads[row_first:row_end],
                preferred_element_type=jnp.float32,
            )
        )
    query_pre = (
        rotate_back(jnp.concatenate(query_grads, axis=0), cosine, sine)
        .astype(jnp.bfloat16)
        .reshape(ROWS, width_local)
    )
    key_pre = rotate_back(key_grad, cosine, sine).astype(jnp.bfloat16).reshape(ROWS, width_local)
    value_pre = value_grad.astype(jnp.bfloat16).reshape(ROWS, width_local)
    grad_query = cross_rows(gathered_a, query_pre)
    grad_keyw = cross_rows(gathered_a, key_pre)
    grad_valuew = cross_rows(gathered_a, value_pre)
    total = rows_dot_t(query_pre, w_query)
    total = total + rows_dot_t(key_pre, w_key)
    d_normed_a = lax.psum_scatter(
        (total + rows_dot_t(value_pre, w_value)).astype(jnp.bfloat16),
        "tensor",
        scatter_dimension=0,
        tiled=True,
    ).astype(jnp.float32)
    gain_attn_part = jnp.sum(d_normed_a * scaled_a, axis=0)
    e_attn = d_normed_a * gain_attn
    grad_input = d_hidden + inv_a * (
        e_attn - scaled_a * jnp.mean(e_attn * scaled_a, axis=-1, keepdims=True)
    )
    all_sums = tuple(
        scatter_sum(grad, "dp", jnp.bfloat16)
        for grad in (
            grad_query,
            grad_keyw,
            grad_valuew,
            grad_out_t,
            grad_gate,
            grad_upw,
            grad_down_t,
        )
    ) + tuple(
        scatter_sum(part, "dp", jnp.float32) for part in (gain_attn_part, gain_mlp_part)
    )
    (
        sum_query,
        sum_key,
        sum_value,
        sum_out_t,
        sum_gate,
        sum_up,
        sum_down_t,
        sum_gain_attn,
        sum_gain_mlp,
    ) = all_sums
    gain_attn_grad = butterfly_sum(sum_gain_attn, "tensor")
    gain_mlp_grad = butterfly_sum(sum_gain_mlp, "tensor")
    return (
        output,
        grad_input,
        gain_attn_grad,
        sum_query,
        sum_key,
        sum_value,
        sum_out_t.T,
        gain_mlp_grad,
        sum_gate,
        sum_up,
        sum_down_t.T,
    )


def solution(mesh):
    in_specs = (
        P(("dp", "tensor"), None),
        P(("dp", "tensor"), None),
        P(),
        P(None, "tensor"),
        P(None, "tensor"),
        P(None, "tensor"),
        P("tensor", None),
        P(),
        P(None, "tensor"),
        P(None, "tensor"),
        P("tensor", None),
        P("dp", None),
        P("dp", None),
        P("dp", None),
    )
    out_specs = (
        P(("dp", "tensor"), None),
        P(("dp", "tensor"), None),
        P("dp"),
        P("dp", "tensor"),
        P("dp", "tensor"),
        P("dp", "tensor"),
        P("tensor", "dp"),
        P("dp"),
        P("dp", "tensor"),
        P("dp", "tensor"),
        P("tensor", "dp"),
    )
    return jax.shard_map(shards, mesh=mesh, in_specs=in_specs, out_specs=out_specs, check_vma=False)
```

```python
import functools

import jax
import jax.numpy as jnp
from jax import lax
from jax.experimental import pallas as pl
from jax.experimental.pallas import tpu as pltpu
from jax.sharding import PartitionSpec as P

HEAD_DIM = 128
ROWS = 1280
DOCS = 3
GROUPS = 8
QTILE = 256

epsilon = 1e-05
masked_score = -1e30
rope_base = 10000.0
NT = (((1,), (1,)), ((), ()))
TN = (((0,), (0,)), ((), ()))
NN = (((1,), (0,)), ((), ()))


def mm(left, right, dims=NN):
    return lax.dot_general(left, right, dims, preferred_element_type=jnp.float32)


def whole(shape):
    return pl.BlockSpec(shape, lambda *_: (0,) * len(shape))


def turn(values, cosine, sine):
    return values * cosine + pltpu.roll(values, HEAD_DIM // 2, 1) * sine


def qkv_body(first, rank_ref, xa_ref, xb_ref, cos_ref, sin_ref, wq_ref, wk_ref, wv_ref, q_ref, k_ref, v_ref):
    rows = xa_ref.shape[0]
    for half, x_ref in enumerate((xa_ref, xb_ref)):
        span = pl.ds(half * rows, rows)
        x = x_ref[...]
        place = pl.ds(pl.multiple_of((rank_ref[0] ^ (first + half)) * rows, rows), rows)
        cosine, sine = cos_ref[place, :], sin_ref[place, :]
        for w_ref, out_ref in ((wq_ref, q_ref), (wk_ref, k_ref)):
            full = mm(x, w_ref[...])
            for head in range(full.shape[1] // HEAD_DIM):
                lanes = slice(head * HEAD_DIM, (head + 1) * HEAD_DIM)
                out_ref[span, lanes] = turn(full[:, lanes], cosine, sine).astype(jnp.bfloat16)
        v_ref[span, :] = mm(x, wv_ref[...]).astype(jnp.bfloat16)


def qkv_pair(first, rank, xa, xb, cosine, sine, wq, wk, wv):
    rows, depth = xa.shape
    width = wq.shape[1]
    tile = 256
    wspec = pl.BlockSpec((depth, tile), lambda j, *_: (0, j))
    ospec = pl.BlockSpec((2 * rows, tile), lambda j, *_: (0, j))
    out = jax.ShapeDtypeStruct((2 * rows, width), jnp.bfloat16)
    return pl.pallas_call(
        functools.partial(qkv_body, first),
        grid_spec=pltpu.PrefetchScalarGridSpec(
            num_scalar_prefetch=1,
            grid=(width // tile,),
            in_specs=[whole(xa.shape)] * 2 + [whole(cosine.shape)] * 2 + [wspec] * 3,
            out_specs=[ospec] * 3,
        ),
        out_shape=[out] * 3,
        compiler_params=pltpu.CompilerParams(vmem_limit_bytes=60 << 20),
        cost_estimate=pl.CostEstimate(
            flops=12 * rows * depth * width, bytes_accessed=6 * depth * width + 4 * rows * depth, transcendentals=0
        ),
        name="qkv",
    )(rank, xa, xb, cosine, sine, wq, wk, wv)


def in_order(rank_ref, near_ref, far_ref, out_ref):
    piece = near_ref.shape[0] // 2
    for index in range(4):
        src = (near_ref, far_ref)[index // 2]
        at = pl.multiple_of((rank_ref[0] ^ index) * piece, piece)
        out_ref[pl.ds(at, piece), :] = src[pl.ds((index % 2) * piece, piece), :]


def out_of_order(rank_ref, src_ref, near_ref, far_ref):
    piece = near_ref.shape[0] // 2
    for index in range(4):
        dst = (near_ref, far_ref)[index // 2]
        at = pl.multiple_of((rank_ref[0] ^ index) * piece, piece)
        dst[pl.ds((index % 2) * piece, piece), :] = src_ref[pl.ds(at, piece), :].astype(dst.dtype)


def attend_body(rank_ref, qn, qf, kn, kf, vn, vf, low_ref, high_ref, on, of, lse_ref, q_s, k_s, v_s, o_s):
    in_order(rank_ref, qn, qf, q_s)
    in_order(rank_ref, kn, kf, k_s)
    in_order(rank_ref, vn, vf, v_s)
    scale = HEAD_DIM ** (-0.5)
    v_t = v_s[...].T
    for block in range(q_s.shape[0] // QTILE):
        span = pl.ds(block * QTILE, QTILE)
        end = (block + 1) * QTILE
        scores = mm(k_s[:end, :], q_s[span, :], NT)
        at = lax.broadcasted_iota(jnp.int32, scores.shape, 0)
        allowed = (at >= low_ref[:, span]) & (at <= high_ref[:, span])
        scores = jnp.where(allowed, scores * scale, masked_score)
        top = jnp.max(scores, axis=0, keepdims=True)
        prob = jnp.exp(scores - top)
        total = jnp.sum(prob, axis=0, keepdims=True)
        lse_ref[0, :, span] = top + jnp.log(total)
        out_t = mm(v_t[:, :end], prob.astype(jnp.bfloat16)) * (1.0 / total)
        o_s[span, :] = out_t.T
    out_of_order(rank_ref, o_s, on, of)


def attend(rank, qs, ks, vs, low, high):
    half, width = qs[0].shape
    rows = 2 * half
    heads = width // HEAD_DIM
    hspec = pl.BlockSpec((half, HEAD_DIM), lambda h, *_: (0, h))
    row = whole((1, rows))
    return pl.pallas_call(
        attend_body,
        grid_spec=pltpu.PrefetchScalarGridSpec(
            num_scalar_prefetch=1,
            grid=(heads,),
            in_specs=[hspec] * 6 + [row] * 2,
            out_specs=[hspec] * 2 + [pl.BlockSpec((1, 1, rows), lambda h, *_: (h, 0, 0))],
            scratch_shapes=[pltpu.VMEM((rows, HEAD_DIM), jnp.bfloat16)] * 3 + [pltpu.VMEM((rows, HEAD_DIM), jnp.float32)],
        ),
        out_shape=[jax.ShapeDtypeStruct((half, width), jnp.bfloat16)] * 2
        + [jax.ShapeDtypeStruct((heads, 1, rows), jnp.float32)],
        compiler_params=pltpu.CompilerParams(vmem_limit_bytes=60 << 20),
        cost_estimate=pl.CostEstimate(
            flops=8 * rows * rows * width, bytes_accessed=8 * rows * width, transcendentals=heads * rows * rows // 2
        ),
        name="attend",
    )(rank, *qs, *ks, *vs, low, high)


def attend_back_body(
    rank_ref, qn, qf, kn, kf, vn, vf, gn, gf, low_ref, high_ref, lse_ref, cos_ref, sin_ref,
    dqn, dqf, dkn, dkf, dvn, dvf, q_s, k_s, v_s, g_s, dq_s, dk_s, dv_s,
):
    in_order(rank_ref, qn, qf, q_s)
    in_order(rank_ref, kn, kf, k_s)
    in_order(rank_ref, vn, vf, v_s)
    in_order(rank_ref, gn, gf, g_s)
    scale = HEAD_DIM ** (-0.5)
    k_t = k_s[...].T
    blocks = q_s.shape[0] // QTILE
    for block in reversed(range(blocks)):
        span = pl.ds(block * QTILE, QTILE)
        end = (block + 1) * QTILE
        query, grad = q_s[span, :], g_s[span, :]
        scores = mm(k_s[:end, :], query, NT) * scale
        at = lax.broadcasted_iota(jnp.int32, scores.shape, 0)
        allowed = (at >= low_ref[:, span]) & (at <= high_ref[:, span])
        prob = jnp.exp(jnp.where(allowed, scores, masked_score) - lse_ref[0, :, span])
        d_prob = mm(v_s[:end, :], grad, NT)
        dot = jnp.sum(prob * d_prob, axis=0, keepdims=True)
        d_score = (prob * (d_prob - dot) * scale).astype(jnp.bfloat16)
        dq_s[span, :] = mm(k_t[:, :end], d_score).T
        d_key = mm(d_score, query)
        d_value = mm(prob.astype(jnp.bfloat16), grad)
        if block == blocks - 1:
            dk_s[...] = d_key
            dv_s[...] = d_value
        else:
            dk_s[:end, :] += d_key
            dv_s[:end, :] += d_value
    dq_s[...] = turn(dq_s[...], cos_ref[...], sin_ref[...])
    dk_s[...] = turn(dk_s[...], cos_ref[...], sin_ref[...])
    out_of_order(rank_ref, dq_s, dqn, dqf)
    out_of_order(rank_ref, dk_s, dkn, dkf)
    out_of_order(rank_ref, dv_s, dvn, dvf)


def attend_back(rank, qs, ks, vs, gs, low, high, lse, cosine, back_sine):
    half, width = qs[0].shape
    rows = 2 * half
    heads = width // HEAD_DIM
    hspec = pl.BlockSpec((half, HEAD_DIM), lambda h, *_: (0, h))
    row = whole((1, rows))
    return pl.pallas_call(
        attend_back_body,
        grid_spec=pltpu.PrefetchScalarGridSpec(
            num_scalar_prefetch=1,
            grid=(heads,),
            in_specs=[hspec] * 8
            + [row] * 2
            + [pl.BlockSpec((1, 1, rows), lambda h, *_: (h, 0, 0))]
            + [whole((rows, HEAD_DIM))] * 2,
            out_specs=[hspec] * 6,
            scratch_shapes=[pltpu.VMEM((rows, HEAD_DIM), jnp.bfloat16)] * 4
            + [pltpu.VMEM((rows, HEAD_DIM), jnp.float32)] * 3,
        ),
        out_shape=[jax.ShapeDtypeStruct((half, width), jnp.bfloat16)] * 6,
        compiler_params=pltpu.CompilerParams(vmem_limit_bytes=60 << 20),
        cost_estimate=pl.CostEstimate(
            flops=20 * rows * rows * width, bytes_accessed=16 * rows * width, transcendentals=heads * rows * rows // 2
        ),
        name="attend_back",
    )(rank, *qs, *ks, *vs, *gs, low, high, lse, cosine, back_sine)


def mlp_body(xa_ref, xb_ref, ca_ref, cb_ref, wg_ref, wu_ref, wd_ref, mid_ref, dg_ref, du_ref):
    rows = xa_ref.shape[0]
    for half, (x_ref, c_ref) in enumerate(((xa_ref, ca_ref), (xb_ref, cb_ref))):
        span = pl.ds(half * rows, rows)
        x = x_ref[...]
        gate = mm(x, wg_ref[...])
        up = mm(x, wu_ref[...])
        d_mid = mm(c_ref[...], wd_ref[...], NT)
        sigma = 1.0 / (1.0 + jnp.exp(-gate))
        active = gate * sigma
        mid_ref[span, :] = (active * up).astype(jnp.bfloat16)
        dg_ref[span, :] = (d_mid * up * sigma * (1.0 + gate * (1.0 - sigma))).astype(jnp.bfloat16)
        du_ref[span, :] = (d_mid * active).astype(jnp.bfloat16)


def mlp_pair(xa, xb, ca, cb, wg, wu, wd):
    rows, depth = xa.shape
    width = wg.shape[1]
    tile = 256
    wspec = pl.BlockSpec((depth, tile), lambda j: (0, j))
    ospec = pl.BlockSpec((2 * rows, tile), lambda j: (0, j))
    return pl.pallas_call(
        mlp_body,
        grid=(pl.cdiv(width, tile),),
        in_specs=[whole(xa.shape)] * 4 + [wspec] * 2 + [pl.BlockSpec((tile, depth), lambda j: (j, 0))],
        out_specs=[ospec] * 3,
        out_shape=[jax.ShapeDtypeStruct((2 * rows, width), jnp.bfloat16)] * 3,
        compiler_params=pltpu.CompilerParams(vmem_limit_bytes=60 << 20),
        cost_estimate=pl.CostEstimate(
            flops=12 * rows * depth * width,
            bytes_accessed=6 * depth * width + 8 * rows * depth + 12 * rows * width,
            transcendentals=2 * rows * width,
        ),
        name="mlp",
    )(xa, xb, ca, cb, wg, wu, wd)


def gather_rows(parts, out_ref):
    at = 0
    for part in parts:
        out_ref[at : at + part.shape[0], :] = part[...]
        at += part.shape[0]


def grad_send_body(pieces, halves, _, *refs):
    left, rights = refs[:pieces], refs[pieces : pieces + halves]
    out_ref, left_s, right_s = refs[pieces + halves :]

    @pl.when(pl.program_id(0) == 0)
    def _():
        gather_sides(rights, right_s)

    gather_rows(left, left_s)
    out_ref[...] = mm(left_s[...], right_s[...], TN).astype(out_ref.dtype)


def gather_sides(rights, out_ref):
    at = 0
    for near, far in zip(rights[::2], rights[1::2]):
        rows, width = near.shape
        out_ref[:rows, at : at + width] = near[...]
        out_ref[rows:, at : at + width] = far[...]
        at += width


def grad_keep_body(pieces, halves, send, _, *refs):
    left, rights = refs[:pieces], refs[pieces : pieces + halves]
    got_ref, away_ref, own_ref, left_s, right_s = refs[pieces + halves :]
    step = pl.program_id(0)

    @pl.when(step == 0)
    def _():
        gather_sides(rights, right_s)

    gather_rows(left, left_s)
    total = mm(left_s[...], right_s[...], TN) + got_ref[...].astype(jnp.float32)

    @pl.when(step < send)
    def _():
        away_ref[...] = total.astype(away_ref.dtype)

    @pl.when(step >= send)
    def _():
        own_ref[...] = total


def grad_call(order, pieces, rights, tile, got=None):
    rows, depth = pieces[0].shape[0] * len(pieces), pieces[0].shape[1]
    width = sum(near.shape[1] for near in rights[::2])
    count = order.shape[0]
    lspec = pl.BlockSpec((pieces[0].shape[0], tile), lambda j, s: (0, s[j]))
    in_specs = [lspec] * len(pieces) + [whole(r.shape) for r in rights]
    args = [order, *pieces, *rights]
    if got is None:
        body = functools.partial(grad_send_body, len(pieces), len(rights))
        out_specs = pl.BlockSpec((tile, width), lambda j, *_: (j, 0))
        out_shape = jax.ShapeDtypeStruct((count * tile, width), jnp.bfloat16)
    else:
        send = count // 2
        body = functools.partial(grad_keep_body, len(pieces), len(rights), send)
        in_specs.append(pl.BlockSpec((tile, width), lambda j, s: (s[j] // 2, 0)))
        args.append(got)
        out_specs = [
            pl.BlockSpec((tile, width), lambda j, *_: (jnp.minimum(j, send - 1), 0)),
            pl.BlockSpec((tile, width), lambda j, *_: (jnp.maximum(j - send, 0), 0)),
        ]
        out_shape = [
            jax.ShapeDtypeStruct((send * tile, width), jnp.bfloat16),
            jax.ShapeDtypeStruct(((count - send) * tile, width), jnp.float32),
        ]
    return pl.pallas_call(
        body,
        grid_spec=pltpu.PrefetchScalarGridSpec(
            num_scalar_prefetch=1,
            grid=(count,),
            in_specs=in_specs,
            out_specs=out_specs,
            scratch_shapes=[pltpu.VMEM((rows, tile), jnp.bfloat16), pltpu.VMEM((rows, width), jnp.bfloat16)],
        ),
        out_shape=out_shape,
        compiler_params=pltpu.CompilerParams(vmem_limit_bytes=60 << 20),
        cost_estimate=pl.CostEstimate(
            flops=2 * rows * tile * count * width,
            bytes_accessed=2 * rows * (tile * count + width) + 3 * tile * count * width,
            transcendentals=0,
        ),
        name="weight_grad",
    )(*args)


def row_tables(length_row, group_row, mask_row):
    starts = jnp.cumsum(length_row) - length_row
    token = jnp.arange(ROWS, dtype=jnp.int32)
    doc_index = jnp.sum((token[:, None] >= starts[None, 1:]).astype(jnp.int32), axis=1)
    onehot = doc_index[:, None] == jnp.arange(DOCS, dtype=jnp.int32)[None, :]
    first = jnp.sum(jnp.where(onehot, starts[None, :], 0), axis=1)
    group_tok = jnp.sum(jnp.where(onehot, group_row[None, :], 0), axis=1)
    real = jnp.sum(jnp.where(onehot, mask_row[:, None], 0), axis=0)
    last_real = first + jnp.sum(jnp.where(onehot, real[None, :], 0), axis=1) - 1
    return (token - first, first, jnp.minimum(token, last_real), group_tok)


def rope_tables(inside):
    freq = rope_base ** (-jnp.arange(0, HEAD_DIM // 2, dtype=jnp.float32) * 2.0 / HEAD_DIM)
    angle = inside.astype(jnp.float32)[:, None] * freq[None, :]
    cosine, sine = jnp.cos(angle), jnp.sin(angle)
    return (
        jnp.concatenate([cosine, cosine], axis=-1),
        jnp.concatenate([-sine, sine], axis=-1),
        jnp.concatenate([sine, -sine], axis=-1),
    )


def rows_dot(left, right):
    return jnp.dot(left, right, preferred_element_type=jnp.float32)


def rows_dot_t(left, right):
    return lax.dot_general(left, right, NT, preferred_element_type=jnp.float32)


def exchange(values, axis, bit):
    size = lax.axis_size(axis)
    return lax.ppermute(values, axis, [(rank, rank ^ bit) for rank in range(size)])


def butterfly_sum(values, axis):
    size = lax.axis_size(axis)
    bit = 1
    while bit < size:
        values = values + exchange(values, axis, bit)
        bit *= 2
    return values


def after(values, *others):
    return lax.optimization_barrier((values, *others))[0]


def scatter_rest(kept, away, axis, bit):
    size = lax.axis_size(axis)
    rank = lax.axis_index(axis)
    while True:
        got = exchange(away.astype(jnp.bfloat16), axis, bit)
        bit *= 2
        if bit == size:
            return kept.astype(jnp.float32) + got.astype(jnp.float32)
        total = kept.astype(jnp.float32) + got.astype(jnp.float32)
        pairs = total.reshape((total.shape[0] // 2, 2) + total.shape[1:])
        side = (rank // bit) % 2
        kept = lax.dynamic_index_in_dim(pairs, side, axis=1, keepdims=False)
        away = lax.dynamic_index_in_dim(pairs, 1 - side, axis=1, keepdims=False)


def scatter_small(values, axis):
    size = lax.axis_size(axis)
    rank = lax.axis_index(axis)
    kept = values
    bit = 1
    while bit < size:
        pairs = kept.reshape((kept.shape[0], kept.shape[1] // 2, 2) + kept.shape[2:])
        side = (rank // bit) % 2
        own = lax.dynamic_index_in_dim(pairs, side, axis=2, keepdims=False)
        away = lax.dynamic_index_in_dim(pairs, 1 - side, axis=2, keepdims=False)
        kept = own + exchange(away, axis, bit)
        bit *= 2
    return kept[:, 0]


class WeightGrad:
    def __init__(self, pieces, rights):
        self.pieces, self.rights = pieces, rights
        self.size = lax.axis_size("dp")
        self.rank = lax.axis_index("dp")
        self.tile = pieces[0].shape[1] // self.size
        self.blocks = self.tile % 128 == 0 and self.size >= 4

    def send(self):
        if self.blocks:
            order = 2 * jnp.arange(self.size // 2, dtype=jnp.int32) + (1 - self.rank % 2)
            return grad_call(order, self.pieces, self.rights, self.tile)
        left = jnp.concatenate(self.pieces, axis=0)
        right = jnp.concatenate([jnp.concatenate(self.rights[::2], axis=1), jnp.concatenate(self.rights[1::2], axis=1)], axis=0)
        full = lax.dot_general(left, right, TN, preferred_element_type=jnp.float32)
        pairs = full.reshape(self.size // 2, 2, self.tile, -1)
        self.own = lax.dynamic_index_in_dim(pairs, self.rank % 2, axis=1, keepdims=False)
        away = lax.dynamic_index_in_dim(pairs, 1 - self.rank % 2, axis=1, keepdims=False)
        return away.reshape(self.size // 2 * self.tile, -1).astype(jnp.bfloat16)

    def finish(self, got):
        width = got.shape[1]
        if self.blocks:
            place = jnp.arange(self.size // 4, dtype=jnp.int32)
            side = (self.rank // 2) % 2
            blocks = jnp.concatenate([2 * place + 1 - side, 2 * place + side])
            away, kept = grad_call(2 * blocks + self.rank % 2, self.pieces, self.rights, self.tile, got)
            away, kept = (a.reshape(-1, self.tile, width) for a in (away, kept))
        else:
            total = self.own + got.reshape(self.own.shape).astype(jnp.float32)
            pairs = total.reshape(self.size // 4, 2, self.tile, width)
            side = (self.rank // 2) % 2
            kept = lax.dynamic_index_in_dim(pairs, side, axis=1, keepdims=False)
            away = lax.dynamic_index_in_dim(pairs, 1 - side, axis=1, keepdims=False)
        return scatter_rest(kept, away, "dp", 2)[0]


def cut(values):
    half = values.shape[0] // 2
    return values[:half], values[half:]


def send_far(far):
    mine, others = cut(far)
    return (mine.astype(jnp.float32) + exchange(others, "tensor", 1).astype(jnp.float32)).astype(jnp.bfloat16)


def sum_near(near, got):
    mine, others = cut(near)
    return (
        mine.astype(jnp.float32)
        + exchange(others, "tensor", 1).astype(jnp.float32)
        + got.astype(jnp.float32)
    )


def shards(
    hidden_in,
    cotangent,
    gain_attn,
    w_query,
    w_key,
    w_value,
    w_out,
    gain_mlp,
    w_gate,
    w_up,
    w_down,
    doc_lengths,
    doc_groups,
    pad_mask,
):
    rows_local = hidden_in.shape[0]
    rank = lax.axis_index("tensor").astype(jnp.int32)
    rank_ref = rank[None]

    def to_far(values):
        return exchange(values, "tensor", 2)

    def to_mate(values):
        return exchange(values, "tensor", 1)

    x_f = hidden_in.astype(jnp.float32)
    inv_a = lax.rsqrt(jnp.mean(x_f * x_f, axis=-1, keepdims=True) + epsilon)
    a0 = (x_f * inv_a * gain_attn).astype(jnp.bfloat16)
    a2 = to_far(a0)
    a1 = to_mate(a0)
    a3 = to_mate(a2)

    inside, low, high, group_tok = row_tables(doc_lengths[0], doc_groups[0], pad_mask[0])
    low, high = low[None], high[None]
    real_tok = pad_mask[0].astype(jnp.float32)
    onehot_g = group_tok[:, None] == jnp.arange(GROUPS, dtype=jnp.int32)[None, :]
    counts = butterfly_sum(jnp.sum(jnp.where(onehot_g, real_tok[:, None], 0.0), axis=0), "dp")
    live = jnp.sum(counts)
    group_scale = jnp.sqrt(live / (GROUPS * jnp.maximum(counts, 1.0)))
    token_weight = real_tok * jnp.sum(jnp.where(onehot_g, group_scale[None, :], 0.0), axis=-1)
    weight_local = lax.dynamic_slice_in_dim(token_weight, rank * rows_local, rows_local)
    c0 = (cotangent.astype(jnp.float32) * weight_local[:, None]).astype(jnp.bfloat16)
    cosine, sine, back_sine = rope_tables(inside)

    near = qkv_pair(0, rank_ref, a0, a1, cosine, sine, w_query, w_key, w_value)
    c0 = after(c0, a2)
    c2 = to_far(c0)
    c1 = to_mate(c0)
    c3 = to_mate(c2)
    far = qkv_pair(2, rank_ref, a2, a3, cosine, sine, w_query, w_key, w_value)
    qs, ks, vs = zip(near, far)
    heads_near, heads_far, lse = attend(rank_ref, qs, ks, vs, low, high)

    got = to_far(send_far(rows_dot(heads_far, w_out).astype(jnp.bfloat16)))
    mid_h = x_f + sum_near(rows_dot(heads_near, w_out).astype(jnp.bfloat16), got)
    inv_b = lax.rsqrt(jnp.mean(mid_h * mid_h, axis=-1, keepdims=True) + epsilon)
    b0 = (mid_h * inv_b * gain_mlp).astype(jnp.bfloat16)
    b2 = to_far(b0)
    b1 = to_mate(b0)
    b3 = to_mate(b2)
    mid_near, dg_near, du_near = mlp_pair(b0, b1, c0, c1, w_gate, w_up, w_down)
    mid_far, dg_far, du_far = mlp_pair(b2, b3, c2, c3, w_gate, w_up, w_down)

    grad_down = WeightGrad((c0, c1, c2, c3), (mid_near, mid_far))
    grad_gate = WeightGrad((b0, b1, b2, b3), (dg_near, dg_far))
    grad_up = WeightGrad((b0, b1, b2, b3), (du_near, du_far))
    send_down = grad_down.send()
    dg_far, du_far, send_down = lax.optimization_barrier((dg_far, du_far, send_down))
    x_down = exchange(send_down, "dp", 1)
    far_b = (rows_dot_t(dg_far, w_gate) + rows_dot_t(du_far, w_up)).astype(jnp.bfloat16)
    near_b = (rows_dot_t(dg_near, w_gate) + rows_dot_t(du_near, w_up)).astype(jnp.bfloat16)
    got = to_far(send_far(far_b))
    d_b = sum_near(near_b, got)
    send_gate = grad_gate.send()
    send_up = grad_up.send()
    d_b, send_gate, send_up = lax.optimization_barrier((d_b, send_gate, send_up))
    n_b = mid_h * inv_b
    gain_mlp_part = jnp.sum(d_b * n_b, axis=0)
    e_b = d_b * gain_mlp
    weighted = cotangent.astype(jnp.float32) * weight_local[:, None]
    d_h = weighted + inv_b * (e_b - n_b * jnp.mean(e_b * n_b, axis=-1, keepdims=True))
    t0 = d_h.astype(jnp.bfloat16)
    t2 = to_far(t0)
    t1 = to_mate(t0)
    t3 = to_mate(t2)
    gs_near = rows_dot_t(jnp.concatenate([t0, t1], axis=0), w_out).astype(jnp.bfloat16)
    out_far = rows_dot(mid_far, w_down).astype(jnp.bfloat16)
    out_near = rows_dot(mid_near, w_down).astype(jnp.bfloat16)
    gs_far = rows_dot_t(jnp.concatenate([t2, t3], axis=0), w_out).astype(jnp.bfloat16)
    gs_near, gs_far, x_down = lax.optimization_barrier((gs_near, gs_far, x_down))
    x_gate = exchange(after(send_gate, x_down), "dp", 1)
    got = to_far(send_far(after(out_far, t2)))
    output = (mid_h + sum_near(out_near, got)).astype(jnp.bfloat16)
    sum_down = grad_down.finish(x_down)

    dqn, dqf, dkn, dkf, dvn, dvf = attend_back(
        rank_ref, qs, ks, vs, (gs_near, gs_far), low, high, lse, cosine, back_sine
    )
    grad_out = WeightGrad((t0, t1, t2, t3), (heads_near, heads_far))
    grad_qkv = [
        WeightGrad((a0, a1, a2, a3), pair) for pair in ((dqn, dqf), (dkn, dkf), (dvn, dvf))
    ]
    send_out = grad_out.send()
    send_qkv = [grad.send() for grad in grad_qkv]

    def to_input(q_part, k_part, v_part):
        total = rows_dot_t(q_part, w_query)
        total = total + rows_dot_t(k_part, w_key)
        return (total + rows_dot_t(v_part, w_value)).astype(jnp.bfloat16)

    got = to_far(send_far(to_input(dqf, dkf, dvf)))
    d_a = sum_near(to_input(dqn, dkn, dvn), got)
    n_a = x_f * inv_a
    gain_attn_part = jnp.sum(d_a * n_a, axis=0)
    e_a = d_a * gain_attn
    grad_input = d_h + inv_a * (e_a - n_a * jnp.mean(e_a * n_a, axis=-1, keepdims=True))
    gains = jnp.stack([gain_attn_part, gain_mlp_part])
    gains = butterfly_sum(scatter_small(gains.reshape(2, lax.axis_size("dp"), -1), "dp"), "tensor")

    x_up = exchange(after(send_up, x_gate), "dp", 1)
    sum_gate = grad_gate.finish(x_gate)
    x_out = exchange(after(send_out, x_up), "dp", 1)
    sum_up = grad_up.finish(x_up)
    last = x_out
    sum_out = grad_out.finish(x_out)
    sums = []
    for grad, send in zip(grad_qkv, send_qkv):
        last = exchange(after(send, last), "dp", 1)
        sums.append(grad.finish(last))
    return (
        output,
        grad_input,
        gains[0],
        sums[0],
        sums[1],
        sums[2],
        sum_out.T,
        gains[1],
        sum_gate,
        sum_up,
        sum_down.T,
    )


def solution(mesh):
    rows, columns, split = P(("dp", "tensor"), None), P(None, "tensor"), P("tensor", None)
    in_specs = (
        rows,
        rows,
        P(),
        columns,
        columns,
        columns,
        split,
        P(),
        columns,
        columns,
        split,
        P("dp", None),
        P("dp", None),
        P("dp", None),
    )
    grads = P("dp", "tensor")
    grads_t = P("tensor", "dp")
    out_specs = (rows, rows, P("dp"), grads, grads, grads, grads_t, P("dp"), grads, grads, grads_t)
    return jax.shard_map(shards, mesh=mesh, in_specs=in_specs, out_specs=out_specs, check_vma=False)
```

```python
import functools

import jax
import jax.numpy as jnp
from jax import lax
from jax.experimental import pallas as pl
from jax.experimental.pallas import tpu as pltpu
from jax.sharding import PartitionSpec as P

HEAD_DIM = 128
ROWS = 1280
DOCS = 3
GROUPS = 8
QTILE = 256

epsilon = 1e-05
masked_score = -1e30
rope_base = 10000.0
COST = 1000


def cost(flops, bytes_accessed, transcendentals):
    return pl.CostEstimate(
        flops=flops // COST, bytes_accessed=bytes_accessed // COST, transcendentals=transcendentals // COST
    )


NT = (((1,), (1,)), ((), ()))
TN = (((0,), (0,)), ((), ()))
NN = (((1,), (0,)), ((), ()))


def mm(left, right, dims=NN):
    return lax.dot_general(left, right, dims, preferred_element_type=jnp.float32)


def whole(shape):
    return pl.BlockSpec(shape, lambda *_: (0,) * len(shape))


def turn(values, cosine, sine):
    return values * cosine + pltpu.roll(values, HEAD_DIM // 2, 1) * sine


def qkv_body(first, rank_ref, xa_ref, xb_ref, cos_ref, sin_ref, wq_ref, wk_ref, wv_ref, q_ref, k_ref, v_ref):
    rows = xa_ref.shape[0]
    for half, x_ref in enumerate((xa_ref, xb_ref)):
        span = pl.ds(half * rows, rows)
        x = x_ref[...]
        place = pl.ds(pl.multiple_of((rank_ref[0] ^ (first + half)) * rows, rows), rows)
        cosine, sine = cos_ref[place, :], sin_ref[place, :]
        for w_ref, out_ref in ((wq_ref, q_ref), (wk_ref, k_ref)):
            full = mm(x, w_ref[...])
            for head in range(full.shape[1] // HEAD_DIM):
                lanes = slice(head * HEAD_DIM, (head + 1) * HEAD_DIM)
                out_ref[span, lanes] = turn(full[:, lanes], cosine, sine).astype(jnp.bfloat16)
        v_ref[span, :] = mm(x, wv_ref[...]).astype(jnp.bfloat16)


def qkv_pair(first, rank, xa, xb, cosine, sine, wq, wk, wv):
    rows, depth = xa.shape
    width = wq.shape[1]
    tile = 256
    wspec = pl.BlockSpec((depth, tile), lambda j, *_: (0, j))
    ospec = pl.BlockSpec((2 * rows, tile), lambda j, *_: (0, j))
    out = jax.ShapeDtypeStruct((2 * rows, width), jnp.bfloat16)
    return pl.pallas_call(
        functools.partial(qkv_body, first),
        grid_spec=pltpu.PrefetchScalarGridSpec(
            num_scalar_prefetch=1,
            grid=(width // tile,),
            in_specs=[whole(xa.shape)] * 2 + [whole(cosine.shape)] * 2 + [wspec] * 3,
            out_specs=[ospec] * 3,
        ),
        out_shape=[out] * 3,
        compiler_params=pltpu.CompilerParams(vmem_limit_bytes=60 << 20),
        cost_estimate=cost(
            flops=12 * rows * depth * width, bytes_accessed=6 * depth * width + 4 * rows * depth, transcendentals=0
        ),
        name="qkv",
    )(rank, xa, xb, cosine, sine, wq, wk, wv)


def in_order(rank_ref, near_ref, far_ref, out_ref):
    piece = near_ref.shape[0] // 2
    for index in range(4):
        src = (near_ref, far_ref)[index // 2]
        at = pl.multiple_of((rank_ref[0] ^ index) * piece, piece)
        out_ref[pl.ds(at, piece), :] = src[pl.ds((index % 2) * piece, piece), :]


def out_of_order(rank_ref, src_ref, near_ref, far_ref):
    piece = near_ref.shape[0] // 2
    for index in range(4):
        dst = (near_ref, far_ref)[index // 2]
        at = pl.multiple_of((rank_ref[0] ^ index) * piece, piece)
        dst[pl.ds((index % 2) * piece, piece), :] = src_ref[pl.ds(at, piece), :].astype(dst.dtype)


def attend_body(rank_ref, qn, qf, kn, kf, vn, vf, low_ref, high_ref, on, of, lse_ref, q_s, k_s, v_s, o_s):
    in_order(rank_ref, qn, qf, q_s)
    in_order(rank_ref, kn, kf, k_s)
    in_order(rank_ref, vn, vf, v_s)
    scale = HEAD_DIM ** (-0.5)
    v_t = v_s[...].T
    for block in range(q_s.shape[0] // QTILE):
        span = pl.ds(block * QTILE, QTILE)
        end = (block + 1) * QTILE
        scores = mm(k_s[:end, :], q_s[span, :], NT)
        at = lax.broadcasted_iota(jnp.int32, scores.shape, 0)
        allowed = (at >= low_ref[:, span]) & (at <= high_ref[:, span])
        scores = jnp.where(allowed, scores * scale, masked_score)
        top = jnp.max(scores, axis=0, keepdims=True)
        prob = jnp.exp(scores - top)
        total = jnp.sum(prob, axis=0, keepdims=True)
        lse_ref[0, :, span] = top + jnp.log(total)
        out_t = mm(v_t[:, :end], prob.astype(jnp.bfloat16)) * (1.0 / total)
        o_s[span, :] = out_t.T
    out_of_order(rank_ref, o_s, on, of)


def attend(rank, qs, ks, vs, low, high):
    half, width = qs[0].shape
    rows = 2 * half
    heads = width // HEAD_DIM
    hspec = pl.BlockSpec((half, HEAD_DIM), lambda h, *_: (0, h))
    row = whole((1, rows))
    return pl.pallas_call(
        attend_body,
        grid_spec=pltpu.PrefetchScalarGridSpec(
            num_scalar_prefetch=1,
            grid=(heads,),
            in_specs=[hspec] * 6 + [row] * 2,
            out_specs=[hspec] * 2 + [pl.BlockSpec((1, 1, rows), lambda h, *_: (h, 0, 0))],
            scratch_shapes=[pltpu.VMEM((rows, HEAD_DIM), jnp.bfloat16)] * 3 + [pltpu.VMEM((rows, HEAD_DIM), jnp.float32)],
        ),
        out_shape=[jax.ShapeDtypeStruct((half, width), jnp.bfloat16)] * 2
        + [jax.ShapeDtypeStruct((heads, 1, rows), jnp.float32)],
        compiler_params=pltpu.CompilerParams(vmem_limit_bytes=60 << 20),
        cost_estimate=cost(
            flops=8 * rows * rows * width, bytes_accessed=8 * rows * width, transcendentals=heads * rows * rows // 2
        ),
        name="attend",
    )(rank, *qs, *ks, *vs, low, high)


def attend_back_body(
    rank_ref, qn, qf, kn, kf, vn, vf, gn, gf, low_ref, high_ref, lse_ref, cos_ref, sin_ref,
    dqn, dqf, dkn, dkf, dvn, dvf, q_s, k_s, v_s, g_s, dq_s, dk_s, dv_s,
):
    in_order(rank_ref, qn, qf, q_s)
    in_order(rank_ref, kn, kf, k_s)
    in_order(rank_ref, vn, vf, v_s)
    in_order(rank_ref, gn, gf, g_s)
    scale = HEAD_DIM ** (-0.5)
    k_t = k_s[...].T
    blocks = q_s.shape[0] // QTILE
    for block in reversed(range(blocks)):
        span = pl.ds(block * QTILE, QTILE)
        end = (block + 1) * QTILE
        query, grad = q_s[span, :], g_s[span, :]
        scores = mm(k_s[:end, :], query, NT) * scale
        at = lax.broadcasted_iota(jnp.int32, scores.shape, 0)
        allowed = (at >= low_ref[:, span]) & (at <= high_ref[:, span])
        prob = jnp.exp(jnp.where(allowed, scores, masked_score) - lse_ref[0, :, span])
        d_prob = mm(v_s[:end, :], grad, NT)
        dot = jnp.sum(prob * d_prob, axis=0, keepdims=True)
        d_score = (prob * (d_prob - dot) * scale).astype(jnp.bfloat16)
        dq_s[span, :] = mm(k_t[:, :end], d_score).T
        d_key = mm(d_score, query)
        d_value = mm(prob.astype(jnp.bfloat16), grad)
        if block == blocks - 1:
            dk_s[...] = d_key
            dv_s[...] = d_value
        else:
            dk_s[:end, :] += d_key
            dv_s[:end, :] += d_value
    dq_s[...] = turn(dq_s[...], cos_ref[...], sin_ref[...])
    dk_s[...] = turn(dk_s[...], cos_ref[...], sin_ref[...])
    out_of_order(rank_ref, dq_s, dqn, dqf)
    out_of_order(rank_ref, dk_s, dkn, dkf)
    out_of_order(rank_ref, dv_s, dvn, dvf)


def attend_back(rank, qs, ks, vs, gs, low, high, lse, cosine, back_sine):
    half, width = qs[0].shape
    rows = 2 * half
    heads = width // HEAD_DIM
    hspec = pl.BlockSpec((half, HEAD_DIM), lambda h, *_: (0, h))
    row = whole((1, rows))
    return pl.pallas_call(
        attend_back_body,
        grid_spec=pltpu.PrefetchScalarGridSpec(
            num_scalar_prefetch=1,
            grid=(heads,),
            in_specs=[hspec] * 8
            + [row] * 2
            + [pl.BlockSpec((1, 1, rows), lambda h, *_: (h, 0, 0))]
            + [whole((rows, HEAD_DIM))] * 2,
            out_specs=[hspec] * 6,
            scratch_shapes=[pltpu.VMEM((rows, HEAD_DIM), jnp.bfloat16)] * 4
            + [pltpu.VMEM((rows, HEAD_DIM), jnp.float32)] * 3,
        ),
        out_shape=[jax.ShapeDtypeStruct((half, width), jnp.bfloat16)] * 6,
        compiler_params=pltpu.CompilerParams(vmem_limit_bytes=60 << 20),
        cost_estimate=cost(
            flops=20 * rows * rows * width, bytes_accessed=16 * rows * width, transcendentals=heads * rows * rows // 2
        ),
        name="attend_back",
    )(rank, *qs, *ks, *vs, *gs, low, high, lse, cosine, back_sine)


def mlp_body(xa_ref, xb_ref, ca_ref, cb_ref, wg_ref, wu_ref, wd_ref, mid_ref, dg_ref, du_ref):
    rows = xa_ref.shape[0]
    for half, (x_ref, c_ref) in enumerate(((xa_ref, ca_ref), (xb_ref, cb_ref))):
        span = pl.ds(half * rows, rows)
        x = x_ref[...]
        gate = mm(x, wg_ref[...])
        up = mm(x, wu_ref[...])
        d_mid = mm(c_ref[...], wd_ref[...], NT)
        sigma = 1.0 / (1.0 + jnp.exp(-gate))
        active = gate * sigma
        mid_ref[span, :] = (active * up).astype(jnp.bfloat16)
        dg_ref[span, :] = (d_mid * up * sigma * (1.0 + gate * (1.0 - sigma))).astype(jnp.bfloat16)
        du_ref[span, :] = (d_mid * active).astype(jnp.bfloat16)


def mlp_pair(xa, xb, ca, cb, wg, wu, wd):
    rows, depth = xa.shape
    width = wg.shape[1]
    tile = 256
    wspec = pl.BlockSpec((depth, tile), lambda j: (0, j))
    ospec = pl.BlockSpec((2 * rows, tile), lambda j: (0, j))
    return pl.pallas_call(
        mlp_body,
        grid=(pl.cdiv(width, tile),),
        in_specs=[whole(xa.shape)] * 4 + [wspec] * 2 + [pl.BlockSpec((tile, depth), lambda j: (j, 0))],
        out_specs=[ospec] * 3,
        out_shape=[jax.ShapeDtypeStruct((2 * rows, width), jnp.bfloat16)] * 3,
        compiler_params=pltpu.CompilerParams(vmem_limit_bytes=60 << 20),
        cost_estimate=cost(
            flops=12 * rows * depth * width,
            bytes_accessed=6 * depth * width + 8 * rows * depth + 12 * rows * width,
            transcendentals=2 * rows * width,
        ),
        name="mlp",
    )(xa, xb, ca, cb, wg, wu, wd)


def gather_rows(parts, out_ref):
    at = 0
    for part in parts:
        out_ref[at : at + part.shape[0], :] = part[...]
        at += part.shape[0]


def gather_sides(rights, out_ref):
    at = 0
    for near, far in zip(rights[::2], rights[1::2]):
        rows, width = near.shape
        out_ref[:rows, at : at + width] = near[...]
        out_ref[rows:, at : at + width] = far[...]
        at += width


def grad_body(pieces, halves, groups, _, *refs):
    left, rights = refs[:pieces], refs[pieces : pieces + halves]
    outs, (left_s, right_s) = refs[pieces + halves : -2], refs[-2:]
    step = pl.program_id(0)

    @pl.when(step == 0)
    def _():
        gather_sides(rights, right_s)

    gather_rows(left, left_s)
    total = mm(left_s[...], right_s[...], TN).astype(jnp.bfloat16)
    first = 0
    for out_ref, count in zip(outs, groups):

        @pl.when((step >= first) & (step < first + count))
        def _():
            out_ref[0] = total

        first += count


def grad_call(order, groups, pieces, rights, tile):
    rows, depth = pieces[0].shape[0] * len(pieces), pieces[0].shape[1]
    width = sum(near.shape[1] for near in rights[::2])
    count = sum(groups)
    lspec = pl.BlockSpec((pieces[0].shape[0], tile), lambda j, s: (0, s[j]))
    out_specs = []
    for index, size in enumerate(groups):
        first = sum(groups[:index])
        out_specs.append(
            pl.BlockSpec(
                (1, tile, width),
                lambda j, *_, first=first, size=size: (jnp.clip(j - first, 0, size - 1), 0, 0),
            )
        )
    return pl.pallas_call(
        functools.partial(grad_body, len(pieces), len(rights), groups),
        grid_spec=pltpu.PrefetchScalarGridSpec(
            num_scalar_prefetch=1,
            grid=(count,),
            in_specs=[lspec] * len(pieces) + [whole(r.shape) for r in rights],
            out_specs=out_specs,
            scratch_shapes=[pltpu.VMEM((rows, tile), jnp.bfloat16), pltpu.VMEM((rows, width), jnp.bfloat16)],
        ),
        out_shape=[jax.ShapeDtypeStruct((size, tile, width), jnp.bfloat16) for size in groups],
        compiler_params=pltpu.CompilerParams(vmem_limit_bytes=60 << 20),
        cost_estimate=cost(
            flops=2 * rows * tile * count * width,
            bytes_accessed=2 * rows * (tile * count + width) + 2 * tile * count * width,
            transcendentals=0,
        ),
        name="weight_grad",
    )(order, *pieces, *rights)


def project_body(terms, split, *refs):
    at, lefts, weights = 0, [], []
    for pieces, dims in terms:
        lefts.append(refs[at : at + pieces])
        weights.append((refs[at + pieces], dims))
        at += pieces + 1
    outs = refs[at:]
    rows = outs[0].shape[0] // (1 if split else 2)
    for half in range(2):
        span = pl.ds(half * rows, rows)
        total = None
        for left, (w_ref, dims) in zip(lefts, weights):
            value = mm(left[half][...] if len(left) == 2 else left[0][span, :], w_ref[...], dims)
            total = value if total is None else total + value
        if split:
            outs[half][...] = total.astype(jnp.bfloat16)
        else:
            outs[0][span, :] = total.astype(jnp.bfloat16)


def project(terms, split):
    terms = [(left if isinstance(left, tuple) else (left,), w, NT if flip else NN) for left, w, flip in terms]
    rows = sum(piece.shape[0] for piece in terms[0][0])
    width = terms[0][1].shape[0 if terms[0][2] is NT else 1]
    tile = min(512, width)
    in_specs, args, flops = [], [], 0
    for left, w, dims in terms:
        depth = left[0].shape[1]
        in_specs += [whole(piece.shape) for piece in left]
        in_specs.append(
            pl.BlockSpec((tile, depth), lambda j: (j, 0)) if dims is NT else pl.BlockSpec((depth, tile), lambda j: (0, j))
        )
        args += [*left, w]
        flops += 2 * rows * depth * width
    count = 2 if split else 1
    out = jax.ShapeDtypeStruct((rows // count, width), jnp.bfloat16)
    result = pl.pallas_call(
        functools.partial(project_body, [(len(left), dims) for left, _, dims in terms], split),
        grid=(width // tile,),
        in_specs=in_specs,
        out_specs=[pl.BlockSpec((rows // count, tile), lambda j: (0, j))] * count,
        out_shape=[out] * count,
        compiler_params=pltpu.CompilerParams(vmem_limit_bytes=60 << 20),
        cost_estimate=cost(
            flops=flops, bytes_accessed=sum(2 * a.size for a in args) + 2 * rows * width, transcendentals=0
        ),
        name="project",
    )(*args)
    return tuple(result) if split else result[0]


def row_tables(length_row, group_row, mask_row):
    starts = jnp.cumsum(length_row) - length_row
    token = jnp.arange(ROWS, dtype=jnp.int32)
    doc_index = jnp.sum((token[:, None] >= starts[None, 1:]).astype(jnp.int32), axis=1)
    onehot = doc_index[:, None] == jnp.arange(DOCS, dtype=jnp.int32)[None, :]
    first = jnp.sum(jnp.where(onehot, starts[None, :], 0), axis=1)
    group_tok = jnp.sum(jnp.where(onehot, group_row[None, :], 0), axis=1)
    real = jnp.sum(jnp.where(onehot, mask_row[:, None], 0), axis=0)
    last_real = first + jnp.sum(jnp.where(onehot, real[None, :], 0), axis=1) - 1
    return (token - first, first, jnp.minimum(token, last_real), group_tok)


def rope_tables(inside):
    freq = rope_base ** (-jnp.arange(0, HEAD_DIM // 2, dtype=jnp.float32) * 2.0 / HEAD_DIM)
    angle = inside.astype(jnp.float32)[:, None] * freq[None, :]
    cosine, sine = jnp.cos(angle), jnp.sin(angle)
    return (
        jnp.concatenate([cosine, cosine], axis=-1),
        jnp.concatenate([-sine, sine], axis=-1),
        jnp.concatenate([sine, -sine], axis=-1),
    )


def rows_dot(left, right):
    return jnp.dot(left, right, preferred_element_type=jnp.float32)


def rows_dot_t(left, right):
    return lax.dot_general(left, right, NT, preferred_element_type=jnp.float32)


def exchange(values, axis, bit):
    size = lax.axis_size(axis)
    return lax.ppermute(values, axis, [(rank, rank ^ bit) for rank in range(size)])


def butterfly_sum(values, axis):
    size = lax.axis_size(axis)
    bit = 1
    while bit < size:
        values = values + exchange(values, axis, bit)
        bit *= 2
    return values


def tie(*values):
    return lax.optimization_barrier(values)


def scatter_small(values, axis):
    size = lax.axis_size(axis)
    rank = lax.axis_index(axis)
    kept = values
    bit = 1
    while bit < size:
        pairs = kept.reshape((kept.shape[0], kept.shape[1] // 2, 2) + kept.shape[2:])
        side = (rank // bit) % 2
        own = lax.dynamic_index_in_dim(pairs, side, axis=2, keepdims=False)
        away = lax.dynamic_index_in_dim(pairs, 1 - side, axis=2, keepdims=False)
        kept = own + exchange(away, axis, bit)
        bit *= 2
    return kept[:, 0]


class WeightGrad:
    def __init__(self, pieces, rights, start=1):
        self.pieces, self.rights = pieces, rights
        self.size, self.rank = lax.axis_size("dp"), lax.axis_index("dp").astype(jnp.int32)
        self.start = start
        self.tile = pieces[0].shape[1] // self.size
        self.width = sum(near.shape[1] for near in rights[::2])
        self.kernel = self.tile % 128 == 0

    def order(self):
        place = jnp.arange(self.size // 2, dtype=jnp.int32)
        blocks = place // self.start * (2 * self.start) + place % self.start
        side = (self.rank // self.start) % 2
        return blocks + self.start * (1 - side), blocks + self.start * side

    def compute(self, *groups):
        named = dict(zip(("send", "own"), self.order()))
        lists = [named[kind][first : first + count] for kind, first, count in groups]
        if self.kernel:
            order = jnp.concatenate(lists)
            return grad_call(order, [count for _, _, count in groups], self.pieces, self.rights, self.tile)
        left = jnp.concatenate(self.pieces, axis=0)
        sides = [jnp.concatenate(side, axis=1) for side in (self.rights[::2], self.rights[1::2])]
        full = lax.dot_general(left, jnp.concatenate(sides, axis=0), TN, preferred_element_type=jnp.float32)
        full = full.astype(jnp.bfloat16).reshape(self.size, self.tile, self.width)
        return [jnp.take(full, indices, axis=0) for indices in lists]

    def halve(self, blocks, bits, bit):
        low = 2 ** bits.index(bit)
        pairs = blocks.reshape((blocks.shape[0] // (2 * low), 2, low) + blocks.shape[1:])
        side = (self.rank // bit) % 2
        away, kept = (
            lax.dynamic_index_in_dim(pairs, at, axis=1, keepdims=False).reshape((-1,) + blocks.shape[1:])
            for at in (1 - side, side)
        )
        return away.astype(jnp.bfloat16), kept

    def bits(self):
        return [2**i for i in range(self.size.bit_length() - 1)]

    def finish(self, kept, got, bits, todo):
        while True:
            kept = kept.astype(jnp.float32) + got.astype(jnp.float32)
            if not todo:
                return kept.reshape(self.tile, self.width)
            away, kept = self.halve(kept, bits, todo[0])
            got = exchange(away, "dp", todo[0])
            bits = [b for b in bits if b != todo[0]]
            todo = todo[1:]

    def after_start(self, own, got):
        left = [b for b in self.bits() if b != self.start]
        return self.finish(own, got, left, left)

    def step(self, own, got, bits, bit):
        total = own.astype(jnp.float32) + got.astype(jnp.float32)
        away, kept = self.halve(total, bits, bit)
        return away, kept, [b for b in bits if b != bit]

    def second(self, own, got):
        total = own.astype(jnp.float32) + got.astype(jnp.float32)
        return self.halve(total, self.bits()[1:-1], 2)

    def third(self, kept, gots):
        first, second = (k + g.astype(jnp.float32) for k, g in zip(kept, gots))
        top = self.rank // (self.size // 2) == 1
        return jnp.where(top, first, second).astype(jnp.bfloat16), jnp.where(top, second, first)

    def last(self, kept, got):
        left = self.bits()[2:-1]
        return self.finish(kept, got, left, left)


def hop(values, bit):
    return exchange(values, "dp", bit)


def send_far(far):
    mine, others = far
    return (mine.astype(jnp.float32) + exchange(others, "tensor", 1).astype(jnp.float32)).astype(jnp.bfloat16)


def sum_near(near, got):
    mine, others = near
    return (
        mine.astype(jnp.float32)
        + exchange(others, "tensor", 1).astype(jnp.float32)
        + got.astype(jnp.float32)
    )


def shards(
    hidden_in,
    cotangent,
    gain_attn,
    w_query,
    w_key,
    w_value,
    w_out,
    gain_mlp,
    w_gate,
    w_up,
    w_down,
    doc_lengths,
    doc_groups,
    pad_mask,
):
    rows_local = hidden_in.shape[0]
    rank = lax.axis_index("tensor").astype(jnp.int32)
    rank_ref = rank[None]

    def to_far(values):
        return exchange(values, "tensor", 2)

    def to_mate(values):
        return exchange(values, "tensor", 1)

    x_f = hidden_in.astype(jnp.float32)
    inv_a = lax.rsqrt(jnp.mean(x_f * x_f, axis=-1, keepdims=True) + epsilon)
    a0 = (x_f * inv_a * gain_attn).astype(jnp.bfloat16)
    a2 = to_far(a0)
    a1 = to_mate(a0)
    a3 = to_mate(a2)

    inside, low, high, group_tok = row_tables(doc_lengths[0], doc_groups[0], pad_mask[0])
    low, high = low[None], high[None]
    real_tok = pad_mask[0].astype(jnp.float32)
    onehot_g = group_tok[:, None] == jnp.arange(GROUPS, dtype=jnp.int32)[None, :]
    counts = butterfly_sum(jnp.sum(jnp.where(onehot_g, real_tok[:, None], 0.0), axis=0), "dp")
    live = jnp.sum(counts)
    group_scale = jnp.sqrt(live / (GROUPS * jnp.maximum(counts, 1.0)))
    token_weight = real_tok * jnp.sum(jnp.where(onehot_g, group_scale[None, :], 0.0), axis=-1)
    weight_local = lax.dynamic_slice_in_dim(token_weight, rank * rows_local, rows_local)
    c0 = (cotangent.astype(jnp.float32) * weight_local[:, None]).astype(jnp.bfloat16)
    cosine, sine, back_sine = rope_tables(inside)

    near = qkv_pair(0, rank_ref, a0, a1, cosine, sine, w_query, w_key, w_value)
    a2, c0, *near = tie(a2, c0, *near)
    a3 = to_mate(a2)
    c2 = to_far(c0)
    c1 = to_mate(c0)
    far = qkv_pair(2, rank_ref, a2, a3, cosine, sine, w_query, w_key, w_value)
    qs, ks, vs = zip(near, far)
    heads_near, heads_far, lse = attend(rank_ref, qs, ks, vs, low, high)
    heads_far, c2 = tie(heads_far, c2)
    c3 = to_mate(c2)
    got = to_far(send_far(project([(heads_far, w_out, False)], True)))
    mid_h = x_f + sum_near(project([(heads_near, w_out, False)], True), got)
    inv_b = lax.rsqrt(jnp.mean(mid_h * mid_h, axis=-1, keepdims=True) + epsilon)
    b0 = (mid_h * inv_b * gain_mlp).astype(jnp.bfloat16)
    b0, c3 = tie(b0, c3)
    b2 = to_far(b0)
    b1 = to_mate(b0)
    mid_near, dg_near, du_near = mlp_pair(b0, b1, c0, c1, w_gate, w_up, w_down)
    b2, mid_near, dg_near, du_near = tie(b2, mid_near, dg_near, du_near)
    b3 = to_mate(b2)
    mid_far, dg_far, du_far = mlp_pair(b2, b3, c2, c3, w_gate, w_up, w_down)

    half = lax.axis_size("dp") // 2
    part = half // 2
    b_all, c_all = (b0, b1, b2, b3), (c0, c1, c2, c3)
    grad_down = WeightGrad(c_all, (mid_near, mid_far))
    grad_gate = WeightGrad(b_all, (dg_near, dg_far), 2)
    grad_up = WeightGrad(b_all, (du_near, du_far))
    sends, owns = ("send", 0, half), ("own", 0, half)
    both = (("send", 0, part), ("send", part, part), ("own", 0, part), ("own", part, part))
    (down_send,) = grad_down.compute(sends)
    (gate_send,) = grad_gate.compute(sends)
    dg_f, du_f, down_send, gate_send = tie(dg_far, du_far, down_send, gate_send)
    down_got = hop(down_send, 1)
    gate_got = hop(gate_send, 2)
    y5 = send_far(project([(dg_f, w_gate, True), (du_f, w_up, True)], True))
    got = to_far(y5)
    dg_n, du_n, y5 = tie(dg_near, du_near, y5)
    d_b = sum_near(project([(dg_n, w_gate, True), (du_n, w_up, True)], True), got)
    (down_own,) = grad_down.compute(owns)
    (gate_own,) = grad_gate.compute(owns)
    d_b, down_got, gate_got, down_own, gate_own = tie(d_b, down_got, gate_got, down_own, gate_own)

    away, down_own, down_bits = grad_down.step(down_own, down_got, grad_down.bits()[1:], 2)
    down_got = hop(away, 2)
    away, gate_own, gate_bits = grad_gate.step(
        gate_own, gate_got, [b for b in grad_gate.bits() if b != 2], 1
    )
    gate_got = hop(away, 1)
    n_b = mid_h * inv_b
    gain_mlp_part = jnp.sum(d_b * n_b, axis=0)
    e_b = d_b * gain_mlp
    weighted = cotangent.astype(jnp.float32) * weight_local[:, None]
    d_h = weighted + inv_b * (e_b - n_b * jnp.mean(e_b * n_b, axis=-1, keepdims=True))
    t0 = d_h.astype(jnp.bfloat16)
    t2 = to_far(t0)
    t1 = to_mate(t0)
    gs_near = project([((t0, t1), w_out, True)], False)
    up0, up1, own_u0, own_u1 = grad_up.compute(*both)
    t2, down_got, gate_got, gs_near, up0, up1 = tie(t2, down_got, gate_got, gs_near, up0, up1)

    up0_got = hop(up0, 1)
    away, gate_own, gate_bits = grad_gate.step(gate_own, gate_got, gate_bits, 4)
    gate_got = hop(away, 4)
    t3 = to_mate(t2)
    gs_far = project([((t2, t3), w_out, True)], False)
    y8 = send_far(project([(mid_far, w_down, False)], True))
    gs_far, y8 = tie(gs_far, y8)
    got8 = to_far(y8)
    dqn, dqf, dkn, dkf, dvn, dvf = attend_back(
        rank_ref, qs, ks, vs, (gs_near, gs_far), low, high, lse, cosine, back_sine
    )
    dqf, dkf, dvf, up0_got, gate_got, got8 = tie(dqf, dkf, dvf, up0_got, gate_got, got8)

    up1_got = hop(up1, 1)
    away, down_own, down_bits = grad_down.step(down_own, down_got, down_bits, 4)
    down_got = hop(away, 4)
    away, kept_u0 = grad_up.second(own_u0, up0_got)
    z_up0 = hop(away, 2)
    y7 = send_far(project([(dqf, w_query, True), (dkf, w_key, True), (dvf, w_value, True)], True))
    got = to_far(y7)
    dqn, dkn, dvn, y7 = tie(dqn, dkn, dvn, y7)
    d_a = sum_near(project([(dqn, w_query, True), (dkn, w_key, True), (dvn, w_value, True)], True), got)
    a_all = (a0, a1, a2, a3)
    grad_out = WeightGrad((t0, t1, t2, t3), (heads_near, heads_far))
    grad_v = WeightGrad(a_all, (dvn, dvf), 2)
    grad_q, grad_k = (WeightGrad(a_all, rights) for rights in ((dqn, dqf), (dkn, dkf)))
    v_send, v_own = grad_v.compute(sends, owns)
    q_send, q_own = grad_q.compute(sends, owns)
    k_send, k_own = grad_k.compute(sends, owns)
    d_a, up1_got, down_got, z_up0, v_send, q_send, k_send = tie(
        d_a, up1_got, down_got, z_up0, v_send, q_send, k_send
    )

    q_got = hop(q_send, 1)
    v_got = hop(v_send, 2)
    away, kept_u1 = grad_up.second(own_u1, up1_got)
    z_up1 = hop(away, 2)
    out_send, out_own = grad_out.compute(sends, owns)
    output = (mid_h + sum_near(project([(mid_near, w_down, False)], True), got8)).astype(jnp.bfloat16)
    n_a = x_f * inv_a
    gain_attn_part = jnp.sum(d_a * n_a, axis=0)
    e_a = d_a * gain_attn
    grad_input = d_h + inv_a * (e_a - n_a * jnp.mean(e_a * n_a, axis=-1, keepdims=True))
    gains = jnp.stack([gain_attn_part, gain_mlp_part])
    gains = butterfly_sum(scatter_small(gains.reshape(2, lax.axis_size("dp"), -1), "dp"), "tensor")
    sum_down = grad_down.finish(down_own, down_got, down_bits, down_bits)
    sum_gate = grad_gate.finish(gate_own, gate_got, gate_bits, gate_bits)
    u_away, u_kept = grad_up.third((kept_u0, kept_u1), (z_up0, z_up1))
    sum_up = grad_up.last(u_kept, hop(u_away, half))
    k_got = hop(tie(k_send, q_got)[0], 1)
    out_got = hop(tie(out_send, k_got)[0], 1)
    sum_out = grad_out.after_start(out_own, out_got)
    sums = [
        grad.after_start(own, got)
        for grad, own, got in ((grad_q, q_own, q_got), (grad_k, k_own, k_got), (grad_v, v_own, v_got))
    ]
    return (
        output,
        grad_input,
        gains[0],
        sums[0],
        sums[1],
        sums[2],
        sum_out.T,
        gains[1],
        sum_gate,
        sum_up,
        sum_down.T,
    )


def solution(mesh):
    rows, columns, split = P(("dp", "tensor"), None), P(None, "tensor"), P("tensor", None)
    in_specs = (
        rows,
        rows,
        P(),
        columns,
        columns,
        columns,
        split,
        P(),
        columns,
        columns,
        split,
        P("dp", None),
        P("dp", None),
        P("dp", None),
    )
    grads = P("dp", "tensor")
    grads_t = P("tensor", "dp")
    out_specs = (rows, rows, P("dp"), grads, grads, grads, grads_t, P("dp"), grads, grads, grads_t)
    return jax.shard_map(shards, mesh=mesh, in_specs=in_specs, out_specs=out_specs, check_vma=False)
```

```python
import functools

import jax
import jax.numpy as jnp
from jax import lax
from jax.experimental import pallas as pl
from jax.experimental.pallas import tpu as pltpu
from jax.sharding import PartitionSpec as P

HEAD_DIM = 128
ROWS = 1280
DOCS = 3
GROUPS = 8
QTILE = 256

epsilon = 1e-05
masked_score = -1e30
rope_base = 10000.0
COST = 1000


def cost(flops, bytes_accessed, transcendentals):
    return pl.CostEstimate(
        flops=flops // COST, bytes_accessed=bytes_accessed // COST, transcendentals=transcendentals // COST
    )


NT = (((1,), (1,)), ((), ()))
TN = (((0,), (0,)), ((), ()))
NN = (((1,), (0,)), ((), ()))


def mm(left, right, dims=NN):
    return lax.dot_general(left, right, dims, preferred_element_type=jnp.float32)


def whole(shape):
    return pl.BlockSpec(shape, lambda *_: (0,) * len(shape))


def turn(values, cosine, sine):
    return values * cosine + pltpu.roll(values, HEAD_DIM // 2, 1) * sine


def qkv_body(first, rank_ref, xa_ref, xb_ref, cos_ref, sin_ref, wq_ref, wk_ref, wv_ref, q_ref, k_ref, v_ref):
    rows = xa_ref.shape[0]
    for half, x_ref in enumerate((xa_ref, xb_ref)):
        span = pl.ds(half * rows, rows)
        x = x_ref[...]
        place = pl.ds(pl.multiple_of((rank_ref[0] ^ (first + half)) * rows, rows), rows)
        cosine, sine = cos_ref[place, :], sin_ref[place, :]
        for w_ref, out_ref in ((wq_ref, q_ref), (wk_ref, k_ref)):
            full = mm(x, w_ref[...])
            for head in range(full.shape[1] // HEAD_DIM):
                lanes = slice(head * HEAD_DIM, (head + 1) * HEAD_DIM)
                out_ref[span, lanes] = turn(full[:, lanes], cosine, sine).astype(jnp.bfloat16)
        v_ref[span, :] = mm(x, wv_ref[...]).astype(jnp.bfloat16)


def qkv_pair(first, rank, xa, xb, cosine, sine, wq, wk, wv):
    rows, depth = xa.shape
    width = wq.shape[1]
    tile = 256
    wspec = pl.BlockSpec((depth, tile), lambda j, *_: (0, j))
    ospec = pl.BlockSpec((2 * rows, tile), lambda j, *_: (0, j))
    out = jax.ShapeDtypeStruct((2 * rows, width), jnp.bfloat16)
    return pl.pallas_call(
        functools.partial(qkv_body, first),
        grid_spec=pltpu.PrefetchScalarGridSpec(
            num_scalar_prefetch=1,
            grid=(width // tile,),
            in_specs=[whole(xa.shape)] * 2 + [whole(cosine.shape)] * 2 + [wspec] * 3,
            out_specs=[ospec] * 3,
        ),
        out_shape=[out] * 3,
        compiler_params=pltpu.CompilerParams(vmem_limit_bytes=60 << 20),
        cost_estimate=cost(
            flops=12 * rows * depth * width, bytes_accessed=6 * depth * width + 4 * rows * depth, transcendentals=0
        ),
        name="qkv",
    )(rank, xa, xb, cosine, sine, wq, wk, wv)


def in_order(rank_ref, near_ref, far_ref, out_ref):
    piece = near_ref.shape[0] // 2
    for index in range(4):
        src = (near_ref, far_ref)[index // 2]
        at = pl.multiple_of((rank_ref[0] ^ index) * piece, piece)
        out_ref[pl.ds(at, piece), :] = src[pl.ds((index % 2) * piece, piece), :]


def out_of_order(rank_ref, src_ref, near_ref, far_ref):
    piece = near_ref.shape[0] // 2
    for index in range(4):
        dst = (near_ref, far_ref)[index // 2]
        at = pl.multiple_of((rank_ref[0] ^ index) * piece, piece)
        dst[pl.ds((index % 2) * piece, piece), :] = src_ref[pl.ds(at, piece), :].astype(dst.dtype)


def attend_body(rank_ref, qn, qf, kn, kf, vn, vf, low_ref, high_ref, on, of, lse_ref, q_s, k_s, v_s, o_s):
    in_order(rank_ref, qn, qf, q_s)
    in_order(rank_ref, kn, kf, k_s)
    in_order(rank_ref, vn, vf, v_s)
    scale = HEAD_DIM ** (-0.5)
    v_t = v_s[...].T
    for block in range(q_s.shape[0] // QTILE):
        span = pl.ds(block * QTILE, QTILE)
        end = (block + 1) * QTILE
        scores = mm(k_s[:end, :], q_s[span, :], NT)
        at = lax.broadcasted_iota(jnp.int32, scores.shape, 0)
        allowed = (at >= low_ref[:, span]) & (at <= high_ref[:, span])
        scores = jnp.where(allowed, scores * scale, masked_score)
        top = jnp.max(scores, axis=0, keepdims=True)
        prob = jnp.exp(scores - top)
        total = jnp.sum(prob, axis=0, keepdims=True)
        lse_ref[0, :, span] = top + jnp.log(total)
        out_t = mm(v_t[:, :end], prob.astype(jnp.bfloat16)) * (1.0 / total)
        o_s[span, :] = out_t.T
    out_of_order(rank_ref, o_s, on, of)


def attend(rank, qs, ks, vs, low, high):
    half, width = qs[0].shape
    rows = 2 * half
    heads = width // HEAD_DIM
    hspec = pl.BlockSpec((half, HEAD_DIM), lambda h, *_: (0, h))
    row = whole((1, rows))
    return pl.pallas_call(
        attend_body,
        grid_spec=pltpu.PrefetchScalarGridSpec(
            num_scalar_prefetch=1,
            grid=(heads,),
            in_specs=[hspec] * 6 + [row] * 2,
            out_specs=[hspec] * 2 + [pl.BlockSpec((1, 1, rows), lambda h, *_: (h, 0, 0))],
            scratch_shapes=[pltpu.VMEM((rows, HEAD_DIM), jnp.bfloat16)] * 3 + [pltpu.VMEM((rows, HEAD_DIM), jnp.float32)],
        ),
        out_shape=[jax.ShapeDtypeStruct((half, width), jnp.bfloat16)] * 2
        + [jax.ShapeDtypeStruct((heads, 1, rows), jnp.float32)],
        compiler_params=pltpu.CompilerParams(vmem_limit_bytes=60 << 20),
        cost_estimate=cost(
            flops=8 * rows * rows * width, bytes_accessed=8 * rows * width, transcendentals=heads * rows * rows // 2
        ),
        name="attend",
    )(rank, *qs, *ks, *vs, low, high)


def attend_back_body(
    rank_ref, qn, qf, kn, kf, vn, vf, gn, gf, low_ref, high_ref, lse_ref, cos_ref, sin_ref,
    dqn, dqf, dkn, dkf, dvn, dvf, q_s, k_s, v_s, g_s, dq_s, dk_s, dv_s,
):
    in_order(rank_ref, qn, qf, q_s)
    in_order(rank_ref, kn, kf, k_s)
    in_order(rank_ref, vn, vf, v_s)
    in_order(rank_ref, gn, gf, g_s)
    scale = HEAD_DIM ** (-0.5)
    k_t = k_s[...].T
    blocks = q_s.shape[0] // QTILE
    for block in reversed(range(blocks)):
        span = pl.ds(block * QTILE, QTILE)
        end = (block + 1) * QTILE
        query, grad = q_s[span, :], g_s[span, :]
        scores = mm(k_s[:end, :], query, NT) * scale
        at = lax.broadcasted_iota(jnp.int32, scores.shape, 0)
        allowed = (at >= low_ref[:, span]) & (at <= high_ref[:, span])
        prob = jnp.exp(jnp.where(allowed, scores, masked_score) - lse_ref[0, :, span])
        d_prob = mm(v_s[:end, :], grad, NT)
        dot = jnp.sum(prob * d_prob, axis=0, keepdims=True)
        d_score = (prob * (d_prob - dot) * scale).astype(jnp.bfloat16)
        dq_s[span, :] = mm(k_t[:, :end], d_score).T
        d_key = mm(d_score, query)
        d_value = mm(prob.astype(jnp.bfloat16), grad)
        if block == blocks - 1:
            dk_s[...] = d_key
            dv_s[...] = d_value
        else:
            dk_s[:end, :] += d_key
            dv_s[:end, :] += d_value
    dq_s[...] = turn(dq_s[...], cos_ref[...], sin_ref[...])
    dk_s[...] = turn(dk_s[...], cos_ref[...], sin_ref[...])
    out_of_order(rank_ref, dq_s, dqn, dqf)
    out_of_order(rank_ref, dk_s, dkn, dkf)
    out_of_order(rank_ref, dv_s, dvn, dvf)


def attend_back(rank, qs, ks, vs, gs, low, high, lse, cosine, back_sine):
    half, width = qs[0].shape
    rows = 2 * half
    heads = width // HEAD_DIM
    hspec = pl.BlockSpec((half, HEAD_DIM), lambda h, *_: (0, h))
    row = whole((1, rows))
    return pl.pallas_call(
        attend_back_body,
        grid_spec=pltpu.PrefetchScalarGridSpec(
            num_scalar_prefetch=1,
            grid=(heads,),
            in_specs=[hspec] * 8
            + [row] * 2
            + [pl.BlockSpec((1, 1, rows), lambda h, *_: (h, 0, 0))]
            + [whole((rows, HEAD_DIM))] * 2,
            out_specs=[hspec] * 6,
            scratch_shapes=[pltpu.VMEM((rows, HEAD_DIM), jnp.bfloat16)] * 4
            + [pltpu.VMEM((rows, HEAD_DIM), jnp.float32)] * 3,
        ),
        out_shape=[jax.ShapeDtypeStruct((half, width), jnp.bfloat16)] * 6,
        compiler_params=pltpu.CompilerParams(vmem_limit_bytes=60 << 20),
        cost_estimate=cost(
            flops=20 * rows * rows * width, bytes_accessed=16 * rows * width, transcendentals=heads * rows * rows // 2
        ),
        name="attend_back",
    )(rank, *qs, *ks, *vs, *gs, low, high, lse, cosine, back_sine)


def mlp_body(xa_ref, xb_ref, dm_ref, wg_ref, wu_ref, mid_ref, dg_ref, du_ref):
    rows = xa_ref.shape[0]
    for half, x_ref in enumerate((xa_ref, xb_ref)):
        span = pl.ds(half * rows, rows)
        x = x_ref[...]
        gate = mm(x, wg_ref[...])
        up = mm(x, wu_ref[...])
        d_mid = dm_ref[span, :]
        sigma = 1.0 / (1.0 + jnp.exp(-gate))
        active = gate * sigma
        mid_ref[span, :] = (active * up).astype(jnp.bfloat16)
        dg_ref[span, :] = (d_mid * up * sigma * (1.0 + gate * (1.0 - sigma))).astype(jnp.bfloat16)
        du_ref[span, :] = (d_mid * active).astype(jnp.bfloat16)


def mlp_pair(xa, xb, d_mid, wg, wu):
    rows, depth = xa.shape
    width = wg.shape[1]
    tile = 256
    wspec = pl.BlockSpec((depth, tile), lambda j: (0, j))
    ospec = pl.BlockSpec((2 * rows, tile), lambda j: (0, j))
    return pl.pallas_call(
        mlp_body,
        grid=(pl.cdiv(width, tile),),
        in_specs=[whole(xa.shape)] * 2 + [ospec] + [wspec] * 2,
        out_specs=[ospec] * 3,
        out_shape=[jax.ShapeDtypeStruct((2 * rows, width), jnp.bfloat16)] * 3,
        compiler_params=pltpu.CompilerParams(vmem_limit_bytes=60 << 20),
        cost_estimate=cost(
            flops=8 * rows * depth * width,
            bytes_accessed=4 * depth * width + 4 * rows * depth + 20 * rows * width,
            transcendentals=2 * rows * width,
        ),
        name="mlp",
    )(xa, xb, d_mid, wg, wu)


def gather_rows(parts, out_ref):
    at = 0
    for part in parts:
        out_ref[at : at + part.shape[0], :] = part[...]
        at += part.shape[0]


def gather_sides(rights, out_ref):
    at = 0
    for near, far in zip(rights[::2], rights[1::2]):
        rows, width = near.shape
        out_ref[:rows, at : at + width] = near[...]
        out_ref[rows:, at : at + width] = far[...]
        at += width


def block_at(place, low, side):
    return place // low * (2 * low) + place % low + low * side


def filled(step, low, side):
    group, half = step // (2 * low), step // low % 2
    here = jnp.where(half == side, step % low, jnp.where(half > side, low - 1, -1))
    return jnp.maximum(group * low + here, 0)


def grad_body(pieces, widths, low, sides, rank_ref, *refs):
    left, rights = refs[:pieces], refs[pieces : pieces + 2 * len(widths)]
    outs, (left_s, right_s) = refs[pieces + 2 * len(widths) : -2], refs[-2:]
    step = pl.program_id(0)

    @pl.when(step == 0)
    def _():
        gather_sides(rights, right_s)

    gather_rows(left, left_s)
    total = mm(left_s[...], right_s[...], TN).astype(jnp.bfloat16)

    def store(refs):
        at = 0
        for ref, width in zip(refs, widths):
            ref[0] = total[:, at : at + width]
            at += width

    if len(sides) == 1:
        store(outs)
    else:
        sent = step // low % 2 != rank_ref[0] // low % 2
        pl.when(sent)(lambda: store(outs[: len(widths)]))
        pl.when(jnp.logical_not(sent))(lambda: store(outs[len(widths) :]))


def grad_call(rank, pieces, mats, low, sides, tile):
    rows, depth = pieces[0].shape[0] * len(pieces), pieces[0].shape[1]
    widths = [near.shape[1] for near, _ in mats]
    width, half = sum(widths), depth // tile // 2
    count = half * len(sides)

    def own(s, side):
        bit = s[0] // low % 2
        return 1 - bit if side else bit

    if len(sides) == 1:
        lspec = pl.BlockSpec((pieces[0].shape[0], tile), lambda j, s: (0, block_at(j, low, own(s, sides[0]))))
    else:
        lspec = pl.BlockSpec((pieces[0].shape[0], tile), lambda j, s: (0, j))
    out_specs = []
    for side in sides:
        for w in widths:
            if len(sides) == 1:
                out_specs.append(pl.BlockSpec((1, tile, w), lambda j, s: (j, 0, 0)))
            else:
                out_specs.append(pl.BlockSpec((1, tile, w), lambda j, s, side=side: (filled(j, low, own(s, side)), 0, 0)))
    rights = [part for mat in mats for part in mat]
    return pl.pallas_call(
        functools.partial(grad_body, len(pieces), widths, low, sides),
        grid_spec=pltpu.PrefetchScalarGridSpec(
            num_scalar_prefetch=1,
            grid=(count,),
            in_specs=[lspec] * len(pieces) + [whole(r.shape) for r in rights],
            out_specs=out_specs,
            scratch_shapes=[pltpu.VMEM((rows, tile), jnp.bfloat16), pltpu.VMEM((rows, width), jnp.bfloat16)],
        ),
        out_shape=[jax.ShapeDtypeStruct((half, tile, w), jnp.bfloat16) for _ in sides for w in widths],
        compiler_params=pltpu.CompilerParams(vmem_limit_bytes=60 << 20),
        cost_estimate=cost(
            flops=2 * rows * tile * count * width,
            bytes_accessed=2 * rows * (tile * count + width) + 2 * tile * count * width,
            transcendentals=0,
        ),
        name="weight_grad",
    )(rank, *pieces, *rights)


def merge_body(_, own_away, got_away, own_kept, got_kept, away_ref, kept_ref):
    away_ref[...] = (own_away[...].astype(jnp.float32) + got_away[...].astype(jnp.float32)).astype(jnp.bfloat16)
    kept_ref[...] = (own_kept[...].astype(jnp.float32) + got_kept[...].astype(jnp.float32)).astype(jnp.bfloat16)


def merge_call(rank, own, got, low, bit):
    count, tile, width = own.shape
    away, kept = (
        pl.BlockSpec((1, tile, width), lambda j, s, flip=flip: (block_at(j, low, (s[0] // bit + flip) % 2), 0, 0))
        for flip in (1, 0)
    )
    ospec = pl.BlockSpec((1, tile, width), lambda j, s: (j, 0, 0))
    return pl.pallas_call(
        merge_body,
        grid_spec=pltpu.PrefetchScalarGridSpec(
            num_scalar_prefetch=1,
            grid=(count // 2,),
            in_specs=[away, away, kept, kept],
            out_specs=[ospec] * 2,
        ),
        out_shape=[jax.ShapeDtypeStruct((count // 2, tile, width), jnp.bfloat16)] * 2,
        compiler_params=pltpu.CompilerParams(vmem_limit_bytes=40 << 20),
        cost_estimate=cost(flops=count * tile * width, bytes_accessed=6 * count * tile * width, transcendentals=0),
        name="merge",
    )(rank, own, got, own, got)


def product(lefts, weights, half, rows):
    total = None
    for left, (w_ref, dims) in zip(lefts, weights):
        value = mm(left[half][...] if len(left) == 2 else left[0][pl.ds(half * rows, rows), :], w_ref[...], dims)
        total = value if total is None else total + value
    return total


def project_body(terms, *refs):
    at, lefts, weights = 0, [], []
    for pieces, dims in terms:
        lefts.append(refs[at : at + pieces])
        weights.append((refs[at + pieces], dims))
        at += pieces + 1
    out_ref = refs[at]
    rows = out_ref.shape[0] // 2
    for half in range(2):
        span = pl.ds(half * rows, rows)
        out_ref[span, :] = product(lefts, weights, half, rows).astype(out_ref.dtype)


def terms_of(terms):
    return [(left if isinstance(left, tuple) else (left,), w, NT if flip else NN) for left, w, flip in terms]


def term_specs(terms, tile):
    in_specs, args = [], []
    for left, w, dims in terms:
        depth = left[0].shape[1]
        in_specs += [whole(piece.shape) for piece in left]
        in_specs.append(
            pl.BlockSpec((tile, depth), lambda j: (j, 0)) if dims is NT else pl.BlockSpec((depth, tile), lambda j: (0, j))
        )
        args += [*left, w]
    return in_specs, args


def project(terms, dtype=jnp.bfloat16):
    terms = terms_of(terms)
    rows = sum(piece.shape[0] for piece in terms[0][0])
    width = terms[0][1].shape[0 if terms[0][2] is NT else 1]
    tile = min(512, width)
    in_specs, args = term_specs(terms, tile)
    return pl.pallas_call(
        functools.partial(project_body, [(len(left), dims) for left, _, dims in terms]),
        grid=(pl.cdiv(width, tile),),
        in_specs=in_specs,
        out_specs=pl.BlockSpec((rows, tile), lambda j: (0, j)),
        out_shape=jax.ShapeDtypeStruct((rows, width), dtype),
        compiler_params=pltpu.CompilerParams(vmem_limit_bytes=60 << 20),
        cost_estimate=cost(
            flops=2 * rows * width * sum(left[0].shape[1] for left, _, _ in terms),
            bytes_accessed=sum(2 * a.size for a in args) + 2 * rows * width,
            transcendentals=0,
        ),
        name="project",
    )(*args)


def pair_body(terms, steps, *refs):
    at, lefts, weights = 0, [], []
    for pieces, dims in terms:
        lefts.append(refs[at : at + pieces])
        weights.append((refs[at + pieces], dims))
        at += pieces + 1
    out_ref, mine_s, away_s, got_s, send_sem, recv_sem = refs[at:]
    rows = out_ref.shape[0]
    tile = mine_s.shape[2]
    step = pl.program_id(0)
    me = lax.axis_index("tensor")
    mate = {"tensor": me + 1 - 2 * (me % 2)}

    @pl.when(step == 0)
    def _():
        barrier = pltpu.get_barrier_semaphore()
        pl.semaphore_signal(barrier, inc=1, device_id=mate, device_id_type=pl.DeviceIdType.MESH)
        pl.semaphore_wait(barrier, 1)

    def copy(index):
        return pltpu.make_async_remote_copy(
            src_ref=away_s.at[index],
            dst_ref=got_s.at[index],
            send_sem=send_sem.at[index],
            recv_sem=recv_sem.at[index],
            device_id=mate,
            device_id_type=pl.DeviceIdType.MESH,
        )

    away_s[step] = product(lefts, weights, 1, rows).astype(jnp.bfloat16)
    copy(step).start()
    mine_s[step] = product(lefts, weights, 0, rows)

    @pl.when(step == steps - 1)
    def _():
        for index in range(steps):
            copy(index).wait()
            total = mine_s[index] + got_s[index].astype(jnp.float32)
            out_ref[:, index * tile : (index + 1) * tile] = total.astype(out_ref.dtype)


def pair_sum(terms, ident, dtype):
    terms = terms_of(terms)
    rows = sum(piece.shape[0] for piece in terms[0][0]) // 2
    width = terms[0][1].shape[0 if terms[0][2] is NT else 1]
    tile = min(512, width)
    steps = width // tile
    in_specs, args = term_specs(terms, tile)
    return pl.pallas_call(
        functools.partial(pair_body, [(len(left), dims) for left, _, dims in terms], steps),
        grid=(steps,),
        in_specs=in_specs,
        out_specs=whole((rows, width)),
        out_shape=jax.ShapeDtypeStruct((rows, width), dtype),
        scratch_shapes=[
            pltpu.VMEM((steps, rows, tile), jnp.float32),
            pltpu.VMEM((steps, rows, tile), jnp.bfloat16),
            pltpu.VMEM((steps, rows, tile), jnp.bfloat16),
            pltpu.SemaphoreType.DMA((steps,)),
            pltpu.SemaphoreType.DMA((steps,)),
        ],
        compiler_params=pltpu.CompilerParams(vmem_limit_bytes=60 << 20, collective_id=ident),
        cost_estimate=cost(
            flops=4 * rows * width * sum(left[0].shape[1] for left, _, _ in terms),
            bytes_accessed=sum(2 * a.size for a in args) + 4 * rows * width,
            transcendentals=0,
        ),
        name="pair_sum",
    )(*args)


def row_tables(length_row, group_row, mask_row):
    starts = jnp.cumsum(length_row) - length_row
    token = jnp.arange(ROWS, dtype=jnp.int32)
    doc_index = jnp.sum((token[:, None] >= starts[None, 1:]).astype(jnp.int32), axis=1)
    onehot = doc_index[:, None] == jnp.arange(DOCS, dtype=jnp.int32)[None, :]
    first = jnp.sum(jnp.where(onehot, starts[None, :], 0), axis=1)
    group_tok = jnp.sum(jnp.where(onehot, group_row[None, :], 0), axis=1)
    real = jnp.sum(jnp.where(onehot, mask_row[:, None], 0), axis=0)
    last_real = first + jnp.sum(jnp.where(onehot, real[None, :], 0), axis=1) - 1
    return (token - first, first, jnp.minimum(token, last_real), group_tok)


def rope_tables(inside):
    freq = rope_base ** (-jnp.arange(0, HEAD_DIM // 2, dtype=jnp.float32) * 2.0 / HEAD_DIM)
    angle = inside.astype(jnp.float32)[:, None] * freq[None, :]
    cosine, sine = jnp.cos(angle), jnp.sin(angle)
    return (
        jnp.concatenate([cosine, cosine], axis=-1),
        jnp.concatenate([-sine, sine], axis=-1),
        jnp.concatenate([sine, -sine], axis=-1),
    )


def rows_dot(left, right):
    return jnp.dot(left, right, preferred_element_type=jnp.float32)


def rows_dot_t(left, right):
    return lax.dot_general(left, right, NT, preferred_element_type=jnp.float32)


def exchange(values, axis, bit):
    size = lax.axis_size(axis)
    return lax.ppermute(values, axis, [(rank, rank ^ bit) for rank in range(size)])


def butterfly_sum(values, axis):
    size = lax.axis_size(axis)
    bit = 1
    while bit < size:
        values = values + exchange(values, axis, bit)
        bit *= 2
    return values


def tie(*values):
    return lax.optimization_barrier(values)


def scatter_small(values, axis):
    size = lax.axis_size(axis)
    rank = lax.axis_index(axis)
    kept = values
    bit = 1
    while bit < size:
        pairs = kept.reshape((kept.shape[0], kept.shape[1] // 2, 2) + kept.shape[2:])
        side = (rank // bit) % 2
        own = lax.dynamic_index_in_dim(pairs, side, axis=2, keepdims=False)
        away = lax.dynamic_index_in_dim(pairs, 1 - side, axis=2, keepdims=False)
        kept = own + exchange(away, axis, bit)
        bit *= 2
    return kept[:, 0]


class WeightGrad:
    def __init__(self, rank, pieces, mats, start=1):
        self.rank, self.pieces, self.mats, self.start = rank, pieces, mats, start
        self.size = lax.axis_size("dp")
        self.tile = pieces[0].shape[1] // self.size
        self.kernel = self.tile % 128 == 0

    def bits(self):
        return [2**i for i in range(self.size.bit_length() - 1)]

    def compute(self, *sides):
        if self.kernel:
            outs = grad_call(self.rank, self.pieces, self.mats, self.start, sides, self.tile)
        else:
            left = jnp.concatenate(self.pieces, axis=0)
            place = jnp.arange(self.size // 2, dtype=jnp.int32)
            bit = self.rank[0] // self.start % 2
            fulls = [
                lax.dot_general(left, jnp.concatenate(mat, axis=0), TN, preferred_element_type=jnp.float32)
                .astype(jnp.bfloat16)
                .reshape(self.size, self.tile, -1)
                for mat in self.mats
            ]
            outs = [
                jnp.take(full, block_at(place, self.start, (bit + side) % 2), axis=0) for side in sides for full in fulls
            ]
        return tuple(outs)


class Halving:
    def __init__(self, rank, own, start=1):
        self.rank, self.kept = rank, own
        self.size = lax.axis_size("dp")
        self.left = [2**i for i in range(self.size.bit_length() - 1) if 2**i != start]

    def merge(self, got, bit):
        low = 2 ** self.left.index(bit)
        self.left.remove(bit)
        if got.shape[1] % 128 == 0:
            away, self.kept = merge_call(self.rank, self.kept, got, low, bit)
            return away
        total = self.kept.astype(jnp.float32) + got.astype(jnp.float32)
        place = jnp.arange(total.shape[0] // 2, dtype=jnp.int32)
        side = self.rank[0] // bit % 2
        self.kept = jnp.take(total, block_at(place, low, side), axis=0)
        return jnp.take(total, block_at(place, low, 1 - side), axis=0).astype(jnp.bfloat16)

    def finish(self, got):
        while self.left:
            bit = self.left[0]
            got = exchange(self.merge(got, bit), "dp", bit)
        return (self.kept.astype(jnp.float32) + got.astype(jnp.float32))[0]


def hop(values, bit):
    return exchange(values, "dp", bit)


def shards(
    hidden_in,
    cotangent,
    gain_attn,
    w_query,
    w_key,
    w_value,
    w_out,
    gain_mlp,
    w_gate,
    w_up,
    w_down,
    doc_lengths,
    doc_groups,
    pad_mask,
):
    rows_local = hidden_in.shape[0]
    rank = lax.axis_index("tensor").astype(jnp.int32)
    rank_ref = rank[None]
    dp_rank = lax.axis_index("dp").astype(jnp.int32)[None]

    def to_far(values):
        return exchange(values, "tensor", 2)

    def to_mate(values):
        return exchange(values, "tensor", 1)

    x_f = hidden_in.astype(jnp.float32)
    inv_a = lax.rsqrt(jnp.mean(x_f * x_f, axis=-1, keepdims=True) + epsilon)
    a0 = (x_f * inv_a * gain_attn).astype(jnp.bfloat16)
    a2 = to_far(a0)
    a1 = to_mate(a0)
    a3 = to_mate(a2)

    inside, low, high, group_tok = row_tables(doc_lengths[0], doc_groups[0], pad_mask[0])
    low, high = low[None], high[None]
    real_tok = pad_mask[0].astype(jnp.float32)
    onehot_g = group_tok[:, None] == jnp.arange(GROUPS, dtype=jnp.int32)[None, :]
    counts = butterfly_sum(jnp.sum(jnp.where(onehot_g, real_tok[:, None], 0.0), axis=0), "dp")
    live = jnp.sum(counts)
    group_scale = jnp.sqrt(live / (GROUPS * jnp.maximum(counts, 1.0)))
    token_weight = real_tok * jnp.sum(jnp.where(onehot_g, group_scale[None, :], 0.0), axis=-1)
    weight_local = lax.dynamic_slice_in_dim(token_weight, rank * rows_local, rows_local)
    c0 = (cotangent.astype(jnp.float32) * weight_local[:, None]).astype(jnp.bfloat16)
    cosine, sine, back_sine = rope_tables(inside)

    near = qkv_pair(0, rank_ref, a0, a1, cosine, sine, w_query, w_key, w_value)
    a2, c0, *near = tie(a2, c0, *near)
    a3 = to_mate(a2)
    c2 = to_far(c0)
    c1 = to_mate(c0)
    far = qkv_pair(2, rank_ref, a2, a3, cosine, sine, w_query, w_key, w_value)
    qs, ks, vs = zip(near, far)
    heads_near, heads_far, lse = attend(rank_ref, qs, ks, vs, low, high)
    y1 = pair_sum([(heads_far, w_out, False)], 0, jnp.bfloat16)
    heads_n, c1, c2, y1 = tie(heads_near, c1, c2, y1)
    got = to_far(y1)
    c3 = to_mate(c2)
    mine = pair_sum([(heads_n, w_out, False)], 1, jnp.float32)
    dm_near = project([((c0, c1), w_down, True)], jnp.float32)
    dm_far = project([((c2, c3), w_down, True)], jnp.float32)
    mid_h = x_f + mine + got.astype(jnp.float32)
    inv_b = lax.rsqrt(jnp.mean(mid_h * mid_h, axis=-1, keepdims=True) + epsilon)
    b0 = (mid_h * inv_b * gain_mlp).astype(jnp.bfloat16)
    b0, dm_near, dm_far = tie(b0, dm_near, dm_far)
    b2 = to_far(b0)
    b1 = to_mate(b0)
    mid_near, dg_near, du_near = mlp_pair(b0, b1, dm_near, w_gate, w_up)
    b2, mid_near, dg_near, du_near = tie(b2, mid_near, dg_near, du_near)
    b3 = to_mate(b2)
    mid_far, dg_far, du_far = mlp_pair(b2, b3, dm_far, w_gate, w_up)

    half = lax.axis_size("dp") // 2
    b_all, c_all = (b0, b1, b2, b3), (c0, c1, c2, c3)
    grad_down = WeightGrad(dp_rank, c_all, [(mid_near, mid_far)])
    grad_gate = WeightGrad(dp_rank, b_all, [(dg_near, dg_far)], 2)
    (down_send,) = grad_down.compute(1)
    dg_f, du_f, down_send = tie(dg_far, du_far, down_send)
    down_got = hop(down_send, 1)
    (gate_send,) = grad_gate.compute(1)
    y5 = pair_sum([(dg_f, w_gate, True), (du_f, w_up, True)], 2, jnp.bfloat16)
    dg_n, du_n, y5 = tie(dg_near, du_near, y5)
    gate_got = hop(gate_send, 2)
    got = to_far(y5)
    d_b = pair_sum([(dg_n, w_gate, True), (du_n, w_up, True)], 3, jnp.float32) + got.astype(jnp.float32)
    (up_send,) = WeightGrad(dp_rank, b_all, [(du_n, du_far)]).compute(1)
    d_b, up_send = tie(d_b, up_send)

    n_b = mid_h * inv_b
    gain_mlp_part = jnp.sum(d_b * n_b, axis=0)
    e_b = d_b * gain_mlp
    weighted = cotangent.astype(jnp.float32) * weight_local[:, None]
    d_h = weighted + inv_b * (e_b - n_b * jnp.mean(e_b * n_b, axis=-1, keepdims=True))
    t0 = d_h.astype(jnp.bfloat16)
    t0, mid_f, dg_n, du_n = tie(t0, mid_far, dg_near, du_near)
    t2 = to_far(t0)
    t1 = to_mate(t0)
    gs_near = project([((t0, t1), w_out, True)])
    y8 = pair_sum([(mid_f, w_down, False)], 4, jnp.bfloat16)
    (down_own,) = WeightGrad(dp_rank, c_all, [(mid_near, mid_f)]).compute(0)
    (gate_own,) = WeightGrad(dp_rank, b_all, [(dg_n, dg_far)], 2).compute(0)
    t2, down_got, gate_got, gs_near, y8, down_own, gate_own = tie(t2, down_got, gate_got, gs_near, y8, down_own, gate_own)

    up_got = hop(up_send, 1)
    got8 = to_far(y8)
    down, gate = Halving(dp_rank, down_own), Halving(dp_rank, gate_own, 2)
    down_got = hop(down.merge(down_got, 2), 2)
    t3 = to_mate(t2)
    gs_far = project([((t2, t3), w_out, True)])
    gate_away = gate.merge(gate_got, 1)
    out_send, out_own = WeightGrad(dp_rank, (t0, t1, t2, t3), [(heads_near, heads_far)]).compute(1, 0)
    dqn, dqf, dkn, dkf, dvn, dvf = attend_back(
        rank_ref, qs, ks, vs, (gs_near, gs_far), low, high, lse, cosine, back_sine
    )
    dqf, dkf, dvf, down_got, got8, out_send, gate_away = tie(dqf, dkf, dvf, down_got, got8, out_send, gate_away)

    out_got = hop(out_send, 1)
    y7 = pair_sum([(dqf, w_query, True), (dkf, w_key, True), (dvf, w_value, True)], 6, jnp.bfloat16)
    dqn, dkn, dvn, dun, y7 = tie(dqn, dkn, dvn, du_near, y7)
    got = to_far(y7)
    grad_qkv = WeightGrad(dp_rank, (a0, a1, a2, a3), [(dqn, dqf), (dkn, dkf), (dvn, dvf)])
    *sends, q_own, k_own, v_own = grad_qkv.compute(1, 0)
    down_got = hop(down.merge(down_got, half), half)
    d_a = pair_sum([(dqn, w_query, True), (dkn, w_key, True), (dvn, w_value, True)], 7, jnp.float32) + got.astype(jnp.float32)
    (up_own,) = WeightGrad(dp_rank, b_all, [(dun, du_far)]).compute(0)
    d_a, up_own, up_got, out_got, gate_away, down_got, *sends = tie(
        d_a, up_own, up_got, out_got, gate_away, down_got, *sends
    )

    gate_got = hop(gate_away, 1)
    up = Halving(dp_rank, up_own)
    up_got = hop(up.merge(up_got, 2), 2)
    output = (mid_h + pair_sum([(mid_near, w_down, False)], 5, jnp.float32) + got8.astype(jnp.float32)).astype(jnp.bfloat16)
    n_a = x_f * inv_a
    gain_attn_part = jnp.sum(d_a * n_a, axis=0)
    e_a = d_a * gain_attn
    grad_input = d_h + inv_a * (e_a - n_a * jnp.mean(e_a * n_a, axis=-1, keepdims=True))
    gains = jnp.stack([gain_attn_part, gain_mlp_part])
    gains = butterfly_sum(scatter_small(gains.reshape(2, lax.axis_size("dp"), -1), "dp"), "tensor")
    sum_down = down.finish(down_got)
    sum_gate = gate.finish(gate_got)
    sum_up = up.finish(up_got)
    sum_out = Halving(dp_rank, out_own).finish(out_got)
    sums, last = [], gate_got
    for send, own in zip(sends, (q_own, k_own, v_own)):
        send, last = tie(send, last)
        last = hop(send, 1)
        sums.append(Halving(dp_rank, own).finish(last))
    return (
        output,
        grad_input,
        gains[0],
        sums[0],
        sums[1],
        sums[2],
        sum_out.T,
        gains[1],
        sum_gate,
        sum_up,
        sum_down.T,
    )


def solution(mesh):
    rows, columns, split = P(("dp", "tensor"), None), P(None, "tensor"), P("tensor", None)
    in_specs = (
        rows,
        rows,
        P(),
        columns,
        columns,
        columns,
        split,
        P(),
        columns,
        columns,
        split,
        P("dp", None),
        P("dp", None),
        P("dp", None),
    )
    grads = P("dp", "tensor")
    grads_t = P("tensor", "dp")
    out_specs = (rows, rows, P("dp"), grads, grads, grads, grads_t, P("dp"), grads, grads, grads_t)
    return jax.shard_map(shards, mesh=mesh, in_specs=in_specs, out_specs=out_specs, check_vma=False)
```

```python
import functools

import jax
import jax.numpy as jnp
from jax import lax
from jax.experimental import pallas as pl
from jax.experimental.pallas import tpu as pltpu
from jax.sharding import PartitionSpec as P

HEAD_DIM = 128
ROWS = 1280
DOCS = 3
GROUPS = 8
QTILE = 256

epsilon = 1e-05
masked_score = -1e30
rope_base = 10000.0
COST = 1000


def cost(flops, bytes_accessed, transcendentals):
    return pl.CostEstimate(
        flops=flops // COST, bytes_accessed=bytes_accessed // COST, transcendentals=transcendentals // COST
    )


NT = (((1,), (1,)), ((), ()))
TN = (((0,), (0,)), ((), ()))
NN = (((1,), (0,)), ((), ()))


def mm(left, right, dims=NN):
    return lax.dot_general(left, right, dims, preferred_element_type=jnp.float32)


def whole(shape):
    return pl.BlockSpec(shape, lambda *_: (0,) * len(shape))


def turn(values, cosine, sine):
    return values * cosine + pltpu.roll(values, HEAD_DIM // 2, 1) * sine


def qkv_body(first, rank_ref, xa_ref, xb_ref, cos_ref, sin_ref, wq_ref, wk_ref, wv_ref, q_ref, k_ref, v_ref):
    rows = xa_ref.shape[0]
    for half, x_ref in enumerate((xa_ref, xb_ref)):
        span = pl.ds(half * rows, rows)
        x = x_ref[...]
        place = pl.ds(pl.multiple_of((rank_ref[0] ^ (first + half)) * rows, rows), rows)
        cosine, sine = cos_ref[place, :], sin_ref[place, :]
        for w_ref, out_ref in ((wq_ref, q_ref), (wk_ref, k_ref)):
            full = mm(x, w_ref[...])
            for head in range(full.shape[1] // HEAD_DIM):
                lanes = slice(head * HEAD_DIM, (head + 1) * HEAD_DIM)
                out_ref[span, lanes] = turn(full[:, lanes], cosine, sine).astype(jnp.bfloat16)
        v_ref[span, :] = mm(x, wv_ref[...]).astype(jnp.bfloat16)


def qkv_pair(first, rank, xa, xb, cosine, sine, wq, wk, wv):
    rows, depth = xa.shape
    width = wq.shape[1]
    tile = 256
    wspec = pl.BlockSpec((depth, tile), lambda j, *_: (0, j))
    ospec = pl.BlockSpec((2 * rows, tile), lambda j, *_: (0, j))
    out = jax.ShapeDtypeStruct((2 * rows, width), jnp.bfloat16)
    return pl.pallas_call(
        functools.partial(qkv_body, first),
        grid_spec=pltpu.PrefetchScalarGridSpec(
            num_scalar_prefetch=1,
            grid=(width // tile,),
            in_specs=[whole(xa.shape)] * 2 + [whole(cosine.shape)] * 2 + [wspec] * 3,
            out_specs=[ospec] * 3,
        ),
        out_shape=[out] * 3,
        compiler_params=pltpu.CompilerParams(vmem_limit_bytes=60 << 20),
        cost_estimate=cost(
            flops=12 * rows * depth * width, bytes_accessed=6 * depth * width + 4 * rows * depth, transcendentals=0
        ),
        name="qkv",
    )(rank, xa, xb, cosine, sine, wq, wk, wv)


def in_order(rank_ref, near_ref, far_ref, out_ref):
    piece = near_ref.shape[0] // 2
    for index in range(4):
        src = (near_ref, far_ref)[index // 2]
        at = pl.multiple_of((rank_ref[0] ^ index) * piece, piece)
        out_ref[pl.ds(at, piece), :] = src[pl.ds((index % 2) * piece, piece), :]


def out_of_order(rank_ref, src_ref, near_ref, far_ref):
    piece = near_ref.shape[0] // 2
    for index in range(4):
        dst = (near_ref, far_ref)[index // 2]
        at = pl.multiple_of((rank_ref[0] ^ index) * piece, piece)
        dst[pl.ds((index % 2) * piece, piece), :] = src_ref[pl.ds(at, piece), :].astype(dst.dtype)


def attend_body(rank_ref, qn, qf, kn, kf, vn, vf, low_ref, high_ref, on, of, lse_ref, q_s, k_s, v_s, o_s):
    in_order(rank_ref, qn, qf, q_s)
    in_order(rank_ref, kn, kf, k_s)
    in_order(rank_ref, vn, vf, v_s)
    scale = HEAD_DIM ** (-0.5)
    v_t = v_s[...].T
    for block in range(q_s.shape[0] // QTILE):
        span = pl.ds(block * QTILE, QTILE)
        end = (block + 1) * QTILE
        scores = mm(k_s[:end, :], q_s[span, :], NT)
        at = lax.broadcasted_iota(jnp.int32, scores.shape, 0)
        allowed = (at >= low_ref[:, span]) & (at <= high_ref[:, span])
        scores = jnp.where(allowed, scores * scale, masked_score)
        top = jnp.max(scores, axis=0, keepdims=True)
        prob = jnp.exp(scores - top)
        total = jnp.sum(prob, axis=0, keepdims=True)
        lse_ref[0, :, span] = top + jnp.log(total)
        out_t = mm(v_t[:, :end], prob.astype(jnp.bfloat16)) * (1.0 / total)
        o_s[span, :] = out_t.T
    out_of_order(rank_ref, o_s, on, of)


def attend(rank, qs, ks, vs, low, high):
    half, width = qs[0].shape
    rows = 2 * half
    heads = width // HEAD_DIM
    hspec = pl.BlockSpec((half, HEAD_DIM), lambda h, *_: (0, h))
    row = whole((1, rows))
    return pl.pallas_call(
        attend_body,
        grid_spec=pltpu.PrefetchScalarGridSpec(
            num_scalar_prefetch=1,
            grid=(heads,),
            in_specs=[hspec] * 6 + [row] * 2,
            out_specs=[hspec] * 2 + [pl.BlockSpec((1, 1, rows), lambda h, *_: (h, 0, 0))],
            scratch_shapes=[pltpu.VMEM((rows, HEAD_DIM), jnp.bfloat16)] * 3 + [pltpu.VMEM((rows, HEAD_DIM), jnp.float32)],
        ),
        out_shape=[jax.ShapeDtypeStruct((half, width), jnp.bfloat16)] * 2
        + [jax.ShapeDtypeStruct((heads, 1, rows), jnp.float32)],
        compiler_params=pltpu.CompilerParams(vmem_limit_bytes=60 << 20),
        cost_estimate=cost(
            flops=8 * rows * rows * width, bytes_accessed=8 * rows * width, transcendentals=heads * rows * rows // 2
        ),
        name="attend",
    )(rank, *qs, *ks, *vs, low, high)


def attend_back_body(
    rank_ref, qn, qf, kn, kf, vn, vf, gn, gf, low_ref, high_ref, lse_ref, cos_ref, sin_ref,
    dqn, dqf, dkn, dkf, dvn, dvf, q_s, k_s, v_s, g_s, dq_s, dk_s, dv_s,
):
    in_order(rank_ref, qn, qf, q_s)
    in_order(rank_ref, kn, kf, k_s)
    in_order(rank_ref, vn, vf, v_s)
    in_order(rank_ref, gn, gf, g_s)
    scale = HEAD_DIM ** (-0.5)
    k_t = k_s[...].T
    blocks = q_s.shape[0] // QTILE
    for block in reversed(range(blocks)):
        span = pl.ds(block * QTILE, QTILE)
        end = (block + 1) * QTILE
        query, grad = q_s[span, :], g_s[span, :]
        scores = mm(k_s[:end, :], query, NT) * scale
        at = lax.broadcasted_iota(jnp.int32, scores.shape, 0)
        allowed = (at >= low_ref[:, span]) & (at <= high_ref[:, span])
        prob = jnp.exp(jnp.where(allowed, scores, masked_score) - lse_ref[0, :, span])
        d_prob = mm(v_s[:end, :], grad, NT)
        dot = jnp.sum(prob * d_prob, axis=0, keepdims=True)
        d_score = (prob * (d_prob - dot) * scale).astype(jnp.bfloat16)
        dq_s[span, :] = mm(k_t[:, :end], d_score).T
        d_key = mm(d_score, query)
        d_value = mm(prob.astype(jnp.bfloat16), grad)
        if block == blocks - 1:
            dk_s[...] = d_key
            dv_s[...] = d_value
        else:
            dk_s[:end, :] += d_key
            dv_s[:end, :] += d_value
    dq_s[...] = turn(dq_s[...], cos_ref[...], sin_ref[...])
    dk_s[...] = turn(dk_s[...], cos_ref[...], sin_ref[...])
    out_of_order(rank_ref, dq_s, dqn, dqf)
    out_of_order(rank_ref, dk_s, dkn, dkf)
    out_of_order(rank_ref, dv_s, dvn, dvf)


def attend_back(rank, qs, ks, vs, gs, low, high, lse, cosine, back_sine):
    half, width = qs[0].shape
    rows = 2 * half
    heads = width // HEAD_DIM
    hspec = pl.BlockSpec((half, HEAD_DIM), lambda h, *_: (0, h))
    row = whole((1, rows))
    return pl.pallas_call(
        attend_back_body,
        grid_spec=pltpu.PrefetchScalarGridSpec(
            num_scalar_prefetch=1,
            grid=(heads,),
            in_specs=[hspec] * 8
            + [row] * 2
            + [pl.BlockSpec((1, 1, rows), lambda h, *_: (h, 0, 0))]
            + [whole((rows, HEAD_DIM))] * 2,
            out_specs=[hspec] * 6,
            scratch_shapes=[pltpu.VMEM((rows, HEAD_DIM), jnp.bfloat16)] * 4
            + [pltpu.VMEM((rows, HEAD_DIM), jnp.float32)] * 3,
        ),
        out_shape=[jax.ShapeDtypeStruct((half, width), jnp.bfloat16)] * 6,
        compiler_params=pltpu.CompilerParams(vmem_limit_bytes=60 << 20),
        cost_estimate=cost(
            flops=20 * rows * rows * width, bytes_accessed=16 * rows * width, transcendentals=heads * rows * rows // 2
        ),
        name="attend_back",
    )(rank, *qs, *ks, *vs, *gs, low, high, lse, cosine, back_sine)


def mlp_body(xa_ref, xb_ref, dm_ref, wg_ref, wu_ref, mid_ref, dg_ref, du_ref):
    rows = xa_ref.shape[0]
    for half, x_ref in enumerate((xa_ref, xb_ref)):
        span = pl.ds(half * rows, rows)
        x = x_ref[...]
        gate = mm(x, wg_ref[...])
        up = mm(x, wu_ref[...])
        d_mid = dm_ref[span, :]
        sigma = 1.0 / (1.0 + jnp.exp(-gate))
        active = gate * sigma
        mid_ref[span, :] = (active * up).astype(jnp.bfloat16)
        dg_ref[span, :] = (d_mid * up * sigma * (1.0 + gate * (1.0 - sigma))).astype(jnp.bfloat16)
        du_ref[span, :] = (d_mid * active).astype(jnp.bfloat16)


def mlp_pair(xa, xb, d_mid, wg, wu):
    rows, depth = xa.shape
    width = wg.shape[1]
    tile = 256
    wspec = pl.BlockSpec((depth, tile), lambda j: (0, j))
    ospec = pl.BlockSpec((2 * rows, tile), lambda j: (0, j))
    return pl.pallas_call(
        mlp_body,
        grid=(pl.cdiv(width, tile),),
        in_specs=[whole(xa.shape)] * 2 + [ospec] + [wspec] * 2,
        out_specs=[ospec] * 3,
        out_shape=[jax.ShapeDtypeStruct((2 * rows, width), jnp.bfloat16)] * 3,
        compiler_params=pltpu.CompilerParams(vmem_limit_bytes=60 << 20),
        cost_estimate=cost(
            flops=8 * rows * depth * width,
            bytes_accessed=4 * depth * width + 4 * rows * depth + 20 * rows * width,
            transcendentals=2 * rows * width,
        ),
        name="mlp",
    )(xa, xb, d_mid, wg, wu)


def gather_rows(parts, out_ref):
    at = 0
    for part in parts:
        out_ref[at : at + part.shape[0], :] = part[...]
        at += part.shape[0]


def gather_sides(rights, out_ref):
    at = 0
    for near, far in zip(rights[::2], rights[1::2]):
        rows, width = near.shape
        out_ref[:rows, at : at + width] = near[...]
        out_ref[rows:, at : at + width] = far[...]
        at += width


def block_at(place, low, side):
    return place // low * (2 * low) + place % low + low * side


def filled(step, low, side):
    group, half = step // (2 * low), step // low % 2
    here = jnp.where(half == side, step % low, jnp.where(half > side, low - 1, -1))
    return jnp.maximum(group * low + here, 0)


def grad_body(pieces, widths, low, sides, rank_ref, *refs):
    left, rights = refs[:pieces], refs[pieces : pieces + 2 * len(widths)]
    outs, (left_s, right_s) = refs[pieces + 2 * len(widths) : -2], refs[-2:]
    step = pl.program_id(0)

    @pl.when(step == 0)
    def _():
        gather_sides(rights, right_s)

    gather_rows(left, left_s)
    total = mm(left_s[...], right_s[...], TN).astype(jnp.bfloat16)

    def store(refs):
        at = 0
        for ref, width in zip(refs, widths):
            ref[0] = total[:, at : at + width]
            at += width

    if len(sides) == 1:
        store(outs)
    else:
        sent = step // low % 2 != rank_ref[0] // low % 2
        pl.when(sent)(lambda: store(outs[: len(widths)]))
        pl.when(jnp.logical_not(sent))(lambda: store(outs[len(widths) :]))


def grad_call(rank, pieces, mats, low, sides, tile):
    rows, depth = pieces[0].shape[0] * len(pieces), pieces[0].shape[1]
    widths = [near.shape[1] for near, _ in mats]
    width, half = sum(widths), depth // tile // 2
    count = half * len(sides)

    def own(s, side):
        bit = s[0] // low % 2
        return 1 - bit if side else bit

    if len(sides) == 1:
        lspec = pl.BlockSpec((pieces[0].shape[0], tile), lambda j, s: (0, block_at(j, low, own(s, sides[0]))))
    else:
        lspec = pl.BlockSpec((pieces[0].shape[0], tile), lambda j, s: (0, j))
    out_specs = []
    for side in sides:
        for w in widths:
            if len(sides) == 1:
                out_specs.append(pl.BlockSpec((1, tile, w), lambda j, s: (j, 0, 0)))
            else:
                out_specs.append(pl.BlockSpec((1, tile, w), lambda j, s, side=side: (filled(j, low, own(s, side)), 0, 0)))
    rights = [part for mat in mats for part in mat]
    return pl.pallas_call(
        functools.partial(grad_body, len(pieces), widths, low, sides),
        grid_spec=pltpu.PrefetchScalarGridSpec(
            num_scalar_prefetch=1,
            grid=(count,),
            in_specs=[lspec] * len(pieces) + [whole(r.shape) for r in rights],
            out_specs=out_specs,
            scratch_shapes=[pltpu.VMEM((rows, tile), jnp.bfloat16), pltpu.VMEM((rows, width), jnp.bfloat16)],
        ),
        out_shape=[jax.ShapeDtypeStruct((half, tile, w), jnp.bfloat16) for _ in sides for w in widths],
        compiler_params=pltpu.CompilerParams(vmem_limit_bytes=60 << 20),
        cost_estimate=cost(
            flops=2 * rows * tile * count * width,
            bytes_accessed=2 * rows * (tile * count + width) + 2 * tile * count * width,
            transcendentals=0,
        ),
        name="weight_grad",
    )(rank, *pieces, *rights)


def merge_body(_, own_away, got_away, own_kept, got_kept, away_ref, kept_ref):
    away_ref[...] = (own_away[...].astype(jnp.float32) + got_away[...].astype(jnp.float32)).astype(jnp.bfloat16)
    kept_ref[...] = (own_kept[...].astype(jnp.float32) + got_kept[...].astype(jnp.float32)).astype(jnp.bfloat16)


def merge_call(rank, own, got, low, bit):
    count, tile, width = own.shape
    away, kept = (
        pl.BlockSpec((1, tile, width), lambda j, s, flip=flip: (block_at(j, low, (s[0] // bit + flip) % 2), 0, 0))
        for flip in (1, 0)
    )
    ospec = pl.BlockSpec((1, tile, width), lambda j, s: (j, 0, 0))
    return pl.pallas_call(
        merge_body,
        grid_spec=pltpu.PrefetchScalarGridSpec(
            num_scalar_prefetch=1,
            grid=(count // 2,),
            in_specs=[away, away, kept, kept],
            out_specs=[ospec] * 2,
        ),
        out_shape=[jax.ShapeDtypeStruct((count // 2, tile, width), jnp.bfloat16)] * 2,
        compiler_params=pltpu.CompilerParams(vmem_limit_bytes=40 << 20),
        cost_estimate=cost(flops=count * tile * width, bytes_accessed=6 * count * tile * width, transcendentals=0),
        name="merge",
    )(rank, own, got, own, got)


def product(lefts, weights, half, rows):
    total = None
    for left, (w_ref, dims) in zip(lefts, weights):
        value = mm(left[half][...] if len(left) == 2 else left[0][pl.ds(half * rows, rows), :], w_ref[...], dims)
        total = value if total is None else total + value
    return total


def project_body(terms, *refs):
    at, lefts, weights = 0, [], []
    for pieces, dims in terms:
        lefts.append(refs[at : at + pieces])
        weights.append((refs[at + pieces], dims))
        at += pieces + 1
    out_ref = refs[at]
    rows = out_ref.shape[0] // 2
    for half in range(2):
        span = pl.ds(half * rows, rows)
        out_ref[span, :] = product(lefts, weights, half, rows).astype(out_ref.dtype)


def terms_of(terms):
    return [(left if isinstance(left, tuple) else (left,), w, NT if flip else NN) for left, w, flip in terms]


def term_specs(terms, tile):
    in_specs, args = [], []
    for left, w, dims in terms:
        depth = left[0].shape[1]
        in_specs += [whole(piece.shape) for piece in left]
        in_specs.append(
            pl.BlockSpec((tile, depth), lambda j: (j, 0)) if dims is NT else pl.BlockSpec((depth, tile), lambda j: (0, j))
        )
        args += [*left, w]
    return in_specs, args


def project(terms, dtype=jnp.bfloat16):
    terms = terms_of(terms)
    rows = sum(piece.shape[0] for piece in terms[0][0])
    width = terms[0][1].shape[0 if terms[0][2] is NT else 1]
    tile = min(512, width)
    in_specs, args = term_specs(terms, tile)
    return pl.pallas_call(
        functools.partial(project_body, [(len(left), dims) for left, _, dims in terms]),
        grid=(pl.cdiv(width, tile),),
        in_specs=in_specs,
        out_specs=pl.BlockSpec((rows, tile), lambda j: (0, j)),
        out_shape=jax.ShapeDtypeStruct((rows, width), dtype),
        compiler_params=pltpu.CompilerParams(vmem_limit_bytes=60 << 20),
        cost_estimate=cost(
            flops=2 * rows * width * sum(left[0].shape[1] for left, _, _ in terms),
            bytes_accessed=sum(2 * a.size for a in args) + 2 * rows * width,
            transcendentals=0,
        ),
        name="project",
    )(*args)


def pair_body(terms, steps, *refs):
    at, lefts, weights = 0, [], []
    for pieces, dims in terms:
        lefts.append(refs[at : at + pieces])
        weights.append((refs[at + pieces], dims))
        at += pieces + 1
    out_ref, mine_s, away_s, got_s, send_sem, recv_sem = refs[at:]
    rows = out_ref.shape[0]
    tile = mine_s.shape[2]
    step = pl.program_id(0)
    me = lax.axis_index("tensor")
    mate = {"tensor": me + 1 - 2 * (me % 2)}

    @pl.when(step == 0)
    def _():
        barrier = pltpu.get_barrier_semaphore()
        pl.semaphore_signal(barrier, inc=1, device_id=mate, device_id_type=pl.DeviceIdType.MESH)
        pl.semaphore_wait(barrier, 1)

    def copy(index):
        return pltpu.make_async_remote_copy(
            src_ref=away_s.at[index],
            dst_ref=got_s.at[index],
            send_sem=send_sem.at[index],
            recv_sem=recv_sem.at[index],
            device_id=mate,
            device_id_type=pl.DeviceIdType.MESH,
        )

    away_s[step] = product(lefts, weights, 1, rows).astype(jnp.bfloat16)
    copy(step).start()
    mine_s[step] = product(lefts, weights, 0, rows)

    @pl.when(step == steps - 1)
    def _():
        for index in range(steps):
            copy(index).wait()
            total = mine_s[index] + got_s[index].astype(jnp.float32)
            out_ref[:, index * tile : (index + 1) * tile] = total.astype(out_ref.dtype)


def pair_sum(terms, ident, dtype):
    terms = terms_of(terms)
    rows = sum(piece.shape[0] for piece in terms[0][0]) // 2
    width = terms[0][1].shape[0 if terms[0][2] is NT else 1]
    tile = min(512, width)
    steps = width // tile
    in_specs, args = term_specs(terms, tile)
    return pl.pallas_call(
        functools.partial(pair_body, [(len(left), dims) for left, _, dims in terms], steps),
        grid=(steps,),
        in_specs=in_specs,
        out_specs=whole((rows, width)),
        out_shape=jax.ShapeDtypeStruct((rows, width), dtype),
        scratch_shapes=[
            pltpu.VMEM((steps, rows, tile), jnp.float32),
            pltpu.VMEM((steps, rows, tile), jnp.bfloat16),
            pltpu.VMEM((steps, rows, tile), jnp.bfloat16),
            pltpu.SemaphoreType.DMA((steps,)),
            pltpu.SemaphoreType.DMA((steps,)),
        ],
        compiler_params=pltpu.CompilerParams(vmem_limit_bytes=60 << 20, collective_id=ident),
        cost_estimate=cost(
            flops=4 * rows * width * sum(left[0].shape[1] for left, _, _ in terms),
            bytes_accessed=sum(2 * a.size for a in args) + 4 * rows * width,
            transcendentals=0,
        ),
        name="pair_sum",
    )(*args)


def partner(axis, bit):
    rank = lax.axis_index(axis)
    return {axis: rank + bit - 2 * bit * (rank // bit % 2)}


def last_body(two, three, *refs):
    mats = len(two) + three
    away, kept, refs = refs[:mats], refs[mats : 2 * mats], refs[2 * mats :]
    gains_ref, outs, sums_ref, refs = refs[0], refs[1 : 1 + mats], refs[1 + mats], refs[2 + mats :]
    own, first, refs = refs[:mats], refs[mats : 2 * mats], refs[2 * mats :]
    held, to_z, from_z, refs = refs[:three], refs[three : 2 * three], refs[2 * three : 3 * three], refs[3 * three :]
    to_last, from_last, refs = refs[:mats], refs[mats : 2 * mats], refs[2 * mats :]
    gain_in, gain_out, load_sem, send_sem, recv_sem = refs
    rank = lax.axis_index("dp")
    z1, z2 = rank // 2 % 2, rank // 4 % 2
    hops = [("tensor", 1), ("tensor", 2), ("dp", 1), ("dp", 2), ("dp", 4)]
    copies = []

    barrier = pltpu.get_barrier_semaphore()
    for axis, bit in hops:
        pl.semaphore_signal(barrier, inc=1, device_id=partner(axis, bit), device_id_type=pl.DeviceIdType.MESH)
    pl.semaphore_wait(barrier, len(hops))

    def send(src, dst, axis, bit):
        index = len(copies)
        copy = pltpu.make_async_remote_copy(
            src_ref=src,
            dst_ref=dst,
            send_sem=send_sem.at[index],
            recv_sem=recv_sem.at[index],
            device_id=partner(axis, bit),
            device_id_type=pl.DeviceIdType.MESH,
        )
        copy.start()
        copies.append(copy)
        return copy

    def side(bit, flip):
        return 1 - bit if flip else bit

    loads = [pltpu.make_async_copy(kept[m], own[m], load_sem.at[m]) for m in range(mats)]
    for load in loads:
        load.start()
    stage = {}
    for m in (2, 1, 0):
        for flip in (1, 0):
            stage[m, flip] = send(away[m].at[side(z2, flip)], first[m].at[flip], "dp", two[m])

    gain_out[0] = gains_ref[...]
    stage["gains"] = send(gain_out.at[0], gain_in.at[0], *hops[0])

    def gain_hop(index):
        stage["gains"].wait_recv()
        total = gain_out[index] + gain_in[index]
        if index + 1 < len(hops):
            gain_out[index + 1] = total
            stage["gains"] = send(gain_out.at[index + 1], gain_in.at[index + 1], *hops[index + 1])
        else:
            sums_ref[...] = total

    gain_hop(0)
    gain_hop(1)
    for m in range(len(two), mats):
        for a in (1, 0):
            for c in (1, 0):
                stage[m, a, c] = send(away[m].at[side(z1, a) + 2 * side(z2, c)], first[m].at[2 * a + c], "dp", 1)
    for load in loads:
        load.wait()

    def wide(value):
        return value.astype(jnp.float32)

    def near_last(m, flip):
        stage[m, flip].wait_recv()
        total = wide(own[m][side(z2, flip)]) + wide(first[m][flip])
        if flip:
            to_last[m][...] = total.astype(jnp.bfloat16)
            stage[m, "last"] = send(to_last[m], from_last[m], "dp", 4)
        else:
            outs[m][...] = total

    def from_x(m, a, c):
        stage[m, a, c].wait_recv()
        total = wide(own[m][side(z1, a) + 2 * side(z2, c)]) + wide(first[m][2 * a + c])
        i = m - len(two)
        if a:
            to_z[i][c] = total.astype(jnp.bfloat16)
            stage[m, "z", c] = send(to_z[i].at[c], from_z[i].at[c], "dp", 2)
        else:
            held[i][c] = total

    def from_near(m, c):
        stage[m, "z", c].wait_recv()
        i = m - len(two)
        total = held[i][c] + wide(from_z[i][c])
        if c:
            to_last[m][...] = total.astype(jnp.bfloat16)
            stage[m, "last"] = send(to_last[m], from_last[m], "dp", 4)
        else:
            outs[m][...] = total

    def finish(m):
        stage[m, "last"].wait_recv()
        outs[m][...] += wide(from_last[m][...])

    gate, up, out, q, k, v = range(6)
    near_last(out, 1)
    near_last(out, 0)
    near_last(gate, 1)
    near_last(up, 1)
    near_last(gate, 0)
    gain_hop(2)
    from_x(q, 1, 1)
    from_x(q, 1, 0)
    near_last(up, 0)
    gain_hop(3)
    from_x(q, 0, 1)
    from_x(q, 0, 0)
    from_near(q, 1)
    from_x(k, 1, 1)
    from_near(q, 0)
    from_x(k, 1, 0)
    from_x(k, 0, 1)
    from_x(k, 0, 0)
    finish(out)
    from_near(k, 1)
    from_x(v, 1, 1)
    from_near(k, 0)
    from_x(v, 1, 0)
    from_x(v, 0, 1)
    from_x(v, 0, 0)
    from_near(v, 1)
    finish(gate)
    from_near(v, 0)
    gain_hop(4)
    for m in (up, q, k, v):
        finish(m)
    for copy in copies:
        copy.wait_send()


def last_stages(two, three, gains):
    mats = [t[:2] for t in two] + list(three)
    away, kept = [m[0] for m in mats], [m[1] for m in mats]
    shapes = [a.shape for a in away]
    low = jnp.bfloat16
    late = shapes[len(two) :]
    any_space = pl.BlockSpec(memory_space=pl.ANY)
    inside = pl.BlockSpec(memory_space=pltpu.VMEM)
    count = 3 * len(two) + 7 * len(three) + 5
    result = pl.pallas_call(
        functools.partial(last_body, [t[2] for t in two], len(three)),
        in_specs=[any_space] * (2 * len(mats)) + [inside],
        out_specs=[inside] * (len(mats) + 1),
        out_shape=[jax.ShapeDtypeStruct(shape[1:], jnp.float32) for shape in shapes]
        + [jax.ShapeDtypeStruct(gains.shape, jnp.float32)],
        scratch_shapes=[pltpu.VMEM(shape, low) for shape in shapes]
        + [pltpu.VMEM(shape, low) for shape in shapes]
        + [pltpu.VMEM((2,) + shape[1:], jnp.float32) for shape in late]
        + [pltpu.VMEM((2,) + shape[1:], low) for shape in late]
        + [pltpu.VMEM((2,) + shape[1:], low) for shape in late]
        + [pltpu.VMEM(shape[1:], low) for shape in shapes]
        + [pltpu.VMEM(shape[1:], low) for shape in shapes]
        + [pltpu.VMEM((5,) + gains.shape, jnp.float32)] * 2
        + [pltpu.SemaphoreType.DMA((len(mats),)), pltpu.SemaphoreType.DMA((count,)), pltpu.SemaphoreType.DMA((count,))],
        compiler_params=pltpu.CompilerParams(vmem_limit_bytes=62 << 20, collective_id=8),
        cost_estimate=cost(flops=1 << 24, bytes_accessed=1 << 25, transcendentals=0),
        name="last_stages",
    )(*away, *kept, gains)
    return result[:-1], result[-1]


def row_tables(length_row, group_row, mask_row):
    starts = jnp.cumsum(length_row) - length_row
    token = jnp.arange(ROWS, dtype=jnp.int32)
    doc_index = jnp.sum((token[:, None] >= starts[None, 1:]).astype(jnp.int32), axis=1)
    onehot = doc_index[:, None] == jnp.arange(DOCS, dtype=jnp.int32)[None, :]
    first = jnp.sum(jnp.where(onehot, starts[None, :], 0), axis=1)
    group_tok = jnp.sum(jnp.where(onehot, group_row[None, :], 0), axis=1)
    real = jnp.sum(jnp.where(onehot, mask_row[:, None], 0), axis=0)
    last_real = first + jnp.sum(jnp.where(onehot, real[None, :], 0), axis=1) - 1
    return (token - first, first, jnp.minimum(token, last_real), group_tok)


def rope_tables(inside):
    freq = rope_base ** (-jnp.arange(0, HEAD_DIM // 2, dtype=jnp.float32) * 2.0 / HEAD_DIM)
    angle = inside.astype(jnp.float32)[:, None] * freq[None, :]
    cosine, sine = jnp.cos(angle), jnp.sin(angle)
    return (
        jnp.concatenate([cosine, cosine], axis=-1),
        jnp.concatenate([-sine, sine], axis=-1),
        jnp.concatenate([sine, -sine], axis=-1),
    )


def rows_dot(left, right):
    return jnp.dot(left, right, preferred_element_type=jnp.float32)


def rows_dot_t(left, right):
    return lax.dot_general(left, right, NT, preferred_element_type=jnp.float32)


def exchange(values, axis, bit):
    size = lax.axis_size(axis)
    return lax.ppermute(values, axis, [(rank, rank ^ bit) for rank in range(size)])


def butterfly_sum(values, axis):
    size = lax.axis_size(axis)
    bit = 1
    while bit < size:
        values = values + exchange(values, axis, bit)
        bit *= 2
    return values


def tie(*values):
    return lax.optimization_barrier(values)


def scatter_small(values, axis):
    size = lax.axis_size(axis)
    rank = lax.axis_index(axis)
    kept = values
    bit = 1
    while bit < size:
        pairs = kept.reshape((kept.shape[0], kept.shape[1] // 2, 2) + kept.shape[2:])
        side = (rank // bit) % 2
        own = lax.dynamic_index_in_dim(pairs, side, axis=2, keepdims=False)
        away = lax.dynamic_index_in_dim(pairs, 1 - side, axis=2, keepdims=False)
        kept = own + exchange(away, axis, bit)
        bit *= 2
    return kept[:, 0]


class WeightGrad:
    def __init__(self, rank, pieces, mats, start=1):
        self.rank, self.pieces, self.mats, self.start = rank, pieces, mats, start
        self.size = lax.axis_size("dp")
        self.tile = pieces[0].shape[1] // self.size
        self.kernel = self.tile % 128 == 0

    def bits(self):
        return [2**i for i in range(self.size.bit_length() - 1)]

    def compute(self, *sides):
        if self.kernel:
            outs = grad_call(self.rank, self.pieces, self.mats, self.start, sides, self.tile)
        else:
            left = jnp.concatenate(self.pieces, axis=0)
            place = jnp.arange(self.size // 2, dtype=jnp.int32)
            bit = self.rank[0] // self.start % 2
            fulls = [
                lax.dot_general(left, jnp.concatenate(mat, axis=0), TN, preferred_element_type=jnp.float32)
                .astype(jnp.bfloat16)
                .reshape(self.size, self.tile, -1)
                for mat in self.mats
            ]
            outs = [
                jnp.take(full, block_at(place, self.start, (bit + side) % 2), axis=0) for side in sides for full in fulls
            ]
        return tuple(outs)


class Halving:
    def __init__(self, rank, own, start=1):
        self.rank, self.kept = rank, own
        self.size = lax.axis_size("dp")
        self.left = [2**i for i in range(self.size.bit_length() - 1) if 2**i != start]

    def merge(self, got, bit):
        low = 2 ** self.left.index(bit)
        self.left.remove(bit)
        if got.shape[1] % 128 == 0:
            away, self.kept = merge_call(self.rank, self.kept, got, low, bit)
            return away
        total = self.kept.astype(jnp.float32) + got.astype(jnp.float32)
        place = jnp.arange(total.shape[0] // 2, dtype=jnp.int32)
        side = self.rank[0] // bit % 2
        self.kept = jnp.take(total, block_at(place, low, side), axis=0)
        return jnp.take(total, block_at(place, low, 1 - side), axis=0).astype(jnp.bfloat16)

    def finish(self, got):
        while self.left:
            bit = self.left[0]
            got = exchange(self.merge(got, bit), "dp", bit)
        return (self.kept.astype(jnp.float32) + got.astype(jnp.float32))[0]


def hop(values, bit):
    return exchange(values, "dp", bit)


def shards(
    hidden_in,
    cotangent,
    gain_attn,
    w_query,
    w_key,
    w_value,
    w_out,
    gain_mlp,
    w_gate,
    w_up,
    w_down,
    doc_lengths,
    doc_groups,
    pad_mask,
):
    rows_local = hidden_in.shape[0]
    rank = lax.axis_index("tensor").astype(jnp.int32)
    rank_ref = rank[None]
    dp_rank = lax.axis_index("dp").astype(jnp.int32)[None]

    def to_far(values):
        return exchange(values, "tensor", 2)

    def to_mate(values):
        return exchange(values, "tensor", 1)

    x_f = hidden_in.astype(jnp.float32)
    inv_a = lax.rsqrt(jnp.mean(x_f * x_f, axis=-1, keepdims=True) + epsilon)
    a0 = (x_f * inv_a * gain_attn).astype(jnp.bfloat16)
    a2 = to_far(a0)
    a1 = to_mate(a0)
    a3 = to_mate(a2)

    inside, low, high, group_tok = row_tables(doc_lengths[0], doc_groups[0], pad_mask[0])
    low, high = low[None], high[None]
    real_tok = pad_mask[0].astype(jnp.float32)
    onehot_g = group_tok[:, None] == jnp.arange(GROUPS, dtype=jnp.int32)[None, :]
    counts = butterfly_sum(jnp.sum(jnp.where(onehot_g, real_tok[:, None], 0.0), axis=0), "dp")
    live = jnp.sum(counts)
    group_scale = jnp.sqrt(live / (GROUPS * jnp.maximum(counts, 1.0)))
    token_weight = real_tok * jnp.sum(jnp.where(onehot_g, group_scale[None, :], 0.0), axis=-1)
    weight_local = lax.dynamic_slice_in_dim(token_weight, rank * rows_local, rows_local)
    c0 = (cotangent.astype(jnp.float32) * weight_local[:, None]).astype(jnp.bfloat16)
    cosine, sine, back_sine = rope_tables(inside)

    near = qkv_pair(0, rank_ref, a0, a1, cosine, sine, w_query, w_key, w_value)
    a2, c0, *near = tie(a2, c0, *near)
    a3 = to_mate(a2)
    c2 = to_far(c0)
    c1 = to_mate(c0)
    far = qkv_pair(2, rank_ref, a2, a3, cosine, sine, w_query, w_key, w_value)
    qs, ks, vs = zip(near, far)
    heads_near, heads_far, lse = attend(rank_ref, qs, ks, vs, low, high)
    y1 = pair_sum([(heads_far, w_out, False)], 0, jnp.bfloat16)
    heads_n, c1, c2, y1 = tie(heads_near, c1, c2, y1)
    got = to_far(y1)
    c3 = to_mate(c2)
    mine = pair_sum([(heads_n, w_out, False)], 1, jnp.float32)
    dm_near = project([((c0, c1), w_down, True)], jnp.float32)
    dm_far = project([((c2, c3), w_down, True)], jnp.float32)
    mid_h = x_f + mine + got.astype(jnp.float32)
    inv_b = lax.rsqrt(jnp.mean(mid_h * mid_h, axis=-1, keepdims=True) + epsilon)
    b0 = (mid_h * inv_b * gain_mlp).astype(jnp.bfloat16)
    b0, dm_near, dm_far = tie(b0, dm_near, dm_far)
    b2 = to_far(b0)
    b1 = to_mate(b0)
    mid_near, dg_near, du_near = mlp_pair(b0, b1, dm_near, w_gate, w_up)
    mine8 = pair_sum([(mid_near, w_down, False)], 5, jnp.float32)
    b2, mid_near, dg_near, du_near, mine8 = tie(b2, mid_near, dg_near, du_near, mine8)
    b3 = to_mate(b2)
    mid_far, dg_far, du_far = mlp_pair(b2, b3, dm_far, w_gate, w_up)

    half = lax.axis_size("dp") // 2
    b_all, c_all = (b0, b1, b2, b3), (c0, c1, c2, c3)
    grad_down = WeightGrad(dp_rank, c_all, [(mid_near, mid_far)])
    grad_gate = WeightGrad(dp_rank, b_all, [(dg_near, dg_far)], 2)
    (down_send,) = grad_down.compute(1)
    dg_f, du_f, down_send = tie(dg_far, du_far, down_send)
    down_got = hop(down_send, 1)
    (gate_send,) = grad_gate.compute(1)
    y5 = pair_sum([(dg_f, w_gate, True), (du_f, w_up, True)], 2, jnp.bfloat16)
    dg_n, du_n, y5 = tie(dg_near, du_near, y5)
    gate_got = hop(gate_send, 2)
    got = to_far(y5)
    d_b = pair_sum([(dg_n, w_gate, True), (du_n, w_up, True)], 3, jnp.float32) + got.astype(jnp.float32)
    (up_send,) = WeightGrad(dp_rank, b_all, [(du_n, du_far)]).compute(1)
    d_b, up_send = tie(d_b, up_send)

    n_b = mid_h * inv_b
    gain_mlp_part = jnp.sum(d_b * n_b, axis=0)
    e_b = d_b * gain_mlp
    weighted = cotangent.astype(jnp.float32) * weight_local[:, None]
    d_h = weighted + inv_b * (e_b - n_b * jnp.mean(e_b * n_b, axis=-1, keepdims=True))
    t0 = d_h.astype(jnp.bfloat16)
    t0, mid_f, dg_n, du_n = tie(t0, mid_far, dg_near, du_near)
    t2 = to_far(t0)
    t1 = to_mate(t0)
    gs_near = project([((t0, t1), w_out, True)])
    y8 = pair_sum([(mid_f, w_down, False)], 4, jnp.bfloat16)
    (down_own,) = WeightGrad(dp_rank, c_all, [(mid_near, mid_f)]).compute(0)
    (gate_own,) = WeightGrad(dp_rank, b_all, [(dg_n, dg_far)], 2).compute(0)
    t2, down_got, gate_got, gs_near, y8, down_own, gate_own = tie(t2, down_got, gate_got, gs_near, y8, down_own, gate_own)

    up_got = hop(up_send, 1)
    got8 = to_far(y8)
    down, gate = Halving(dp_rank, down_own), Halving(dp_rank, gate_own, 2)
    down_got = hop(down.merge(down_got, 2), 2)
    t3 = to_mate(t2)
    gs_far = project([((t2, t3), w_out, True)])
    gate_away = gate.merge(gate_got, 1)
    out_send, out_own = WeightGrad(dp_rank, (t0, t1, t2, t3), [(heads_near, heads_far)]).compute(1, 0)
    dqn, dqf, dkn, dkf, dvn, dvf = attend_back(
        rank_ref, qs, ks, vs, (gs_near, gs_far), low, high, lse, cosine, back_sine
    )
    dqf, dkf, dvf, down_got, got8, out_send, gate_away = tie(dqf, dkf, dvf, down_got, got8, out_send, gate_away)

    out_got = hop(out_send, 1)
    y7 = pair_sum([(dqf, w_query, True), (dkf, w_key, True), (dvf, w_value, True)], 6, jnp.bfloat16)
    dqn, dkn, dvn, dun, y7 = tie(dqn, dkn, dvn, du_near, y7)
    got = to_far(y7)
    grad_qkv = WeightGrad(dp_rank, (a0, a1, a2, a3), [(dqn, dqf), (dkn, dkf), (dvn, dvf)])
    *sends, q_own, k_own, v_own = grad_qkv.compute(1, 0)
    down_got = hop(down.merge(down_got, half), half)
    d_a = pair_sum([(dqn, w_query, True), (dkn, w_key, True), (dvn, w_value, True)], 7, jnp.float32) + got.astype(jnp.float32)
    (up_own,) = WeightGrad(dp_rank, b_all, [(dun, du_far)]).compute(0)
    d_a, up_own, up_got, out_got, gate_away, down_got, *sends = tie(
        d_a, up_own, up_got, out_got, gate_away, down_got, *sends
    )

    up, out = Halving(dp_rank, up_own), Halving(dp_rank, out_own)
    up_away, out_away = up.merge(up_got, 2), out.merge(out_got, 2)
    output = (mid_h + mine8 + got8.astype(jnp.float32)).astype(jnp.bfloat16)
    n_a = x_f * inv_a
    gain_attn_part = jnp.sum(d_a * n_a, axis=0)
    e_a = d_a * gain_attn
    grad_input = d_h + inv_a * (e_a - n_a * jnp.mean(e_a * n_a, axis=-1, keepdims=True))
    gains = jnp.stack([gain_attn_part, gain_mlp_part])
    sum_down = down.finish(down_got)
    if grad_qkv.kernel and half == 4:
        (sum_gate, sum_up, sum_out, *sums), gains = last_stages(
            [(gate_away, gate.kept, 1), (up_away, up.kept, 2), (out_away, out.kept, 2)],
            list(zip(sends, (q_own, k_own, v_own))),
            gains,
        )
        gains = lax.dynamic_slice_in_dim(gains, dp_rank[0] * grad_qkv.tile, grad_qkv.tile, 1)
    else:
        gains = butterfly_sum(scatter_small(gains.reshape(2, lax.axis_size("dp"), -1), "dp"), "tensor")
        sum_gate = gate.finish(hop(gate_away, 1))
        sum_up = up.finish(hop(up_away, 2))
        sum_out = out.finish(hop(out_away, 2))
        sums = [Halving(dp_rank, own).finish(hop(send, 1)) for send, own in zip(sends, (q_own, k_own, v_own))]
    return (
        output,
        grad_input,
        gains[0],
        sums[0],
        sums[1],
        sums[2],
        sum_out.T,
        gains[1],
        sum_gate,
        sum_up,
        sum_down.T,
    )


def solution(mesh):
    rows, columns, split = P(("dp", "tensor"), None), P(None, "tensor"), P("tensor", None)
    in_specs = (
        rows,
        rows,
        P(),
        columns,
        columns,
        columns,
        split,
        P(),
        columns,
        columns,
        split,
        P("dp", None),
        P("dp", None),
        P("dp", None),
    )
    grads = P("dp", "tensor")
    grads_t = P("tensor", "dp")
    out_specs = (rows, rows, P("dp"), grads, grads, grads, grads_t, P("dp"), grads, grads, grads_t)
    return jax.shard_map(shards, mesh=mesh, in_specs=in_specs, out_specs=out_specs, check_vma=False)
```

```python
import functools

import jax
import jax.numpy as jnp
from jax import lax
from jax.experimental import pallas as pl
from jax.experimental.pallas import tpu as pltpu
from jax.sharding import PartitionSpec as P

HEAD_DIM = 128
ROWS = 1280
DOCS = 3
GROUPS = 8
QTILE = 256

epsilon = 1e-05
masked_score = -1e30
rope_base = 10000.0
COST = 1000


def cost(flops, bytes_accessed, transcendentals):
    return pl.CostEstimate(
        flops=flops // COST, bytes_accessed=bytes_accessed // COST, transcendentals=transcendentals // COST
    )


NT = (((1,), (1,)), ((), ()))
TN = (((0,), (0,)), ((), ()))
NN = (((1,), (0,)), ((), ()))


def mm(left, right, dims=NN):
    return lax.dot_general(left, right, dims, preferred_element_type=jnp.float32)


def whole(shape):
    return pl.BlockSpec(shape, lambda *_: (0,) * len(shape))


def turn(values, cosine, sine):
    return values * cosine + pltpu.roll(values, HEAD_DIM // 2, 1) * sine


def qkv_body(first, rank_ref, xa_ref, xb_ref, cos_ref, sin_ref, wq_ref, wk_ref, wv_ref, q_ref, k_ref, v_ref):
    rows = xa_ref.shape[0]
    for half, x_ref in enumerate((xa_ref, xb_ref)):
        span = pl.ds(half * rows, rows)
        x = x_ref[...]
        place = pl.ds(pl.multiple_of((rank_ref[0] ^ (first + half)) * rows, rows), rows)
        cosine, sine = cos_ref[place, :], sin_ref[place, :]
        for w_ref, out_ref in ((wq_ref, q_ref), (wk_ref, k_ref)):
            full = mm(x, w_ref[...])
            for head in range(full.shape[1] // HEAD_DIM):
                lanes = slice(head * HEAD_DIM, (head + 1) * HEAD_DIM)
                out_ref[span, lanes] = turn(full[:, lanes], cosine, sine).astype(jnp.bfloat16)
        v_ref[span, :] = mm(x, wv_ref[...]).astype(jnp.bfloat16)


def qkv_pair(first, rank, xa, xb, cosine, sine, wq, wk, wv):
    rows, depth = xa.shape
    width = wq.shape[1]
    tile = 256
    wspec = pl.BlockSpec((depth, tile), lambda j, *_: (0, j))
    ospec = pl.BlockSpec((2 * rows, tile), lambda j, *_: (0, j))
    out = jax.ShapeDtypeStruct((2 * rows, width), jnp.bfloat16)
    return pl.pallas_call(
        functools.partial(qkv_body, first),
        grid_spec=pltpu.PrefetchScalarGridSpec(
            num_scalar_prefetch=1,
            grid=(width // tile,),
            in_specs=[whole(xa.shape)] * 2 + [whole(cosine.shape)] * 2 + [wspec] * 3,
            out_specs=[ospec] * 3,
        ),
        out_shape=[out] * 3,
        compiler_params=pltpu.CompilerParams(vmem_limit_bytes=60 << 20),
        cost_estimate=cost(
            flops=12 * rows * depth * width, bytes_accessed=6 * depth * width + 4 * rows * depth, transcendentals=0
        ),
        name="qkv",
    )(rank, xa, xb, cosine, sine, wq, wk, wv)


def in_order(rank_ref, near_ref, far_ref, out_ref):
    piece = near_ref.shape[0] // 2
    for index in range(4):
        src = (near_ref, far_ref)[index // 2]
        at = pl.multiple_of((rank_ref[0] ^ index) * piece, piece)
        out_ref[pl.ds(at, piece), :] = src[pl.ds((index % 2) * piece, piece), :]


def out_of_order(rank_ref, src_ref, near_ref, far_ref):
    piece = near_ref.shape[0] // 2
    for index in range(4):
        dst = (near_ref, far_ref)[index // 2]
        at = pl.multiple_of((rank_ref[0] ^ index) * piece, piece)
        dst[pl.ds((index % 2) * piece, piece), :] = src_ref[pl.ds(at, piece), :].astype(dst.dtype)


def attend_body(rank_ref, qn, qf, kn, kf, vn, vf, low_ref, high_ref, on, of, lse_ref, q_s, k_s, v_s, o_s):
    in_order(rank_ref, qn, qf, q_s)
    in_order(rank_ref, kn, kf, k_s)
    in_order(rank_ref, vn, vf, v_s)
    scale = HEAD_DIM ** (-0.5)
    v_t = v_s[...].T
    for block in range(q_s.shape[0] // QTILE):
        span = pl.ds(block * QTILE, QTILE)
        end = (block + 1) * QTILE
        scores = mm(k_s[:end, :], q_s[span, :], NT)
        at = lax.broadcasted_iota(jnp.int32, scores.shape, 0)
        allowed = (at >= low_ref[:, span]) & (at <= high_ref[:, span])
        scores = jnp.where(allowed, scores * scale, masked_score)
        top = jnp.max(scores, axis=0, keepdims=True)
        prob = jnp.exp(scores - top)
        total = jnp.sum(prob, axis=0, keepdims=True)
        lse_ref[0, :, span] = top + jnp.log(total)
        out_t = mm(v_t[:, :end], prob.astype(jnp.bfloat16)) * (1.0 / total)
        o_s[span, :] = out_t.T
    out_of_order(rank_ref, o_s, on, of)


def attend(rank, qs, ks, vs, low, high):
    half, width = qs[0].shape
    rows = 2 * half
    heads = width // HEAD_DIM
    hspec = pl.BlockSpec((half, HEAD_DIM), lambda h, *_: (0, h))
    row = whole((1, rows))
    return pl.pallas_call(
        attend_body,
        grid_spec=pltpu.PrefetchScalarGridSpec(
            num_scalar_prefetch=1,
            grid=(heads,),
            in_specs=[hspec] * 6 + [row] * 2,
            out_specs=[hspec] * 2 + [pl.BlockSpec((1, 1, rows), lambda h, *_: (h, 0, 0))],
            scratch_shapes=[pltpu.VMEM((rows, HEAD_DIM), jnp.bfloat16)] * 3 + [pltpu.VMEM((rows, HEAD_DIM), jnp.float32)],
        ),
        out_shape=[jax.ShapeDtypeStruct((half, width), jnp.bfloat16)] * 2
        + [jax.ShapeDtypeStruct((heads, 1, rows), jnp.float32)],
        compiler_params=pltpu.CompilerParams(vmem_limit_bytes=60 << 20),
        cost_estimate=cost(
            flops=8 * rows * rows * width, bytes_accessed=8 * rows * width, transcendentals=heads * rows * rows // 2
        ),
        name="attend",
    )(rank, *qs, *ks, *vs, low, high)


def attend_back_body(
    rank_ref, qn, qf, kn, kf, vn, vf, gn, gf, low_ref, high_ref, lse_ref, cos_ref, sin_ref,
    dqn, dqf, dkn, dkf, dvn, dvf, q_s, k_s, v_s, g_s, dq_s, dk_s, dv_s,
):
    in_order(rank_ref, qn, qf, q_s)
    in_order(rank_ref, kn, kf, k_s)
    in_order(rank_ref, vn, vf, v_s)
    in_order(rank_ref, gn, gf, g_s)
    scale = HEAD_DIM ** (-0.5)
    k_t = k_s[...].T
    blocks = q_s.shape[0] // QTILE
    for block in reversed(range(blocks)):
        span = pl.ds(block * QTILE, QTILE)
        end = (block + 1) * QTILE
        query, grad = q_s[span, :], g_s[span, :]
        scores = mm(k_s[:end, :], query, NT) * scale
        at = lax.broadcasted_iota(jnp.int32, scores.shape, 0)
        allowed = (at >= low_ref[:, span]) & (at <= high_ref[:, span])
        prob = jnp.exp(jnp.where(allowed, scores, masked_score) - lse_ref[0, :, span])
        d_prob = mm(v_s[:end, :], grad, NT)
        dot = jnp.sum(prob * d_prob, axis=0, keepdims=True)
        d_score = (prob * (d_prob - dot) * scale).astype(jnp.bfloat16)
        dq_s[span, :] = mm(k_t[:, :end], d_score).T
        d_key = mm(d_score, query)
        d_value = mm(prob.astype(jnp.bfloat16), grad)
        if block == blocks - 1:
            dk_s[...] = d_key
            dv_s[...] = d_value
        else:
            dk_s[:end, :] += d_key
            dv_s[:end, :] += d_value
    dq_s[...] = turn(dq_s[...], cos_ref[...], sin_ref[...])
    dk_s[...] = turn(dk_s[...], cos_ref[...], sin_ref[...])
    out_of_order(rank_ref, dq_s, dqn, dqf)
    out_of_order(rank_ref, dk_s, dkn, dkf)
    out_of_order(rank_ref, dv_s, dvn, dvf)


def attend_back(rank, qs, ks, vs, gs, low, high, lse, cosine, back_sine):
    half, width = qs[0].shape
    rows = 2 * half
    heads = width // HEAD_DIM
    hspec = pl.BlockSpec((half, HEAD_DIM), lambda h, *_: (0, h))
    row = whole((1, rows))
    return pl.pallas_call(
        attend_back_body,
        grid_spec=pltpu.PrefetchScalarGridSpec(
            num_scalar_prefetch=1,
            grid=(heads,),
            in_specs=[hspec] * 8
            + [row] * 2
            + [pl.BlockSpec((1, 1, rows), lambda h, *_: (h, 0, 0))]
            + [whole((rows, HEAD_DIM))] * 2,
            out_specs=[hspec] * 6,
            scratch_shapes=[pltpu.VMEM((rows, HEAD_DIM), jnp.bfloat16)] * 4
            + [pltpu.VMEM((rows, HEAD_DIM), jnp.float32)] * 3,
        ),
        out_shape=[jax.ShapeDtypeStruct((half, width), jnp.bfloat16)] * 6,
        compiler_params=pltpu.CompilerParams(vmem_limit_bytes=60 << 20),
        cost_estimate=cost(
            flops=20 * rows * rows * width, bytes_accessed=16 * rows * width, transcendentals=heads * rows * rows // 2
        ),
        name="attend_back",
    )(rank, *qs, *ks, *vs, *gs, low, high, lse, cosine, back_sine)


def mlp_body(xa_ref, xb_ref, dm_ref, wg_ref, wu_ref, mid_ref, dg_ref, du_ref):
    rows = xa_ref.shape[0]
    for half, x_ref in enumerate((xa_ref, xb_ref)):
        span = pl.ds(half * rows, rows)
        x = x_ref[...]
        gate = mm(x, wg_ref[...])
        up = mm(x, wu_ref[...])
        d_mid = dm_ref[span, :]
        sigma = 1.0 / (1.0 + jnp.exp(-gate))
        active = gate * sigma
        mid_ref[span, :] = (active * up).astype(jnp.bfloat16)
        dg_ref[span, :] = (d_mid * up * sigma * (1.0 + gate * (1.0 - sigma))).astype(jnp.bfloat16)
        du_ref[span, :] = (d_mid * active).astype(jnp.bfloat16)


def mlp_pair(xa, xb, d_mid, wg, wu):
    rows, depth = xa.shape
    width = wg.shape[1]
    tile = 256
    wspec = pl.BlockSpec((depth, tile), lambda j: (0, j))
    ospec = pl.BlockSpec((2 * rows, tile), lambda j: (0, j))
    return pl.pallas_call(
        mlp_body,
        grid=(pl.cdiv(width, tile),),
        in_specs=[whole(xa.shape)] * 2 + [ospec] + [wspec] * 2,
        out_specs=[ospec] * 3,
        out_shape=[jax.ShapeDtypeStruct((2 * rows, width), jnp.bfloat16)] * 3,
        compiler_params=pltpu.CompilerParams(vmem_limit_bytes=60 << 20),
        cost_estimate=cost(
            flops=8 * rows * depth * width,
            bytes_accessed=4 * depth * width + 4 * rows * depth + 20 * rows * width,
            transcendentals=2 * rows * width,
        ),
        name="mlp",
    )(xa, xb, d_mid, wg, wu)


def gather_rows(parts, out_ref):
    at = 0
    for part in parts:
        out_ref[at : at + part.shape[0], :] = part[...]
        at += part.shape[0]


def gather_sides(rights, out_ref):
    at = 0
    for near, far in zip(rights[::2], rights[1::2]):
        rows, width = near.shape
        out_ref[:rows, at : at + width] = near[...]
        out_ref[rows:, at : at + width] = far[...]
        at += width


def block_at(place, low, side):
    return place // low * (2 * low) + place % low + low * side


def filled(step, low, side):
    group, half = step // (2 * low), step // low % 2
    here = jnp.where(half == side, step % low, jnp.where(half > side, low - 1, -1))
    return jnp.maximum(group * low + here, 0)


def grad_body(pieces, widths, low, sides, rank_ref, *refs):
    left, rights = refs[:pieces], refs[pieces : pieces + 2 * len(widths)]
    outs, (left_s, right_s) = refs[pieces + 2 * len(widths) : -2], refs[-2:]
    step = pl.program_id(0)

    @pl.when(step == 0)
    def _():
        gather_sides(rights, right_s)

    gather_rows(left, left_s)
    total = mm(left_s[...], right_s[...], TN).astype(jnp.bfloat16)

    def store(refs):
        at = 0
        for ref, width in zip(refs, widths):
            ref[0] = total[:, at : at + width]
            at += width

    if len(sides) == 1:
        store(outs)
    else:
        sent = step // low % 2 != rank_ref[0] // low % 2
        pl.when(sent)(lambda: store(outs[: len(widths)]))
        pl.when(jnp.logical_not(sent))(lambda: store(outs[len(widths) :]))


def grad_call(rank, pieces, mats, low, sides, tile):
    rows, depth = pieces[0].shape[0] * len(pieces), pieces[0].shape[1]
    widths = [near.shape[1] for near, _ in mats]
    width, half = sum(widths), depth // tile // 2
    count = half * len(sides)

    def own(s, side):
        bit = s[0] // low % 2
        return 1 - bit if side else bit

    if len(sides) == 1:
        lspec = pl.BlockSpec((pieces[0].shape[0], tile), lambda j, s: (0, block_at(j, low, own(s, sides[0]))))
    else:
        lspec = pl.BlockSpec((pieces[0].shape[0], tile), lambda j, s: (0, j))
    out_specs = []
    for side in sides:
        for w in widths:
            if len(sides) == 1:
                out_specs.append(pl.BlockSpec((1, tile, w), lambda j, s: (j, 0, 0)))
            else:
                out_specs.append(pl.BlockSpec((1, tile, w), lambda j, s, side=side: (filled(j, low, own(s, side)), 0, 0)))
    rights = [part for mat in mats for part in mat]
    return pl.pallas_call(
        functools.partial(grad_body, len(pieces), widths, low, sides),
        grid_spec=pltpu.PrefetchScalarGridSpec(
            num_scalar_prefetch=1,
            grid=(count,),
            in_specs=[lspec] * len(pieces) + [whole(r.shape) for r in rights],
            out_specs=out_specs,
            scratch_shapes=[pltpu.VMEM((rows, tile), jnp.bfloat16), pltpu.VMEM((rows, width), jnp.bfloat16)],
        ),
        out_shape=[jax.ShapeDtypeStruct((half, tile, w), jnp.bfloat16) for _ in sides for w in widths],
        compiler_params=pltpu.CompilerParams(vmem_limit_bytes=60 << 20),
        cost_estimate=cost(
            flops=2 * rows * tile * count * width,
            bytes_accessed=2 * rows * (tile * count + width) + 2 * tile * count * width,
            transcendentals=0,
        ),
        name="weight_grad",
    )(rank, *pieces, *rights)


def merge_body(_, own_away, got_away, own_kept, got_kept, away_ref, kept_ref):
    away_ref[...] = (own_away[...].astype(jnp.float32) + got_away[...].astype(jnp.float32)).astype(jnp.bfloat16)
    kept_ref[...] = (own_kept[...].astype(jnp.float32) + got_kept[...].astype(jnp.float32)).astype(jnp.bfloat16)


def merge_call(rank, own, got, low, bit):
    count, tile, width = own.shape
    away, kept = (
        pl.BlockSpec((1, tile, width), lambda j, s, flip=flip: (block_at(j, low, (s[0] // bit + flip) % 2), 0, 0))
        for flip in (1, 0)
    )
    ospec = pl.BlockSpec((1, tile, width), lambda j, s: (j, 0, 0))
    return pl.pallas_call(
        merge_body,
        grid_spec=pltpu.PrefetchScalarGridSpec(
            num_scalar_prefetch=1,
            grid=(count // 2,),
            in_specs=[away, away, kept, kept],
            out_specs=[ospec] * 2,
        ),
        out_shape=[jax.ShapeDtypeStruct((count // 2, tile, width), jnp.bfloat16)] * 2,
        compiler_params=pltpu.CompilerParams(vmem_limit_bytes=40 << 20),
        cost_estimate=cost(flops=count * tile * width, bytes_accessed=6 * count * tile * width, transcendentals=0),
        name="merge",
    )(rank, own, got, own, got)


def product(lefts, weights, half, rows):
    total = None
    for left, (w_ref, dims) in zip(lefts, weights):
        value = mm(left[half][...] if len(left) == 2 else left[0][pl.ds(half * rows, rows), :], w_ref[...], dims)
        total = value if total is None else total + value
    return total


def project_body(terms, *refs):
    at, lefts, weights = 0, [], []
    for pieces, dims in terms:
        lefts.append(refs[at : at + pieces])
        weights.append((refs[at + pieces], dims))
        at += pieces + 1
    out_ref = refs[at]
    rows = out_ref.shape[0] // 2
    for half in range(2):
        span = pl.ds(half * rows, rows)
        out_ref[span, :] = product(lefts, weights, half, rows).astype(out_ref.dtype)


def terms_of(terms):
    return [(left if isinstance(left, tuple) else (left,), w, NT if flip else NN) for left, w, flip in terms]


def term_specs(terms, tile):
    in_specs, args = [], []
    for left, w, dims in terms:
        depth = left[0].shape[1]
        in_specs += [whole(piece.shape) for piece in left]
        in_specs.append(
            pl.BlockSpec((tile, depth), lambda j: (j, 0)) if dims is NT else pl.BlockSpec((depth, tile), lambda j: (0, j))
        )
        args += [*left, w]
    return in_specs, args


def project(terms, dtype=jnp.bfloat16):
    terms = terms_of(terms)
    rows = sum(piece.shape[0] for piece in terms[0][0])
    width = terms[0][1].shape[0 if terms[0][2] is NT else 1]
    tile = min(512, width)
    in_specs, args = term_specs(terms, tile)
    return pl.pallas_call(
        functools.partial(project_body, [(len(left), dims) for left, _, dims in terms]),
        grid=(pl.cdiv(width, tile),),
        in_specs=in_specs,
        out_specs=pl.BlockSpec((rows, tile), lambda j: (0, j)),
        out_shape=jax.ShapeDtypeStruct((rows, width), dtype),
        compiler_params=pltpu.CompilerParams(vmem_limit_bytes=60 << 20),
        cost_estimate=cost(
            flops=2 * rows * width * sum(left[0].shape[1] for left, _, _ in terms),
            bytes_accessed=sum(2 * a.size for a in args) + 2 * rows * width,
            transcendentals=0,
        ),
        name="project",
    )(*args)


def pair_body(terms, steps, *refs):
    at, lefts, weights = 0, [], []
    for pieces, dims in terms:
        lefts.append(refs[at : at + pieces])
        weights.append((refs[at + pieces], dims))
        at += pieces + 1
    out_ref, mine_s, away_s, got_s, send_sem, recv_sem = refs[at:]
    rows = out_ref.shape[0]
    tile = mine_s.shape[2]
    step = pl.program_id(0)
    me = lax.axis_index("tensor")
    mate = {"tensor": me + 1 - 2 * (me % 2)}

    @pl.when(step == 0)
    def _():
        barrier = pltpu.get_barrier_semaphore()
        pl.semaphore_signal(barrier, inc=1, device_id=mate, device_id_type=pl.DeviceIdType.MESH)
        pl.semaphore_wait(barrier, 1)

    def copy(index):
        return pltpu.make_async_remote_copy(
            src_ref=away_s.at[index],
            dst_ref=got_s.at[index],
            send_sem=send_sem.at[index],
            recv_sem=recv_sem.at[index],
            device_id=mate,
            device_id_type=pl.DeviceIdType.MESH,
        )

    away_s[step] = product(lefts, weights, 1, rows).astype(jnp.bfloat16)
    copy(step).start()
    mine_s[step] = product(lefts, weights, 0, rows)

    @pl.when(step == steps - 1)
    def _():
        for index in range(steps):
            copy(index).wait()
            total = mine_s[index] + got_s[index].astype(jnp.float32)
            out_ref[:, index * tile : (index + 1) * tile] = total.astype(out_ref.dtype)


def pair_sum(terms, ident, dtype):
    terms = terms_of(terms)
    rows = sum(piece.shape[0] for piece in terms[0][0]) // 2
    width = terms[0][1].shape[0 if terms[0][2] is NT else 1]
    tile = min(512, width)
    steps = width // tile
    in_specs, args = term_specs(terms, tile)
    return pl.pallas_call(
        functools.partial(pair_body, [(len(left), dims) for left, _, dims in terms], steps),
        grid=(steps,),
        in_specs=in_specs,
        out_specs=whole((rows, width)),
        out_shape=jax.ShapeDtypeStruct((rows, width), dtype),
        scratch_shapes=[
            pltpu.VMEM((steps, rows, tile), jnp.float32),
            pltpu.VMEM((steps, rows, tile), jnp.bfloat16),
            pltpu.VMEM((steps, rows, tile), jnp.bfloat16),
            pltpu.SemaphoreType.DMA((steps,)),
            pltpu.SemaphoreType.DMA((steps,)),
        ],
        compiler_params=pltpu.CompilerParams(vmem_limit_bytes=60 << 20, collective_id=ident),
        cost_estimate=cost(
            flops=4 * rows * width * sum(left[0].shape[1] for left, _, _ in terms),
            bytes_accessed=sum(2 * a.size for a in args) + 4 * rows * width,
            transcendentals=0,
        ),
        name="pair_sum",
    )(*args)


def partner(axis, bit):
    rank = lax.axis_index(axis)
    return {axis: rank + bit - 2 * bit * (rank // bit % 2)}


def last_body(ones, twos, threes, *refs):
    mats = ones + twos + threes
    away, kept, refs = refs[:mats], refs[mats : 2 * mats], refs[2 * mats :]
    ready_ref, got_ref, gains_ref, refs = refs[0], refs[1], refs[2], refs[3:]
    outs, done_ref, sums_ref, refs = refs[:mats], refs[mats], refs[mats + 1], refs[mats + 2 :]
    own, first, refs = refs[:mats], refs[mats : 2 * mats], refs[2 * mats :]
    held, to_z, from_z, refs = refs[:threes], refs[threes : 2 * threes], refs[2 * threes : 3 * threes], refs[3 * threes :]
    late = twos + threes
    to_last, from_last, total_s, refs = refs[:late], refs[late : 2 * late], refs[2 * late : 2 * late + twos], refs[2 * late + twos :]
    gain_in, gain_out, load_sem, send_sem, recv_sem = refs
    rank = lax.axis_index("dp")
    z1, z2 = rank // 2 % 2, rank // 4 % 2
    hops = [("tensor", 1), ("tensor", 2), ("dp", 1), ("dp", 2), ("dp", 4)]
    copies = []

    barrier = pltpu.get_barrier_semaphore()
    for axis, bit in hops:
        pl.semaphore_signal(barrier, inc=1, device_id=partner(axis, bit), device_id_type=pl.DeviceIdType.MESH)
    pl.semaphore_wait(barrier, len(hops))

    def send(src, dst, axis, bit):
        index = len(copies)
        copy = pltpu.make_async_remote_copy(
            src_ref=src,
            dst_ref=dst,
            send_sem=send_sem.at[index],
            recv_sem=recv_sem.at[index],
            device_id=partner(axis, bit),
            device_id_type=pl.DeviceIdType.MESH,
        )
        copy.start()
        copies.append(copy)
        return copy

    def side(bit, flip):
        return 1 - bit if flip else bit

    stage = {}
    gain_out[0] = gains_ref[...]
    stage["gains"] = send(gain_out.at[0], gain_in.at[0], *hops[0])

    def gain_hop(index):
        stage["gains"].wait_recv()
        total = gain_out[index] + gain_in[index]
        if index + 1 < len(hops):
            gain_out[index + 1] = total
            stage["gains"] = send(gain_out.at[index + 1], gain_in.at[index + 1], *hops[index + 1])
        else:
            sums_ref[...] = total

    for m in range(ones, ones + twos):
        for c in (1, 0):
            stage[m, "z", c] = send(away[m].at[side(z2, c)], first[m].at[c], "dp", 2)
    for m in range(ones):
        stage[m, "last"] = send(away[m], first[m], "dp", 4)

    def send_all(m):
        for a in (1, 0):
            for c in (1, 0):
                stage[m, a, c] = send(away[m].at[side(z1, a) + 2 * side(z2, c)], first[m].at[2 * a + c], "dp", 1)

    loads = [pltpu.make_async_copy(kept[m], own[m], load_sem.at[m]) for m in range(mats)]
    for load in loads:
        load.start()
    send_all(ones + twos)
    gain_hop(0)
    gain_hop(1)
    for m in range(ones + twos + 1, mats):
        send_all(m)
    for load in loads:
        load.wait()

    def wide(value):
        return value.astype(jnp.float32)

    def from_x(m, a, c):
        stage[m, a, c].wait_recv()
        total = wide(own[m][side(z1, a) + 2 * side(z2, c)]) + wide(first[m][2 * a + c])
        i = m - ones - twos
        if a:
            to_z[i][c] = total.astype(jnp.bfloat16)
            stage[m, "z", c] = send(to_z[i].at[c], from_z[i].at[c], "dp", 2)
        else:
            held[i][c] = total

    def from_near(m, c):
        stage[m, "z", c].wait_recv()
        if m < ones + twos:
            total = wide(own[m][side(z2, c)]) + wide(first[m][c])
            dst = total_s[m - ones]
        else:
            total = held[m - ones - twos][c] + wide(from_z[m - ones - twos][c])
            dst = outs[m]
        if c:
            to_last[m - ones][...] = total.astype(jnp.bfloat16)
            stage[m, "last"] = send(to_last[m - ones], from_last[m - ones], "dp", 4)
        else:
            dst[...] = total

    def finish(m):
        stage[m, "last"].wait_recv()
        if m < ones:
            outs[m][...] = wide(own[m][0]) + wide(first[m][0])
        elif m < ones + twos:
            outs[m][...] = (total_s[m - ones][...] + wide(from_last[m - ones][...])).T
        else:
            outs[m][...] += wide(from_last[m - ones][...])

    gate, up, out, q, k, v = range(6)
    from_near(out, 1)
    from_x(q, 1, 1)
    from_x(q, 1, 0)
    from_near(out, 0)
    from_x(q, 0, 1)
    from_x(q, 0, 0)
    done_ref[...] = (wide(ready_ref[0]) + wide(got_ref[0])).T
    from_x(k, 1, 1)
    from_near(q, 1)
    from_x(k, 1, 0)
    from_near(q, 0)
    from_x(k, 0, 1)
    finish(gate)
    from_x(k, 0, 0)
    gain_hop(2)
    from_x(v, 1, 1)
    from_near(k, 1)
    from_x(v, 1, 0)
    from_near(k, 0)
    gain_hop(3)
    finish(up)
    from_x(v, 0, 1)
    from_x(v, 0, 0)
    finish(out)
    from_near(v, 1)
    from_near(v, 0)
    gain_hop(4)
    for m in (q, k, v):
        finish(m)
    for copy in copies:
        copy.wait_send()


def last_stages(ones, twos, threes, ready, gains):
    mats = [*ones, *twos, *threes]
    away, kept = [m[0] for m in mats], [m[1] for m in mats]
    shapes = [a.shape for a in away]
    low, wide = jnp.bfloat16, jnp.float32
    late, last = shapes[len(ones) + len(twos) :], shapes[len(ones) :]
    flat = [shape[1:] for shape in shapes]
    for m in range(len(ones), len(ones) + len(twos)):
        flat[m] = flat[m][::-1]
    any_space = pl.BlockSpec(memory_space=pl.ANY)
    inside = pl.BlockSpec(memory_space=pltpu.VMEM)
    count = len(ones) + 3 * len(twos) + 7 * len(threes) + 5
    result = pl.pallas_call(
        functools.partial(last_body, len(ones), len(twos), len(threes)),
        in_specs=[any_space] * (2 * len(mats)) + [inside] * 3,
        out_specs=[inside] * (len(mats) + 2),
        out_shape=[jax.ShapeDtypeStruct(shape, wide) for shape in flat]
        + [jax.ShapeDtypeStruct(ready[0].shape[:0:-1], wide), jax.ShapeDtypeStruct(gains.shape, wide)],
        scratch_shapes=[pltpu.VMEM(shape, low) for shape in shapes]
        + [pltpu.VMEM(shape, low) for shape in shapes]
        + [pltpu.VMEM((2,) + shape[1:], wide) for shape in late]
        + [pltpu.VMEM((2,) + shape[1:], low) for shape in late]
        + [pltpu.VMEM((2,) + shape[1:], low) for shape in late]
        + [pltpu.VMEM(shape[1:], low) for shape in last]
        + [pltpu.VMEM(shape[1:], low) for shape in last]
        + [pltpu.VMEM(shape[1:], wide) for shape in last[: len(twos)]]
        + [pltpu.VMEM((5,) + gains.shape, wide)] * 2
        + [pltpu.SemaphoreType.DMA((len(mats),)), pltpu.SemaphoreType.DMA((count,)), pltpu.SemaphoreType.DMA((count,))],
        compiler_params=pltpu.CompilerParams(vmem_limit_bytes=62 << 20, collective_id=8),
        cost_estimate=cost(flops=1 << 24, bytes_accessed=1 << 25, transcendentals=0),
        name="last_stages",
    )(*away, *kept, *ready, gains)
    return result[:-2], result[-2], result[-1]


def row_tables(length_row, group_row, mask_row):
    starts = jnp.cumsum(length_row) - length_row
    token = jnp.arange(ROWS, dtype=jnp.int32)
    doc_index = jnp.sum((token[:, None] >= starts[None, 1:]).astype(jnp.int32), axis=1)
    onehot = doc_index[:, None] == jnp.arange(DOCS, dtype=jnp.int32)[None, :]
    first = jnp.sum(jnp.where(onehot, starts[None, :], 0), axis=1)
    group_tok = jnp.sum(jnp.where(onehot, group_row[None, :], 0), axis=1)
    real = jnp.sum(jnp.where(onehot, mask_row[:, None], 0), axis=0)
    last_real = first + jnp.sum(jnp.where(onehot, real[None, :], 0), axis=1) - 1
    return (token - first, first, jnp.minimum(token, last_real), group_tok)


def rope_tables(inside):
    freq = rope_base ** (-jnp.arange(0, HEAD_DIM // 2, dtype=jnp.float32) * 2.0 / HEAD_DIM)
    angle = inside.astype(jnp.float32)[:, None] * freq[None, :]
    cosine, sine = jnp.cos(angle), jnp.sin(angle)
    return (
        jnp.concatenate([cosine, cosine], axis=-1),
        jnp.concatenate([-sine, sine], axis=-1),
        jnp.concatenate([sine, -sine], axis=-1),
    )


def rows_dot(left, right):
    return jnp.dot(left, right, preferred_element_type=jnp.float32)


def rows_dot_t(left, right):
    return lax.dot_general(left, right, NT, preferred_element_type=jnp.float32)


def exchange(values, axis, bit):
    size = lax.axis_size(axis)
    return lax.ppermute(values, axis, [(rank, rank ^ bit) for rank in range(size)])


def butterfly_sum(values, axis):
    size = lax.axis_size(axis)
    bit = 1
    while bit < size:
        values = values + exchange(values, axis, bit)
        bit *= 2
    return values


def tie(*values):
    return lax.optimization_barrier(values)


def scatter_small(values, axis):
    size = lax.axis_size(axis)
    rank = lax.axis_index(axis)
    kept = values
    bit = 1
    while bit < size:
        pairs = kept.reshape((kept.shape[0], kept.shape[1] // 2, 2) + kept.shape[2:])
        side = (rank // bit) % 2
        own = lax.dynamic_index_in_dim(pairs, side, axis=2, keepdims=False)
        away = lax.dynamic_index_in_dim(pairs, 1 - side, axis=2, keepdims=False)
        kept = own + exchange(away, axis, bit)
        bit *= 2
    return kept[:, 0]


class WeightGrad:
    def __init__(self, rank, pieces, mats, start=1):
        self.rank, self.pieces, self.mats, self.start = rank, pieces, mats, start
        self.size = lax.axis_size("dp")
        self.tile = pieces[0].shape[1] // self.size
        self.kernel = self.tile % 128 == 0

    def bits(self):
        return [2**i for i in range(self.size.bit_length() - 1)]

    def compute(self, *sides):
        if self.kernel:
            outs = grad_call(self.rank, self.pieces, self.mats, self.start, sides, self.tile)
        else:
            left = jnp.concatenate(self.pieces, axis=0)
            place = jnp.arange(self.size // 2, dtype=jnp.int32)
            bit = self.rank[0] // self.start % 2
            fulls = [
                lax.dot_general(left, jnp.concatenate(mat, axis=0), TN, preferred_element_type=jnp.float32)
                .astype(jnp.bfloat16)
                .reshape(self.size, self.tile, -1)
                for mat in self.mats
            ]
            outs = [
                jnp.take(full, block_at(place, self.start, (bit + side) % 2), axis=0) for side in sides for full in fulls
            ]
        return tuple(outs)


class Halving:
    def __init__(self, rank, own, start=1):
        self.rank, self.kept = rank, own
        self.size = lax.axis_size("dp")
        self.left = [2**i for i in range(self.size.bit_length() - 1) if 2**i != start]

    def merge(self, got, bit):
        low = 2 ** self.left.index(bit)
        self.left.remove(bit)
        if got.shape[1] % 128 == 0:
            away, self.kept = merge_call(self.rank, self.kept, got, low, bit)
            return away
        total = self.kept.astype(jnp.float32) + got.astype(jnp.float32)
        place = jnp.arange(total.shape[0] // 2, dtype=jnp.int32)
        side = self.rank[0] // bit % 2
        self.kept = jnp.take(total, block_at(place, low, side), axis=0)
        return jnp.take(total, block_at(place, low, 1 - side), axis=0).astype(jnp.bfloat16)

    def finish(self, got):
        while self.left:
            bit = self.left[0]
            got = exchange(self.merge(got, bit), "dp", bit)
        return (self.kept.astype(jnp.float32) + got.astype(jnp.float32))[0]


def hop(values, bit):
    return exchange(values, "dp", bit)


def shards(
    hidden_in,
    cotangent,
    gain_attn,
    w_query,
    w_key,
    w_value,
    w_out,
    gain_mlp,
    w_gate,
    w_up,
    w_down,
    doc_lengths,
    doc_groups,
    pad_mask,
):
    rows_local = hidden_in.shape[0]
    rank = lax.axis_index("tensor").astype(jnp.int32)
    rank_ref = rank[None]
    dp_rank = lax.axis_index("dp").astype(jnp.int32)[None]

    def to_far(values):
        return exchange(values, "tensor", 2)

    def to_mate(values):
        return exchange(values, "tensor", 1)

    x_f = hidden_in.astype(jnp.float32)
    inv_a = lax.rsqrt(jnp.mean(x_f * x_f, axis=-1, keepdims=True) + epsilon)
    a0 = (x_f * inv_a * gain_attn).astype(jnp.bfloat16)
    a2 = to_far(a0)
    a1 = to_mate(a0)
    a3 = to_mate(a2)

    inside, low, high, group_tok = row_tables(doc_lengths[0], doc_groups[0], pad_mask[0])
    low, high = low[None], high[None]
    real_tok = pad_mask[0].astype(jnp.float32)
    onehot_g = group_tok[:, None] == jnp.arange(GROUPS, dtype=jnp.int32)[None, :]
    counts = butterfly_sum(jnp.sum(jnp.where(onehot_g, real_tok[:, None], 0.0), axis=0), "dp")
    live = jnp.sum(counts)
    group_scale = jnp.sqrt(live / (GROUPS * jnp.maximum(counts, 1.0)))
    token_weight = real_tok * jnp.sum(jnp.where(onehot_g, group_scale[None, :], 0.0), axis=-1)
    weight_local = lax.dynamic_slice_in_dim(token_weight, rank * rows_local, rows_local)
    c0 = (cotangent.astype(jnp.float32) * weight_local[:, None]).astype(jnp.bfloat16)
    cosine, sine, back_sine = rope_tables(inside)

    near = qkv_pair(0, rank_ref, a0, a1, cosine, sine, w_query, w_key, w_value)
    a2, c0, *near = tie(a2, c0, *near)
    a3 = to_mate(a2)
    c2 = to_far(c0)
    c1 = to_mate(c0)
    far = qkv_pair(2, rank_ref, a2, a3, cosine, sine, w_query, w_key, w_value)
    qs, ks, vs = zip(near, far)
    heads_near, heads_far, lse = attend(rank_ref, qs, ks, vs, low, high)
    y1 = pair_sum([(heads_far, w_out, False)], 0, jnp.bfloat16)
    heads_n, c1, c2, y1 = tie(heads_near, c1, c2, y1)
    got = to_far(y1)
    c3 = to_mate(c2)
    mine = pair_sum([(heads_n, w_out, False)], 1, jnp.float32)
    dm_near = project([((c0, c1), w_down, True)], jnp.float32)
    dm_far = project([((c2, c3), w_down, True)], jnp.float32)
    got, dm_near, dm_far, mine = tie(got, dm_near, dm_far, mine)
    mid_h = x_f + mine + got.astype(jnp.float32)
    inv_b = lax.rsqrt(jnp.mean(mid_h * mid_h, axis=-1, keepdims=True) + epsilon)
    b0 = (mid_h * inv_b * gain_mlp).astype(jnp.bfloat16)
    b2 = to_far(b0)
    b1 = to_mate(b0)
    mid_near, dg_near, du_near = mlp_pair(b0, b1, dm_near, w_gate, w_up)
    mine8 = pair_sum([(mid_near, w_down, False)], 5, jnp.float32)
    b2, mid_near, dg_near, du_near, mine8 = tie(b2, mid_near, dg_near, du_near, mine8)
    b3 = to_mate(b2)
    mid_far, dg_far, du_far = mlp_pair(b2, b3, dm_far, w_gate, w_up)

    half = lax.axis_size("dp") // 2
    b_all, c_all = (b0, b1, b2, b3), (c0, c1, c2, c3)
    grad_down = WeightGrad(dp_rank, c_all, [(mid_near, mid_far)])
    grad_gate = WeightGrad(dp_rank, b_all, [(dg_near, dg_far)], 2)
    (down_send,) = grad_down.compute(1)
    dg_f, du_f, down_send = tie(dg_far, du_far, down_send)
    down_got = hop(down_send, 1)
    (gate_send,) = grad_gate.compute(1)
    y5 = pair_sum([(dg_f, w_gate, True), (du_f, w_up, True)], 2, jnp.bfloat16)
    dg_n, du_n, mid_n, y5 = tie(dg_near, du_near, mid_near, y5)
    gate_got = hop(gate_send, 2)
    got = to_far(y5)
    d_b = pair_sum([(dg_n, w_gate, True), (du_n, w_up, True)], 3, jnp.float32) + got.astype(jnp.float32)
    (up_send,) = WeightGrad(dp_rank, b_all, [(du_n, du_far)]).compute(1)
    (down_own,) = WeightGrad(dp_rank, c_all, [(mid_n, mid_far)]).compute(0)
    d_b, up_send, down_got, down_own = tie(d_b, up_send, down_got, down_own)
    up_got = hop(up_send, 1)
    down = Halving(dp_rank, down_own)
    down_got = hop(down.merge(down_got, 2), 2)

    n_b = mid_h * inv_b
    gain_mlp_part = jnp.sum(d_b * n_b, axis=0)
    e_b = d_b * gain_mlp
    weighted = cotangent.astype(jnp.float32) * weight_local[:, None]
    d_h = weighted + inv_b * (e_b - n_b * jnp.mean(e_b * n_b, axis=-1, keepdims=True))
    t0 = d_h.astype(jnp.bfloat16)
    t0, mid_f, dg_n, du_n = tie(t0, mid_far, dg_near, du_near)
    t2 = to_far(t0)
    t1 = to_mate(t0)
    gs_near = project([((t0, t1), w_out, True)])
    y8 = pair_sum([(mid_f, w_down, False)], 4, jnp.bfloat16)
    (gate_own,) = WeightGrad(dp_rank, b_all, [(dg_n, dg_far)], 2).compute(0)
    t2, gate_got, gs_near, y8, gate_own = tie(t2, gate_got, gs_near, y8, gate_own)

    got8 = to_far(y8)
    gate = Halving(dp_rank, gate_own, 2)
    t3 = to_mate(t2)
    gs_far = project([((t2, t3), w_out, True)])
    gate_away = gate.merge(gate_got, 1)
    (up_own,) = WeightGrad(dp_rank, b_all, [(du_n, du_far)]).compute(0)
    out_send, out_own = WeightGrad(dp_rank, (t0, t1, t2, t3), [(heads_near, heads_far)]).compute(1, 0)
    dqn, dqf, dkn, dkf, dvn, dvf = attend_back(
        rank_ref, qs, ks, vs, (gs_near, gs_far), low, high, lse, cosine, back_sine
    )
    dqf, dkf, dvf, down_got, got8, out_send, gate_away, up_got, up_own = tie(
        dqf, dkf, dvf, down_got, got8, out_send, gate_away, up_got, up_own
    )

    out_got, gate_got = hop(out_send, 1), hop(gate_away, 1)
    up = Halving(dp_rank, up_own)
    up_got = hop(up.merge(up_got, 2), 2)
    y7 = pair_sum([(dqf, w_query, True), (dkf, w_key, True), (dvf, w_value, True)], 6, jnp.bfloat16)
    dqn, dkn, dvn, y7 = tie(dqn, dkn, dvn, y7)
    got = to_far(y7)
    grad_qkv = WeightGrad(dp_rank, (a0, a1, a2, a3), [(dqn, dqf), (dkn, dkf), (dvn, dvf)])
    *sends, q_own, k_own, v_own = grad_qkv.compute(1, 0)
    down_got = hop(down.merge(down_got, half), half)
    d_a = pair_sum([(dqn, w_query, True), (dkn, w_key, True), (dvn, w_value, True)], 7, jnp.float32) + got.astype(jnp.float32)
    d_a, up_got, out_got, gate_got, down_got, *sends = tie(d_a, up_got, out_got, gate_got, down_got, *sends)

    out = Halving(dp_rank, out_own)
    out_away = out.merge(out_got, 2)
    gate_away, up_away = gate.merge(gate_got, half), up.merge(up_got, half)
    output = (mid_h + mine8 + got8.astype(jnp.float32)).astype(jnp.bfloat16)
    n_a = x_f * inv_a
    gain_attn_part = jnp.sum(d_a * n_a, axis=0)
    e_a = d_a * gain_attn
    grad_input = d_h + inv_a * (e_a - n_a * jnp.mean(e_a * n_a, axis=-1, keepdims=True))
    gains = jnp.stack([gain_attn_part, gain_mlp_part])
    if grad_qkv.kernel and half == 4:
        (sum_gate, sum_up, sum_out, *sums), sum_down, gains = last_stages(
            [(gate_away, gate.kept), (up_away, up.kept)],
            [(out_away, out.kept)],
            list(zip(sends, (q_own, k_own, v_own))),
            (down.kept, down_got),
            gains,
        )
        gains = lax.dynamic_slice_in_dim(gains, dp_rank[0] * grad_qkv.tile, grad_qkv.tile, 1)
    else:
        gains = butterfly_sum(scatter_small(gains.reshape(2, lax.axis_size("dp"), -1), "dp"), "tensor")
        sum_gate = gate.finish(hop(gate_away, half))
        sum_up = up.finish(hop(up_away, half))
        sum_out = out.finish(hop(out_away, 2)).T
        sum_down = down.finish(down_got).T
        sums = [Halving(dp_rank, own).finish(hop(send, 1)) for send, own in zip(sends, (q_own, k_own, v_own))]
    return (
        output,
        grad_input,
        gains[0],
        sums[0],
        sums[1],
        sums[2],
        sum_out,
        gains[1],
        sum_gate,
        sum_up,
        sum_down,
    )


def solution(mesh):
    rows, columns, split = P(("dp", "tensor"), None), P(None, "tensor"), P("tensor", None)
    in_specs = (
        rows,
        rows,
        P(),
        columns,
        columns,
        columns,
        split,
        P(),
        columns,
        columns,
        split,
        P("dp", None),
        P("dp", None),
        P("dp", None),
    )
    grads = P("dp", "tensor")
    grads_t = P("tensor", "dp")
    out_specs = (rows, rows, P("dp"), grads, grads, grads, grads_t, P("dp"), grads, grads, grads_t)
    return jax.shard_map(shards, mesh=mesh, in_specs=in_specs, out_specs=out_specs, check_vma=False)
```

```python
import functools

import jax
import jax.numpy as jnp
from jax import lax
from jax.experimental import pallas as pl
from jax.experimental.pallas import tpu as pltpu
from jax.sharding import PartitionSpec as P

HEAD_DIM = 128
ROWS = 1280
DOCS = 3
GROUPS = 8
QTILE = 256

epsilon = 1e-05
masked_score = -1e30
rope_base = 10000.0
COST = 1000


def cost(flops, bytes_accessed, transcendentals):
    return pl.CostEstimate(
        flops=flops // COST, bytes_accessed=bytes_accessed // COST, transcendentals=transcendentals // COST
    )


NT = (((1,), (1,)), ((), ()))
TN = (((0,), (0,)), ((), ()))
NN = (((1,), (0,)), ((), ()))


def mm(left, right, dims=NN):
    return lax.dot_general(left, right, dims, preferred_element_type=jnp.float32)


def whole(shape):
    return pl.BlockSpec(shape, lambda *_: (0,) * len(shape))


def turn(values, cosine, sine):
    return values * cosine + pltpu.roll(values, HEAD_DIM // 2, 1) * sine


def qkv_body(first, rank_ref, xa_ref, xb_ref, cos_ref, sin_ref, wq_ref, wk_ref, wv_ref, q_ref, k_ref, v_ref):
    rows = xa_ref.shape[0]
    for half, x_ref in enumerate((xa_ref, xb_ref)):
        span = pl.ds(half * rows, rows)
        x = x_ref[...]
        place = pl.ds(pl.multiple_of((rank_ref[0] ^ (first + half)) * rows, rows), rows)
        cosine, sine = cos_ref[place, :], sin_ref[place, :]
        for w_ref, out_ref in ((wq_ref, q_ref), (wk_ref, k_ref)):
            full = mm(x, w_ref[...])
            for head in range(full.shape[1] // HEAD_DIM):
                lanes = slice(head * HEAD_DIM, (head + 1) * HEAD_DIM)
                out_ref[span, lanes] = turn(full[:, lanes], cosine, sine).astype(jnp.bfloat16)
        v_ref[span, :] = mm(x, wv_ref[...]).astype(jnp.bfloat16)


def qkv_pair(first, rank, xa, xb, cosine, sine, wq, wk, wv):
    rows, depth = xa.shape
    width = wq.shape[1]
    tile = 256
    wspec = pl.BlockSpec((depth, tile), lambda j, *_: (0, j))
    ospec = pl.BlockSpec((2 * rows, tile), lambda j, *_: (0, j))
    out = jax.ShapeDtypeStruct((2 * rows, width), jnp.bfloat16)
    return pl.pallas_call(
        functools.partial(qkv_body, first),
        grid_spec=pltpu.PrefetchScalarGridSpec(
            num_scalar_prefetch=1,
            grid=(width // tile,),
            in_specs=[whole(xa.shape)] * 2 + [whole(cosine.shape)] * 2 + [wspec] * 3,
            out_specs=[ospec] * 3,
        ),
        out_shape=[out] * 3,
        compiler_params=pltpu.CompilerParams(vmem_limit_bytes=60 << 20),
        cost_estimate=cost(
            flops=12 * rows * depth * width, bytes_accessed=6 * depth * width + 4 * rows * depth, transcendentals=0
        ),
        name="qkv",
    )(rank, xa, xb, cosine, sine, wq, wk, wv)


def in_order(rank_ref, near_ref, far_ref, out_ref):
    piece = near_ref.shape[0] // 2
    for index in range(4):
        src = (near_ref, far_ref)[index // 2]
        at = pl.multiple_of((rank_ref[0] ^ index) * piece, piece)
        out_ref[pl.ds(at, piece), :] = src[pl.ds((index % 2) * piece, piece), :]


def out_of_order(rank_ref, src_ref, near_ref, far_ref):
    piece = near_ref.shape[0] // 2
    for index in range(4):
        dst = (near_ref, far_ref)[index // 2]
        at = pl.multiple_of((rank_ref[0] ^ index) * piece, piece)
        dst[pl.ds((index % 2) * piece, piece), :] = src_ref[pl.ds(at, piece), :].astype(dst.dtype)


def attend_body(rank_ref, qn, qf, kn, kf, vn, vf, low_ref, high_ref, on, of, lse_ref, q_s, k_s, v_s, o_s):
    in_order(rank_ref, qn, qf, q_s)
    in_order(rank_ref, kn, kf, k_s)
    in_order(rank_ref, vn, vf, v_s)
    scale = HEAD_DIM ** (-0.5)
    v_t = v_s[...].T
    for block in range(q_s.shape[0] // QTILE):
        span = pl.ds(block * QTILE, QTILE)
        end = (block + 1) * QTILE
        scores = mm(k_s[:end, :], q_s[span, :], NT)
        at = lax.broadcasted_iota(jnp.int32, scores.shape, 0)
        allowed = (at >= low_ref[:, span]) & (at <= high_ref[:, span])
        scores = jnp.where(allowed, scores * scale, masked_score)
        top = jnp.max(scores, axis=0, keepdims=True)
        prob = jnp.exp(scores - top)
        total = jnp.sum(prob, axis=0, keepdims=True)
        lse_ref[0, :, span] = top + jnp.log(total)
        out_t = mm(v_t[:, :end], prob.astype(jnp.bfloat16)) * (1.0 / total)
        o_s[span, :] = out_t.T
    out_of_order(rank_ref, o_s, on, of)


def attend(rank, qs, ks, vs, low, high):
    half, width = qs[0].shape
    rows = 2 * half
    heads = width // HEAD_DIM
    hspec = pl.BlockSpec((half, HEAD_DIM), lambda h, *_: (0, h))
    row = whole((1, rows))
    return pl.pallas_call(
        attend_body,
        grid_spec=pltpu.PrefetchScalarGridSpec(
            num_scalar_prefetch=1,
            grid=(heads,),
            in_specs=[hspec] * 6 + [row] * 2,
            out_specs=[hspec] * 2 + [pl.BlockSpec((1, 1, rows), lambda h, *_: (h, 0, 0))],
            scratch_shapes=[pltpu.VMEM((rows, HEAD_DIM), jnp.bfloat16)] * 3 + [pltpu.VMEM((rows, HEAD_DIM), jnp.float32)],
        ),
        out_shape=[jax.ShapeDtypeStruct((half, width), jnp.bfloat16)] * 2
        + [jax.ShapeDtypeStruct((heads, 1, rows), jnp.float32)],
        compiler_params=pltpu.CompilerParams(vmem_limit_bytes=60 << 20),
        cost_estimate=cost(
            flops=8 * rows * rows * width, bytes_accessed=8 * rows * width, transcendentals=heads * rows * rows // 2
        ),
        name="attend",
    )(rank, *qs, *ks, *vs, low, high)


def attend_back_body(
    rank_ref, qn, qf, kn, kf, vn, vf, gn, gf, low_ref, high_ref, lse_ref, cos_ref, sin_ref,
    dqn, dqf, dkn, dkf, dvn, dvf, q_s, k_s, v_s, g_s, dq_s, dk_s, dv_s,
):
    in_order(rank_ref, qn, qf, q_s)
    in_order(rank_ref, kn, kf, k_s)
    in_order(rank_ref, vn, vf, v_s)
    in_order(rank_ref, gn, gf, g_s)
    scale = HEAD_DIM ** (-0.5)
    k_t = k_s[...].T
    blocks = q_s.shape[0] // QTILE
    for block in reversed(range(blocks)):
        span = pl.ds(block * QTILE, QTILE)
        end = (block + 1) * QTILE
        query, grad = q_s[span, :], g_s[span, :]
        scores = mm(k_s[:end, :], query, NT) * scale
        at = lax.broadcasted_iota(jnp.int32, scores.shape, 0)
        allowed = (at >= low_ref[:, span]) & (at <= high_ref[:, span])
        prob = jnp.exp(jnp.where(allowed, scores, masked_score) - lse_ref[0, :, span])
        d_prob = mm(v_s[:end, :], grad, NT)
        dot = jnp.sum(prob * d_prob, axis=0, keepdims=True)
        d_score = (prob * (d_prob - dot) * scale).astype(jnp.bfloat16)
        dq_s[span, :] = mm(k_t[:, :end], d_score).T
        d_key = mm(d_score, query)
        d_value = mm(prob.astype(jnp.bfloat16), grad)
        if block == blocks - 1:
            dk_s[...] = d_key
            dv_s[...] = d_value
        else:
            dk_s[:end, :] += d_key
            dv_s[:end, :] += d_value
    dq_s[...] = turn(dq_s[...], cos_ref[...], sin_ref[...])
    dk_s[...] = turn(dk_s[...], cos_ref[...], sin_ref[...])
    out_of_order(rank_ref, dq_s, dqn, dqf)
    out_of_order(rank_ref, dk_s, dkn, dkf)
    out_of_order(rank_ref, dv_s, dvn, dvf)


def attend_back(rank, qs, ks, vs, gs, low, high, lse, cosine, back_sine):
    half, width = qs[0].shape
    rows = 2 * half
    heads = width // HEAD_DIM
    hspec = pl.BlockSpec((half, HEAD_DIM), lambda h, *_: (0, h))
    row = whole((1, rows))
    return pl.pallas_call(
        attend_back_body,
        grid_spec=pltpu.PrefetchScalarGridSpec(
            num_scalar_prefetch=1,
            grid=(heads,),
            in_specs=[hspec] * 8
            + [row] * 2
            + [pl.BlockSpec((1, 1, rows), lambda h, *_: (h, 0, 0))]
            + [whole((rows, HEAD_DIM))] * 2,
            out_specs=[hspec] * 6,
            scratch_shapes=[pltpu.VMEM((rows, HEAD_DIM), jnp.bfloat16)] * 4
            + [pltpu.VMEM((rows, HEAD_DIM), jnp.float32)] * 3,
        ),
        out_shape=[jax.ShapeDtypeStruct((half, width), jnp.bfloat16)] * 6,
        compiler_params=pltpu.CompilerParams(vmem_limit_bytes=60 << 20),
        cost_estimate=cost(
            flops=20 * rows * rows * width, bytes_accessed=16 * rows * width, transcendentals=heads * rows * rows // 2
        ),
        name="attend_back",
    )(rank, *qs, *ks, *vs, *gs, low, high, lse, cosine, back_sine)


def mlp_body(xa_ref, xb_ref, dm_ref, wg_ref, wu_ref, mid_ref, dg_ref, du_ref):
    rows = xa_ref.shape[0]
    for half, x_ref in enumerate((xa_ref, xb_ref)):
        span = pl.ds(half * rows, rows)
        x = x_ref[...]
        gate = mm(x, wg_ref[...])
        up = mm(x, wu_ref[...])
        d_mid = dm_ref[span, :]
        sigma = 1.0 / (1.0 + jnp.exp(-gate))
        active = gate * sigma
        mid_ref[span, :] = (active * up).astype(jnp.bfloat16)
        dg_ref[span, :] = (d_mid * up * sigma * (1.0 + gate * (1.0 - sigma))).astype(jnp.bfloat16)
        du_ref[span, :] = (d_mid * active).astype(jnp.bfloat16)


def mlp_pair(xa, xb, d_mid, wg, wu):
    rows, depth = xa.shape
    width = wg.shape[1]
    tile = 256
    wspec = pl.BlockSpec((depth, tile), lambda j: (0, j))
    ospec = pl.BlockSpec((2 * rows, tile), lambda j: (0, j))
    return pl.pallas_call(
        mlp_body,
        grid=(pl.cdiv(width, tile),),
        in_specs=[whole(xa.shape)] * 2 + [ospec] + [wspec] * 2,
        out_specs=[ospec] * 3,
        out_shape=[jax.ShapeDtypeStruct((2 * rows, width), jnp.bfloat16)] * 3,
        compiler_params=pltpu.CompilerParams(vmem_limit_bytes=60 << 20),
        cost_estimate=cost(
            flops=8 * rows * depth * width,
            bytes_accessed=4 * depth * width + 4 * rows * depth + 20 * rows * width,
            transcendentals=2 * rows * width,
        ),
        name="mlp",
    )(xa, xb, d_mid, wg, wu)


def gather_rows(parts, out_ref):
    at = 0
    for part in parts:
        out_ref[at : at + part.shape[0], :] = part[...]
        at += part.shape[0]


def gather_sides(rights, out_ref):
    at = 0
    for near, far in zip(rights[::2], rights[1::2]):
        rows, width = near.shape
        out_ref[:rows, at : at + width] = near[...]
        out_ref[rows:, at : at + width] = far[...]
        at += width


def block_at(place, low, side):
    return place // low * (2 * low) + place % low + low * side


def filled(step, low, side):
    group, half = step // (2 * low), step // low % 2
    here = jnp.where(half == side, step % low, jnp.where(half > side, low - 1, -1))
    return jnp.maximum(group * low + here, 0)


def grad_body(pieces, widths, low, sides, rank_ref, *refs):
    left, rights = refs[:pieces], refs[pieces : pieces + 2 * len(widths)]
    outs, (left_s, right_s) = refs[pieces + 2 * len(widths) : -2], refs[-2:]
    step = pl.program_id(0)

    @pl.when(step == 0)
    def _():
        gather_sides(rights, right_s)

    gather_rows(left, left_s)
    total = mm(left_s[...], right_s[...], TN).astype(jnp.bfloat16)

    def store(refs):
        at = 0
        for ref, width in zip(refs, widths):
            ref[0] = total[:, at : at + width]
            at += width

    if len(sides) == 1:
        store(outs)
    else:
        sent = step // low % 2 != rank_ref[0] // low % 2
        pl.when(sent)(lambda: store(outs[: len(widths)]))
        pl.when(jnp.logical_not(sent))(lambda: store(outs[len(widths) :]))


def grad_call(rank, pieces, mats, low, sides, tile):
    rows, depth = pieces[0].shape[0] * len(pieces), pieces[0].shape[1]
    widths = [near.shape[1] for near, _ in mats]
    width, half = sum(widths), depth // tile // 2
    count = half * len(sides)

    def own(s, side):
        bit = s[0] // low % 2
        return 1 - bit if side else bit

    if len(sides) == 1:
        lspec = pl.BlockSpec((pieces[0].shape[0], tile), lambda j, s: (0, block_at(j, low, own(s, sides[0]))))
    else:
        lspec = pl.BlockSpec((pieces[0].shape[0], tile), lambda j, s: (0, j))
    out_specs = []
    for side in sides:
        for w in widths:
            if len(sides) == 1:
                out_specs.append(pl.BlockSpec((1, tile, w), lambda j, s: (j, 0, 0)))
            else:
                out_specs.append(pl.BlockSpec((1, tile, w), lambda j, s, side=side: (filled(j, low, own(s, side)), 0, 0)))
    rights = [part for mat in mats for part in mat]
    return pl.pallas_call(
        functools.partial(grad_body, len(pieces), widths, low, sides),
        grid_spec=pltpu.PrefetchScalarGridSpec(
            num_scalar_prefetch=1,
            grid=(count,),
            in_specs=[lspec] * len(pieces) + [whole(r.shape) for r in rights],
            out_specs=out_specs,
            scratch_shapes=[pltpu.VMEM((rows, tile), jnp.bfloat16), pltpu.VMEM((rows, width), jnp.bfloat16)],
        ),
        out_shape=[jax.ShapeDtypeStruct((half, tile, w), jnp.bfloat16) for _ in sides for w in widths],
        compiler_params=pltpu.CompilerParams(vmem_limit_bytes=60 << 20),
        cost_estimate=cost(
            flops=2 * rows * tile * count * width,
            bytes_accessed=2 * rows * (tile * count + width) + 2 * tile * count * width,
            transcendentals=0,
        ),
        name="weight_grad",
    )(rank, *pieces, *rights)


def merge_body(_, own_away, got_away, own_kept, got_kept, away_ref, kept_ref):
    away_ref[...] = (own_away[...].astype(jnp.float32) + got_away[...].astype(jnp.float32)).astype(jnp.bfloat16)
    kept_ref[...] = (own_kept[...].astype(jnp.float32) + got_kept[...].astype(jnp.float32)).astype(jnp.bfloat16)


def merge_call(rank, own, got, low, bit):
    count, tile, width = own.shape
    away, kept = (
        pl.BlockSpec((1, tile, width), lambda j, s, flip=flip: (block_at(j, low, (s[0] // bit + flip) % 2), 0, 0))
        for flip in (1, 0)
    )
    ospec = pl.BlockSpec((1, tile, width), lambda j, s: (j, 0, 0))
    return pl.pallas_call(
        merge_body,
        grid_spec=pltpu.PrefetchScalarGridSpec(
            num_scalar_prefetch=1,
            grid=(count // 2,),
            in_specs=[away, away, kept, kept],
            out_specs=[ospec] * 2,
        ),
        out_shape=[jax.ShapeDtypeStruct((count // 2, tile, width), jnp.bfloat16)] * 2,
        compiler_params=pltpu.CompilerParams(vmem_limit_bytes=40 << 20),
        cost_estimate=cost(flops=count * tile * width, bytes_accessed=6 * count * tile * width, transcendentals=0),
        name="merge",
    )(rank, own, got, own, got)


def product(lefts, weights, half, rows):
    total = None
    for left, (w_ref, dims) in zip(lefts, weights):
        value = mm(left[half][...] if len(left) == 2 else left[0][pl.ds(half * rows, rows), :], w_ref[...], dims)
        total = value if total is None else total + value
    return total


def project_body(terms, *refs):
    at, lefts, weights = 0, [], []
    for pieces, dims in terms:
        lefts.append(refs[at : at + pieces])
        weights.append((refs[at + pieces], dims))
        at += pieces + 1
    out_ref = refs[at]
    rows = out_ref.shape[0] // 2
    for half in range(2):
        span = pl.ds(half * rows, rows)
        out_ref[span, :] = product(lefts, weights, half, rows).astype(out_ref.dtype)


def terms_of(terms):
    return [(left if isinstance(left, tuple) else (left,), w, NT if flip else NN) for left, w, flip in terms]


def term_specs(terms, tile):
    in_specs, args = [], []
    for left, w, dims in terms:
        depth = left[0].shape[1]
        in_specs += [whole(piece.shape) for piece in left]
        in_specs.append(
            pl.BlockSpec((tile, depth), lambda j: (j, 0)) if dims is NT else pl.BlockSpec((depth, tile), lambda j: (0, j))
        )
        args += [*left, w]
    return in_specs, args


def project(terms, dtype=jnp.bfloat16):
    terms = terms_of(terms)
    rows = sum(piece.shape[0] for piece in terms[0][0])
    width = terms[0][1].shape[0 if terms[0][2] is NT else 1]
    tile = min(512, width)
    in_specs, args = term_specs(terms, tile)
    return pl.pallas_call(
        functools.partial(project_body, [(len(left), dims) for left, _, dims in terms]),
        grid=(pl.cdiv(width, tile),),
        in_specs=in_specs,
        out_specs=pl.BlockSpec((rows, tile), lambda j: (0, j)),
        out_shape=jax.ShapeDtypeStruct((rows, width), dtype),
        compiler_params=pltpu.CompilerParams(vmem_limit_bytes=60 << 20),
        cost_estimate=cost(
            flops=2 * rows * width * sum(left[0].shape[1] for left, _, _ in terms),
            bytes_accessed=sum(2 * a.size for a in args) + 2 * rows * width,
            transcendentals=0,
        ),
        name="project",
    )(*args)


def pair_body(terms, steps, *refs):
    at, lefts, weights = 0, [], []
    for pieces, dims in terms:
        lefts.append(refs[at : at + pieces])
        weights.append((refs[at + pieces], dims))
        at += pieces + 1
    out_ref, mine_s, away_s, got_s, send_sem, recv_sem = refs[at:]
    rows = out_ref.shape[0]
    tile = mine_s.shape[2]
    step = pl.program_id(0)
    me = lax.axis_index("tensor")
    mate = {"tensor": me + 1 - 2 * (me % 2)}

    @pl.when(step == 0)
    def _():
        barrier = pltpu.get_barrier_semaphore()
        pl.semaphore_signal(barrier, inc=1, device_id=mate, device_id_type=pl.DeviceIdType.MESH)
        pl.semaphore_wait(barrier, 1)

    def copy(index):
        return pltpu.make_async_remote_copy(
            src_ref=away_s.at[index],
            dst_ref=got_s.at[index],
            send_sem=send_sem.at[index],
            recv_sem=recv_sem.at[index],
            device_id=mate,
            device_id_type=pl.DeviceIdType.MESH,
        )

    away_s[step] = product(lefts, weights, 1, rows).astype(jnp.bfloat16)
    copy(step).start()
    mine_s[step] = product(lefts, weights, 0, rows)

    @pl.when(step == steps - 1)
    def _():
        for index in range(steps):
            copy(index).wait()
            total = mine_s[index] + got_s[index].astype(jnp.float32)
            out_ref[:, index * tile : (index + 1) * tile] = total.astype(out_ref.dtype)


def pair_sum(terms, ident, dtype):
    terms = terms_of(terms)
    rows = sum(piece.shape[0] for piece in terms[0][0]) // 2
    width = terms[0][1].shape[0 if terms[0][2] is NT else 1]
    tile = min(512, width)
    steps = width // tile
    in_specs, args = term_specs(terms, tile)
    return pl.pallas_call(
        functools.partial(pair_body, [(len(left), dims) for left, _, dims in terms], steps),
        grid=(steps,),
        in_specs=in_specs,
        out_specs=whole((rows, width)),
        out_shape=jax.ShapeDtypeStruct((rows, width), dtype),
        scratch_shapes=[
            pltpu.VMEM((steps, rows, tile), jnp.float32),
            pltpu.VMEM((steps, rows, tile), jnp.bfloat16),
            pltpu.VMEM((steps, rows, tile), jnp.bfloat16),
            pltpu.SemaphoreType.DMA((steps,)),
            pltpu.SemaphoreType.DMA((steps,)),
        ],
        compiler_params=pltpu.CompilerParams(vmem_limit_bytes=60 << 20, collective_id=ident),
        cost_estimate=cost(
            flops=4 * rows * width * sum(left[0].shape[1] for left, _, _ in terms),
            bytes_accessed=sum(2 * a.size for a in args) + 4 * rows * width,
            transcendentals=0,
        ),
        name="pair_sum",
    )(*args)


def partner(axis, bit):
    rank = lax.axis_index(axis)
    return {axis: rank + bit - 2 * bit * (rank // bit % 2)}


def last_body(ones, twos, threes, *refs):
    mats = ones + twos + threes
    away, kept, refs = refs[:mats], refs[mats : 2 * mats], refs[2 * mats :]
    ready_ref, got_ref, gains_ref, refs = refs[0], refs[1], refs[2], refs[3:]
    outs, done_ref, sums_ref, refs = refs[:mats], refs[mats], refs[mats + 1], refs[mats + 2 :]
    own, first, refs = refs[:mats], refs[mats : 2 * mats], refs[2 * mats :]
    held, to_z, from_z, refs = refs[:threes], refs[threes : 2 * threes], refs[2 * threes : 3 * threes], refs[3 * threes :]
    late = twos + threes
    to_last, from_last, total_s, refs = refs[:late], refs[late : 2 * late], refs[2 * late : 2 * late + twos], refs[2 * late + twos :]
    gain_in, gain_out, load_sem, send_sem, recv_sem = refs
    rank = lax.axis_index("dp")
    z1, z2 = rank // 2 % 2, rank // 4 % 2
    hops = [("tensor", 1), ("tensor", 2), ("dp", 1), ("dp", 2), ("dp", 4)]
    copies = []

    barrier = pltpu.get_barrier_semaphore()
    for axis, bit in hops:
        pl.semaphore_signal(barrier, inc=1, device_id=partner(axis, bit), device_id_type=pl.DeviceIdType.MESH)
    pl.semaphore_wait(barrier, len(hops))

    def send(src, dst, axis, bit):
        index = len(copies)
        copy = pltpu.make_async_remote_copy(
            src_ref=src,
            dst_ref=dst,
            send_sem=send_sem.at[index],
            recv_sem=recv_sem.at[index],
            device_id=partner(axis, bit),
            device_id_type=pl.DeviceIdType.MESH,
        )
        copy.start()
        copies.append(copy)
        return copy

    def side(bit, flip):
        return 1 - bit if flip else bit

    stage = {}
    gain_out[0] = gains_ref[...]
    stage["gains"] = send(gain_out.at[0], gain_in.at[0], *hops[0])

    def gain_hop(index):
        stage["gains"].wait_recv()
        total = gain_out[index] + gain_in[index]
        if index + 1 < len(hops):
            gain_out[index + 1] = total
            stage["gains"] = send(gain_out.at[index + 1], gain_in.at[index + 1], *hops[index + 1])
        else:
            sums_ref[...] = total

    for m in range(ones, ones + twos):
        for c in (1, 0):
            stage[m, "z", c] = send(away[m].at[side(z2, c)], first[m].at[c], "dp", 2)
    for m in range(ones):
        stage[m, "last"] = send(away[m], first[m], "dp", 4)

    def send_all(m):
        for a in (1, 0):
            for c in (1, 0):
                stage[m, a, c] = send(away[m].at[side(z1, a) + 2 * side(z2, c)], first[m].at[2 * a + c], "dp", 1)

    loads = [pltpu.make_async_copy(kept[m], own[m], load_sem.at[m]) for m in range(mats)]
    for load in loads:
        load.start()
    send_all(ones + twos)
    gain_hop(0)
    gain_hop(1)
    for m in range(ones + twos + 1, mats):
        send_all(m)
    for load in loads:
        load.wait()

    def wide(value):
        return value.astype(jnp.float32)

    def from_x(m, a, c):
        stage[m, a, c].wait_recv()
        total = wide(own[m][side(z1, a) + 2 * side(z2, c)]) + wide(first[m][2 * a + c])
        i = m - ones - twos
        if a:
            to_z[i][c] = total.astype(jnp.bfloat16)
            stage[m, "z", c] = send(to_z[i].at[c], from_z[i].at[c], "dp", 2)
        else:
            held[i][c] = total

    def from_near(m, c):
        stage[m, "z", c].wait_recv()
        if m < ones + twos:
            total = wide(own[m][side(z2, c)]) + wide(first[m][c])
            dst = total_s[m - ones]
        else:
            total = held[m - ones - twos][c] + wide(from_z[m - ones - twos][c])
            dst = outs[m]
        if c:
            to_last[m - ones][...] = total.astype(jnp.bfloat16)
            stage[m, "last"] = send(to_last[m - ones], from_last[m - ones], "dp", 4)
        else:
            dst[...] = total

    def finish(m):
        stage[m, "last"].wait_recv()
        if m < ones:
            outs[m][...] = wide(own[m][0]) + wide(first[m][0])
        elif m < ones + twos:
            outs[m][...] = (total_s[m - ones][...] + wide(from_last[m - ones][...])).T
        else:
            outs[m][...] += wide(from_last[m - ones][...])

    up, out, q, k, v = range(5)
    from_near(out, 1)
    from_x(q, 1, 1)
    from_x(q, 1, 0)
    from_near(out, 0)
    from_x(q, 0, 1)
    from_x(q, 0, 0)
    done_ref[...] = (wide(ready_ref[0]) + wide(got_ref[0])).T
    from_x(k, 1, 1)
    from_near(q, 1)
    from_x(k, 1, 0)
    from_near(q, 0)
    from_x(k, 0, 1)
    from_x(k, 0, 0)
    gain_hop(2)
    from_x(v, 1, 1)
    from_near(k, 1)
    from_x(v, 1, 0)
    from_near(k, 0)
    gain_hop(3)
    finish(up)
    from_x(v, 0, 1)
    from_x(v, 0, 0)
    finish(out)
    from_near(v, 1)
    from_near(v, 0)
    gain_hop(4)
    for m in (q, k, v):
        finish(m)
    for copy in copies:
        copy.wait_send()


def last_stages(ones, twos, threes, ready, gains):
    mats = [*ones, *twos, *threes]
    away, kept = [m[0] for m in mats], [m[1] for m in mats]
    shapes = [a.shape for a in away]
    low, wide = jnp.bfloat16, jnp.float32
    late, last = shapes[len(ones) + len(twos) :], shapes[len(ones) :]
    flat = [shape[1:] for shape in shapes]
    for m in range(len(ones), len(ones) + len(twos)):
        flat[m] = flat[m][::-1]
    any_space = pl.BlockSpec(memory_space=pl.ANY)
    inside = pl.BlockSpec(memory_space=pltpu.VMEM)
    count = len(ones) + 3 * len(twos) + 7 * len(threes) + 5
    result = pl.pallas_call(
        functools.partial(last_body, len(ones), len(twos), len(threes)),
        in_specs=[any_space] * (2 * len(mats)) + [inside] * 3,
        out_specs=[inside] * (len(mats) + 2),
        out_shape=[jax.ShapeDtypeStruct(shape, wide) for shape in flat]
        + [jax.ShapeDtypeStruct(ready[0].shape[:0:-1], wide), jax.ShapeDtypeStruct(gains.shape, wide)],
        scratch_shapes=[pltpu.VMEM(shape, low) for shape in shapes]
        + [pltpu.VMEM(shape, low) for shape in shapes]
        + [pltpu.VMEM((2,) + shape[1:], wide) for shape in late]
        + [pltpu.VMEM((2,) + shape[1:], low) for shape in late]
        + [pltpu.VMEM((2,) + shape[1:], low) for shape in late]
        + [pltpu.VMEM(shape[1:], low) for shape in last]
        + [pltpu.VMEM(shape[1:], low) for shape in last]
        + [pltpu.VMEM(shape[1:], wide) for shape in last[: len(twos)]]
        + [pltpu.VMEM((5,) + gains.shape, wide)] * 2
        + [pltpu.SemaphoreType.DMA((len(mats),)), pltpu.SemaphoreType.DMA((count,)), pltpu.SemaphoreType.DMA((count,))],
        compiler_params=pltpu.CompilerParams(vmem_limit_bytes=62 << 20, collective_id=8),
        cost_estimate=cost(flops=1 << 24, bytes_accessed=1 << 25, transcendentals=0),
        name="last_stages",
    )(*away, *kept, *ready, gains)
    return result[:-2], result[-2], result[-1]


def row_tables(length_row, group_row, mask_row):
    starts = jnp.cumsum(length_row) - length_row
    token = jnp.arange(ROWS, dtype=jnp.int32)
    doc_index = jnp.sum((token[:, None] >= starts[None, 1:]).astype(jnp.int32), axis=1)
    onehot = doc_index[:, None] == jnp.arange(DOCS, dtype=jnp.int32)[None, :]
    first = jnp.sum(jnp.where(onehot, starts[None, :], 0), axis=1)
    group_tok = jnp.sum(jnp.where(onehot, group_row[None, :], 0), axis=1)
    real = jnp.sum(jnp.where(onehot, mask_row[:, None], 0), axis=0)
    last_real = first + jnp.sum(jnp.where(onehot, real[None, :], 0), axis=1) - 1
    return (token - first, first, jnp.minimum(token, last_real), group_tok)


def rope_tables(inside):
    freq = rope_base ** (-jnp.arange(0, HEAD_DIM // 2, dtype=jnp.float32) * 2.0 / HEAD_DIM)
    angle = inside.astype(jnp.float32)[:, None] * freq[None, :]
    cosine, sine = jnp.cos(angle), jnp.sin(angle)
    return (
        jnp.concatenate([cosine, cosine], axis=-1),
        jnp.concatenate([-sine, sine], axis=-1),
        jnp.concatenate([sine, -sine], axis=-1),
    )


def rows_dot(left, right):
    return jnp.dot(left, right, preferred_element_type=jnp.float32)


def rows_dot_t(left, right):
    return lax.dot_general(left, right, NT, preferred_element_type=jnp.float32)


def exchange(values, axis, bit):
    size = lax.axis_size(axis)
    return lax.ppermute(values, axis, [(rank, rank ^ bit) for rank in range(size)])


def butterfly_sum(values, axis):
    size = lax.axis_size(axis)
    bit = 1
    while bit < size:
        values = values + exchange(values, axis, bit)
        bit *= 2
    return values


def tie(*values):
    return lax.optimization_barrier(values)


def scatter_small(values, axis):
    size = lax.axis_size(axis)
    rank = lax.axis_index(axis)
    kept = values
    bit = 1
    while bit < size:
        pairs = kept.reshape((kept.shape[0], kept.shape[1] // 2, 2) + kept.shape[2:])
        side = (rank // bit) % 2
        own = lax.dynamic_index_in_dim(pairs, side, axis=2, keepdims=False)
        away = lax.dynamic_index_in_dim(pairs, 1 - side, axis=2, keepdims=False)
        kept = own + exchange(away, axis, bit)
        bit *= 2
    return kept[:, 0]


class WeightGrad:
    def __init__(self, rank, pieces, mats, start=1):
        self.rank, self.pieces, self.mats, self.start = rank, pieces, mats, start
        self.size = lax.axis_size("dp")
        self.tile = pieces[0].shape[1] // self.size
        self.kernel = self.tile % 128 == 0

    def bits(self):
        return [2**i for i in range(self.size.bit_length() - 1)]

    def compute(self, *sides):
        if self.kernel:
            outs = grad_call(self.rank, self.pieces, self.mats, self.start, sides, self.tile)
        else:
            left = jnp.concatenate(self.pieces, axis=0)
            place = jnp.arange(self.size // 2, dtype=jnp.int32)
            bit = self.rank[0] // self.start % 2
            fulls = [
                lax.dot_general(left, jnp.concatenate(mat, axis=0), TN, preferred_element_type=jnp.float32)
                .astype(jnp.bfloat16)
                .reshape(self.size, self.tile, -1)
                for mat in self.mats
            ]
            outs = [
                jnp.take(full, block_at(place, self.start, (bit + side) % 2), axis=0) for side in sides for full in fulls
            ]
        return tuple(outs)


class Halving:
    def __init__(self, rank, own, start=1):
        self.rank, self.kept = rank, own
        self.size = lax.axis_size("dp")
        self.left = [2**i for i in range(self.size.bit_length() - 1) if 2**i != start]

    def merge(self, got, bit):
        low = 2 ** self.left.index(bit)
        self.left.remove(bit)
        if got.shape[1] % 128 == 0:
            away, self.kept = merge_call(self.rank, self.kept, got, low, bit)
            return away
        total = self.kept.astype(jnp.float32) + got.astype(jnp.float32)
        place = jnp.arange(total.shape[0] // 2, dtype=jnp.int32)
        side = self.rank[0] // bit % 2
        self.kept = jnp.take(total, block_at(place, low, side), axis=0)
        return jnp.take(total, block_at(place, low, 1 - side), axis=0).astype(jnp.bfloat16)

    def finish(self, got):
        while self.left:
            bit = self.left[0]
            got = exchange(self.merge(got, bit), "dp", bit)
        return (self.kept.astype(jnp.float32) + got.astype(jnp.float32))[0]


def hop(values, bit):
    return exchange(values, "dp", bit)


def shards(
    hidden_in,
    cotangent,
    gain_attn,
    w_query,
    w_key,
    w_value,
    w_out,
    gain_mlp,
    w_gate,
    w_up,
    w_down,
    doc_lengths,
    doc_groups,
    pad_mask,
):
    rows_local = hidden_in.shape[0]
    rank = lax.axis_index("tensor").astype(jnp.int32)
    rank_ref = rank[None]
    dp_rank = lax.axis_index("dp").astype(jnp.int32)[None]

    def to_far(values):
        return exchange(values, "tensor", 2)

    def to_mate(values):
        return exchange(values, "tensor", 1)

    x_f = hidden_in.astype(jnp.float32)
    inv_a = lax.rsqrt(jnp.mean(x_f * x_f, axis=-1, keepdims=True) + epsilon)
    a0 = (x_f * inv_a * gain_attn).astype(jnp.bfloat16)
    a2 = to_far(a0)
    a1 = to_mate(a0)
    a3 = to_mate(a2)

    inside, low, high, group_tok = row_tables(doc_lengths[0], doc_groups[0], pad_mask[0])
    low, high = low[None], high[None]
    real_tok = pad_mask[0].astype(jnp.float32)
    onehot_g = group_tok[:, None] == jnp.arange(GROUPS, dtype=jnp.int32)[None, :]
    counts = butterfly_sum(jnp.sum(jnp.where(onehot_g, real_tok[:, None], 0.0), axis=0), "dp")
    live = jnp.sum(counts)
    group_scale = jnp.sqrt(live / (GROUPS * jnp.maximum(counts, 1.0)))
    token_weight = real_tok * jnp.sum(jnp.where(onehot_g, group_scale[None, :], 0.0), axis=-1)
    weight_local = lax.dynamic_slice_in_dim(token_weight, rank * rows_local, rows_local)
    c0 = (cotangent.astype(jnp.float32) * weight_local[:, None]).astype(jnp.bfloat16)
    cosine, sine, back_sine = rope_tables(inside)

    near = qkv_pair(0, rank_ref, a0, a1, cosine, sine, w_query, w_key, w_value)
    a2, c0, *near = tie(a2, c0, *near)
    a3 = to_mate(a2)
    c2 = to_far(c0)
    c1 = to_mate(c0)
    far = qkv_pair(2, rank_ref, a2, a3, cosine, sine, w_query, w_key, w_value)
    qs, ks, vs = zip(near, far)
    heads_near, heads_far, lse = attend(rank_ref, qs, ks, vs, low, high)
    y1 = pair_sum([(heads_far, w_out, False)], 0, jnp.bfloat16)
    heads_n, c1, c2, y1 = tie(heads_near, c1, c2, y1)
    got = to_far(y1)
    c3 = to_mate(c2)
    mine = pair_sum([(heads_n, w_out, False)], 1, jnp.float32)
    dm_near = project([((c0, c1), w_down, True)], jnp.float32)
    dm_far = project([((c2, c3), w_down, True)], jnp.float32)
    got, dm_near, dm_far, mine = tie(got, dm_near, dm_far, mine)
    mid_h = x_f + mine + got.astype(jnp.float32)
    inv_b = lax.rsqrt(jnp.mean(mid_h * mid_h, axis=-1, keepdims=True) + epsilon)
    b0 = (mid_h * inv_b * gain_mlp).astype(jnp.bfloat16)
    b2 = to_far(b0)
    b1 = to_mate(b0)
    mid_near, dg_near, du_near = mlp_pair(b0, b1, dm_near, w_gate, w_up)
    mine8 = pair_sum([(mid_near, w_down, False)], 5, jnp.float32)
    b2, mid_near, dg_near, du_near, mine8 = tie(b2, mid_near, dg_near, du_near, mine8)
    b3 = to_mate(b2)
    mid_far, dg_far, du_far = mlp_pair(b2, b3, dm_far, w_gate, w_up)

    half = lax.axis_size("dp") // 2
    b_all, c_all = (b0, b1, b2, b3), (c0, c1, c2, c3)
    grad_down = WeightGrad(dp_rank, c_all, [(mid_near, mid_far)])
    grad_gate = WeightGrad(dp_rank, b_all, [(dg_near, dg_far)], 2)
    (down_send,) = grad_down.compute(1)
    dg_f, du_f, down_send = tie(dg_far, du_far, down_send)
    down_got = hop(down_send, 1)
    (gate_send,) = grad_gate.compute(1)
    gate_got = hop(gate_send, 2)
    y5 = pair_sum([(dg_f, w_gate, True), (du_f, w_up, True)], 2, jnp.bfloat16)
    dg_n, du_n, mid_n, y5 = tie(dg_near, du_near, mid_near, y5)
    got = to_far(y5)
    d_b = pair_sum([(dg_n, w_gate, True), (du_n, w_up, True)], 3, jnp.float32) + got.astype(jnp.float32)
    (up_send,) = WeightGrad(dp_rank, b_all, [(du_n, du_far)]).compute(1)
    (down_own,) = WeightGrad(dp_rank, c_all, [(mid_n, mid_far)]).compute(0)
    d_b, up_send, down_got, down_own = tie(d_b, up_send, down_got, down_own)
    up_got = hop(up_send, 1)
    down = Halving(dp_rank, down_own)
    down_got = hop(down.merge(down_got, 2), 2)

    n_b = mid_h * inv_b
    gain_mlp_part = jnp.sum(d_b * n_b, axis=0)
    e_b = d_b * gain_mlp
    weighted = cotangent.astype(jnp.float32) * weight_local[:, None]
    d_h = weighted + inv_b * (e_b - n_b * jnp.mean(e_b * n_b, axis=-1, keepdims=True))
    t0 = d_h.astype(jnp.bfloat16)
    t0, mid_f, dg_n, du_n = tie(t0, mid_far, dg_near, du_near)
    t2 = to_far(t0)
    t1 = to_mate(t0)
    gs_near = project([((t0, t1), w_out, True)])
    y8 = pair_sum([(mid_f, w_down, False)], 4, jnp.bfloat16)
    (gate_own,) = WeightGrad(dp_rank, b_all, [(dg_n, dg_far)], 2).compute(0)
    t2, gate_got, gs_near, y8, gate_own = tie(t2, gate_got, gs_near, y8, gate_own)

    got8 = to_far(y8)
    gate = Halving(dp_rank, gate_own, 2)
    t3 = to_mate(t2)
    gs_far = project([((t2, t3), w_out, True)])
    gate_got = hop(gate.merge(gate_got, 1), 1)
    (up_own,) = WeightGrad(dp_rank, b_all, [(du_n, du_far)]).compute(0)
    out_send, out_own = WeightGrad(dp_rank, (t0, t1, t2, t3), [(heads_near, heads_far)]).compute(1, 0)
    gs_far, up_got, down_got, up_own, out_send = tie(gs_far, up_got, down_got, up_own, out_send)
    up = Halving(dp_rank, up_own)
    up_got = hop(up.merge(up_got, 2), 2)
    down_got = hop(down.merge(down_got, half), half)
    dqn, dqf, dkn, dkf, dvn, dvf = attend_back(
        rank_ref, qs, ks, vs, (gs_near, gs_far), low, high, lse, cosine, back_sine
    )
    dqf, dkf, dvf, got8, out_send = tie(dqf, dkf, dvf, got8, out_send)

    out_got = hop(out_send, 1)
    y7 = pair_sum([(dqf, w_query, True), (dkf, w_key, True), (dvf, w_value, True)], 6, jnp.bfloat16)
    got = to_far(y7)
    dqn, dkn, dvn, y7, up_got, gate_got, down_got = tie(dqn, dkn, dvn, y7, up_got, gate_got, down_got)
    gate_got = hop(gate.merge(gate_got, half), half)
    up_away = up.merge(up_got, half)
    grad_qkv = WeightGrad(dp_rank, (a0, a1, a2, a3), [(dqn, dqf), (dkn, dkf), (dvn, dvf)])
    *sends, q_own, k_own, v_own = grad_qkv.compute(1, 0)
    d_a = pair_sum([(dqn, w_query, True), (dkn, w_key, True), (dvn, w_value, True)], 7, jnp.float32) + got.astype(jnp.float32)
    d_a, out_got, gate_got, up_away, *sends = tie(d_a, out_got, gate_got, up_away, *sends)

    out = Halving(dp_rank, out_own)
    out_away = out.merge(out_got, 2)
    output = (mid_h + mine8 + got8.astype(jnp.float32)).astype(jnp.bfloat16)
    n_a = x_f * inv_a
    gain_attn_part = jnp.sum(d_a * n_a, axis=0)
    e_a = d_a * gain_attn
    grad_input = d_h + inv_a * (e_a - n_a * jnp.mean(e_a * n_a, axis=-1, keepdims=True))
    gains = jnp.stack([gain_attn_part, gain_mlp_part])
    sum_gate = gate.finish(gate_got)
    if grad_qkv.kernel and half == 4:
        (sum_up, sum_out, *sums), sum_down, gains = last_stages(
            [(up_away, up.kept)],
            [(out_away, out.kept)],
            list(zip(sends, (q_own, k_own, v_own))),
            (down.kept, down_got),
            gains,
        )
        gains = lax.dynamic_slice_in_dim(gains, dp_rank[0] * grad_qkv.tile, grad_qkv.tile, 1)
    else:
        gains = butterfly_sum(scatter_small(gains.reshape(2, lax.axis_size("dp"), -1), "dp"), "tensor")
        sum_up = up.finish(hop(up_away, half))
        sum_out = out.finish(hop(out_away, 2)).T
        sum_down = down.finish(down_got).T
        sums = [Halving(dp_rank, own).finish(hop(send, 1)) for send, own in zip(sends, (q_own, k_own, v_own))]
    return (
        output,
        grad_input,
        gains[0],
        sums[0],
        sums[1],
        sums[2],
        sum_out,
        gains[1],
        sum_gate,
        sum_up,
        sum_down,
    )


def solution(mesh):
    rows, columns, split = P(("dp", "tensor"), None), P(None, "tensor"), P("tensor", None)
    in_specs = (
        rows,
        rows,
        P(),
        columns,
        columns,
        columns,
        split,
        P(),
        columns,
        columns,
        split,
        P("dp", None),
        P("dp", None),
        P("dp", None),
    )
    grads = P("dp", "tensor")
    grads_t = P("tensor", "dp")
    out_specs = (rows, rows, P("dp"), grads, grads, grads, grads_t, P("dp"), grads, grads, grads_t)
    return jax.shard_map(shards, mesh=mesh, in_specs=in_specs, out_specs=out_specs, check_vma=False)
```

```python
import functools

import jax
import jax.numpy as jnp
from jax import lax
from jax.experimental import pallas as pl
from jax.experimental.pallas import tpu as pltpu
from jax.sharding import PartitionSpec as P

HEAD_DIM = 128
ROWS = 1280
DOCS = 3
GROUPS = 8
QTILE = 256

epsilon = 1e-05
masked_score = -1e30
rope_base = 10000.0
COST = 1000


def cost(flops, bytes_accessed, transcendentals):
    return pl.CostEstimate(
        flops=flops // COST, bytes_accessed=bytes_accessed // COST, transcendentals=transcendentals // COST
    )


NT = (((1,), (1,)), ((), ()))
TN = (((0,), (0,)), ((), ()))
NN = (((1,), (0,)), ((), ()))


def mm(left, right, dims=NN):
    return lax.dot_general(left, right, dims, preferred_element_type=jnp.float32)


def whole(shape):
    return pl.BlockSpec(shape, lambda *_: (0,) * len(shape))


def turn(values, cosine, sine):
    return values * cosine + pltpu.roll(values, HEAD_DIM // 2, 1) * sine


def qkv_body(first, rank_ref, xa_ref, xb_ref, cos_ref, sin_ref, wq_ref, wk_ref, wv_ref, q_ref, k_ref, v_ref, x_s):
    rows = xa_ref.shape[0]
    lay_together((xa_ref, xb_ref), x_s)
    for w_ref, out_ref in ((wq_ref, q_ref), (wk_ref, k_ref)):
        full = mm(x_s[...], w_ref[...])
        for half in range(2):
            span = pl.ds(half * rows, rows)
            place = pl.ds(pl.multiple_of((rank_ref[0] ^ (first + half)) * rows, rows), rows)
            cosine, sine = cos_ref[place, :], sin_ref[place, :]
            for head in range(full.shape[1] // HEAD_DIM):
                lanes = slice(head * HEAD_DIM, (head + 1) * HEAD_DIM)
                part = full[half * rows : (half + 1) * rows, lanes]
                out_ref[span, lanes] = turn(part, cosine, sine).astype(jnp.bfloat16)
    v_ref[...] = mm(x_s[...], wv_ref[...]).astype(jnp.bfloat16)


def qkv_pair(first, rank, xa, xb, cosine, sine, wq, wk, wv):
    rows, depth = xa.shape
    width = wq.shape[1]
    tile = 256
    wspec = pl.BlockSpec((depth, tile), lambda j, *_: (0, j))
    ospec = pl.BlockSpec((2 * rows, tile), lambda j, *_: (0, j))
    out = jax.ShapeDtypeStruct((2 * rows, width), jnp.bfloat16)
    return pl.pallas_call(
        functools.partial(qkv_body, first),
        grid_spec=pltpu.PrefetchScalarGridSpec(
            num_scalar_prefetch=1,
            grid=(width // tile,),
            in_specs=[whole(xa.shape)] * 2 + [whole(cosine.shape)] * 2 + [wspec] * 3,
            out_specs=[ospec] * 3,
            scratch_shapes=[pltpu.VMEM((2 * rows, depth), jnp.bfloat16)],
        ),
        out_shape=[out] * 3,
        compiler_params=pltpu.CompilerParams(vmem_limit_bytes=60 << 20),
        cost_estimate=cost(
            flops=12 * rows * depth * width, bytes_accessed=6 * depth * width + 4 * rows * depth, transcendentals=0
        ),
        name="qkv",
    )(rank, xa, xb, cosine, sine, wq, wk, wv)


def in_order(rank_ref, near_ref, far_ref, out_ref):
    piece = near_ref.shape[0] // 2
    for index in range(4):
        src = (near_ref, far_ref)[index // 2]
        at = pl.multiple_of((rank_ref[0] ^ index) * piece, piece)
        out_ref[pl.ds(at, piece), :] = src[pl.ds((index % 2) * piece, piece), :]


def out_of_order(rank_ref, src_ref, near_ref, far_ref):
    piece = near_ref.shape[0] // 2
    for index in range(4):
        dst = (near_ref, far_ref)[index // 2]
        at = pl.multiple_of((rank_ref[0] ^ index) * piece, piece)
        dst[pl.ds((index % 2) * piece, piece), :] = src_ref[pl.ds(at, piece), :].astype(dst.dtype)


def attend_body(rank_ref, qn, qf, kn, kf, vn, vf, low_ref, high_ref, on, of, lse_ref, q_s, k_s, v_s, o_s):
    in_order(rank_ref, qn, qf, q_s)
    in_order(rank_ref, kn, kf, k_s)
    in_order(rank_ref, vn, vf, v_s)
    scale = HEAD_DIM ** (-0.5)
    v_t = v_s[...].T
    for block in range(q_s.shape[0] // QTILE):
        span = pl.ds(block * QTILE, QTILE)
        end = (block + 1) * QTILE
        scores = mm(k_s[:end, :], q_s[span, :], NT)
        at = lax.broadcasted_iota(jnp.int32, scores.shape, 0)
        allowed = (at >= low_ref[:, span]) & (at <= high_ref[:, span])
        scores = jnp.where(allowed, scores * scale, masked_score)
        top = jnp.max(scores, axis=0, keepdims=True)
        prob = jnp.exp(scores - top)
        total = jnp.sum(prob, axis=0, keepdims=True)
        lse_ref[0, :, span] = top + jnp.log(total)
        out_t = mm(v_t[:, :end], prob.astype(jnp.bfloat16)) * (1.0 / total)
        o_s[span, :] = out_t.T
    out_of_order(rank_ref, o_s, on, of)


def attend(rank, qs, ks, vs, low, high):
    half, width = qs[0].shape
    rows = 2 * half
    heads = width // HEAD_DIM
    hspec = pl.BlockSpec((half, HEAD_DIM), lambda h, *_: (0, h))
    row = whole((1, rows))
    return pl.pallas_call(
        attend_body,
        grid_spec=pltpu.PrefetchScalarGridSpec(
            num_scalar_prefetch=1,
            grid=(heads,),
            in_specs=[hspec] * 6 + [row] * 2,
            out_specs=[hspec] * 2 + [pl.BlockSpec((1, 1, rows), lambda h, *_: (h, 0, 0))],
            scratch_shapes=[pltpu.VMEM((rows, HEAD_DIM), jnp.bfloat16)] * 3 + [pltpu.VMEM((rows, HEAD_DIM), jnp.float32)],
        ),
        out_shape=[jax.ShapeDtypeStruct((half, width), jnp.bfloat16)] * 2
        + [jax.ShapeDtypeStruct((heads, 1, rows), jnp.float32)],
        compiler_params=pltpu.CompilerParams(vmem_limit_bytes=60 << 20),
        cost_estimate=cost(
            flops=8 * rows * rows * width, bytes_accessed=8 * rows * width, transcendentals=heads * rows * rows // 2
        ),
        name="attend",
    )(rank, *qs, *ks, *vs, low, high)


def attend_back_body(
    rank_ref, qn, qf, kn, kf, vn, vf, gn, gf, low_ref, high_ref, lse_ref, cos_ref, sin_ref,
    dqn, dqf, dkn, dkf, dvn, dvf, q_s, k_s, v_s, g_s, dq_s, dk_s, dv_s,
):
    in_order(rank_ref, qn, qf, q_s)
    in_order(rank_ref, kn, kf, k_s)
    in_order(rank_ref, vn, vf, v_s)
    in_order(rank_ref, gn, gf, g_s)
    scale = HEAD_DIM ** (-0.5)
    k_t = k_s[...].T
    blocks = q_s.shape[0] // QTILE
    for block in reversed(range(blocks)):
        span = pl.ds(block * QTILE, QTILE)
        end = (block + 1) * QTILE
        query, grad = q_s[span, :], g_s[span, :]
        scores = mm(k_s[:end, :], query, NT) * scale
        at = lax.broadcasted_iota(jnp.int32, scores.shape, 0)
        allowed = (at >= low_ref[:, span]) & (at <= high_ref[:, span])
        prob = jnp.exp(jnp.where(allowed, scores, masked_score) - lse_ref[0, :, span])
        d_prob = mm(v_s[:end, :], grad, NT)
        dot = jnp.sum(prob * d_prob, axis=0, keepdims=True)
        d_score = (prob * (d_prob - dot) * scale).astype(jnp.bfloat16)
        dq_s[span, :] = mm(k_t[:, :end], d_score).T
        d_key = mm(d_score, query)
        d_value = mm(prob.astype(jnp.bfloat16), grad)
        if block == blocks - 1:
            dk_s[...] = d_key
            dv_s[...] = d_value
        else:
            dk_s[:end, :] += d_key
            dv_s[:end, :] += d_value
    dq_s[...] = turn(dq_s[...], cos_ref[...], sin_ref[...])
    dk_s[...] = turn(dk_s[...], cos_ref[...], sin_ref[...])
    out_of_order(rank_ref, dq_s, dqn, dqf)
    out_of_order(rank_ref, dk_s, dkn, dkf)
    out_of_order(rank_ref, dv_s, dvn, dvf)


def attend_back(rank, qs, ks, vs, gs, low, high, lse, cosine, back_sine):
    half, width = qs[0].shape
    rows = 2 * half
    heads = width // HEAD_DIM
    hspec = pl.BlockSpec((half, HEAD_DIM), lambda h, *_: (0, h))
    row = whole((1, rows))
    return pl.pallas_call(
        attend_back_body,
        grid_spec=pltpu.PrefetchScalarGridSpec(
            num_scalar_prefetch=1,
            grid=(heads,),
            in_specs=[hspec] * 8
            + [row] * 2
            + [pl.BlockSpec((1, 1, rows), lambda h, *_: (h, 0, 0))]
            + [whole((rows, HEAD_DIM))] * 2,
            out_specs=[hspec] * 6,
            scratch_shapes=[pltpu.VMEM((rows, HEAD_DIM), jnp.bfloat16)] * 4
            + [pltpu.VMEM((rows, HEAD_DIM), jnp.float32)] * 3,
        ),
        out_shape=[jax.ShapeDtypeStruct((half, width), jnp.bfloat16)] * 6,
        compiler_params=pltpu.CompilerParams(vmem_limit_bytes=60 << 20),
        cost_estimate=cost(
            flops=20 * rows * rows * width, bytes_accessed=16 * rows * width, transcendentals=heads * rows * rows // 2
        ),
        name="attend_back",
    )(rank, *qs, *ks, *vs, *gs, low, high, lse, cosine, back_sine)


def mlp_body(xa_ref, xb_ref, dm_ref, wg_ref, wu_ref, mid_ref, dg_ref, du_ref, x_s):
    rows = xa_ref.shape[0]
    lay_together((xa_ref, xb_ref), x_s)
    gates, ups = mm(x_s[...], wg_ref[...]), mm(x_s[...], wu_ref[...])
    for half in range(2):
        span = pl.ds(half * rows, rows)
        gate, up = (both[half * rows : (half + 1) * rows, :] for both in (gates, ups))
        d_mid = dm_ref[span, :]
        sigma = 1.0 / (1.0 + jnp.exp(-gate))
        active = gate * sigma
        mid_ref[span, :] = (active * up).astype(jnp.bfloat16)
        dg_ref[span, :] = (d_mid * up * sigma * (1.0 + gate * (1.0 - sigma))).astype(jnp.bfloat16)
        du_ref[span, :] = (d_mid * active).astype(jnp.bfloat16)


def mlp_pair(xa, xb, d_mid, wg, wu):
    rows, depth = xa.shape
    width = wg.shape[1]
    tile = 256
    wspec = pl.BlockSpec((depth, tile), lambda j: (0, j))
    ospec = pl.BlockSpec((2 * rows, tile), lambda j: (0, j))
    return pl.pallas_call(
        mlp_body,
        grid=(pl.cdiv(width, tile),),
        in_specs=[whole(xa.shape)] * 2 + [ospec] + [wspec] * 2,
        out_specs=[ospec] * 3,
        out_shape=[jax.ShapeDtypeStruct((2 * rows, width), jnp.bfloat16)] * 3,
        scratch_shapes=[pltpu.VMEM((2 * rows, depth), jnp.bfloat16)],
        compiler_params=pltpu.CompilerParams(vmem_limit_bytes=60 << 20),
        cost_estimate=cost(
            flops=8 * rows * depth * width,
            bytes_accessed=4 * depth * width + 4 * rows * depth + 20 * rows * width,
            transcendentals=2 * rows * width,
        ),
        name="mlp",
    )(xa, xb, d_mid, wg, wu)


def gather_rows(parts, out_ref):
    at = 0
    for part in parts:
        out_ref[at : at + part.shape[0], :] = part[...]
        at += part.shape[0]


def gather_sides(rights, out_ref):
    at = 0
    for near, far in zip(rights[::2], rights[1::2]):
        rows, width = near.shape
        out_ref[:rows, at : at + width] = near[...]
        out_ref[rows:, at : at + width] = far[...]
        at += width


def block_at(place, low, side):
    return place // low * (2 * low) + place % low + low * side


def filled(step, low, side):
    group, half = step // (2 * low), step // low % 2
    here = jnp.where(half == side, step % low, jnp.where(half > side, low - 1, -1))
    return jnp.maximum(group * low + here, 0)


def grad_body(pieces, widths, low, sides, rank_ref, *refs):
    left, rights = refs[:pieces], refs[pieces : pieces + 2 * len(widths)]
    outs, (left_s, right_s) = refs[pieces + 2 * len(widths) : -2], refs[-2:]
    step = pl.program_id(0)

    @pl.when(step == 0)
    def _():
        gather_sides(rights, right_s)

    gather_rows(left, left_s)
    total = mm(left_s[...], right_s[...], TN).astype(jnp.bfloat16)

    def store(refs):
        at = 0
        for ref, width in zip(refs, widths):
            ref[0] = total[:, at : at + width]
            at += width

    if len(sides) == 1:
        store(outs)
    else:
        sent = step // low % 2 != rank_ref[0] // low % 2
        pl.when(sent)(lambda: store(outs[: len(widths)]))
        pl.when(jnp.logical_not(sent))(lambda: store(outs[len(widths) :]))


def grad_call(rank, pieces, mats, low, sides, tile):
    rows, depth = pieces[0].shape[0] * len(pieces), pieces[0].shape[1]
    widths = [near.shape[1] for near, _ in mats]
    width, half = sum(widths), depth // tile // 2
    count = half * len(sides)

    def own(s, side):
        bit = s[0] // low % 2
        return 1 - bit if side else bit

    if len(sides) == 1:
        lspec = pl.BlockSpec((pieces[0].shape[0], tile), lambda j, s: (0, block_at(j, low, own(s, sides[0]))))
    else:
        lspec = pl.BlockSpec((pieces[0].shape[0], tile), lambda j, s: (0, j))
    out_specs = []
    for side in sides:
        for w in widths:
            if len(sides) == 1:
                out_specs.append(pl.BlockSpec((1, tile, w), lambda j, s: (j, 0, 0)))
            else:
                out_specs.append(pl.BlockSpec((1, tile, w), lambda j, s, side=side: (filled(j, low, own(s, side)), 0, 0)))
    rights = [part for mat in mats for part in mat]
    return pl.pallas_call(
        functools.partial(grad_body, len(pieces), widths, low, sides),
        grid_spec=pltpu.PrefetchScalarGridSpec(
            num_scalar_prefetch=1,
            grid=(count,),
            in_specs=[lspec] * len(pieces) + [whole(r.shape) for r in rights],
            out_specs=out_specs,
            scratch_shapes=[pltpu.VMEM((rows, tile), jnp.bfloat16), pltpu.VMEM((rows, width), jnp.bfloat16)],
        ),
        out_shape=[jax.ShapeDtypeStruct((half, tile, w), jnp.bfloat16) for _ in sides for w in widths],
        compiler_params=pltpu.CompilerParams(vmem_limit_bytes=60 << 20),
        cost_estimate=cost(
            flops=2 * rows * tile * count * width,
            bytes_accessed=2 * rows * (tile * count + width) + 2 * tile * count * width,
            transcendentals=0,
        ),
        name="weight_grad",
    )(rank, *pieces, *rights)


def merge_body(_, own_away, got_away, own_kept, got_kept, away_ref, kept_ref):
    away_ref[...] = (own_away[...].astype(jnp.float32) + got_away[...].astype(jnp.float32)).astype(jnp.bfloat16)
    kept_ref[...] = (own_kept[...].astype(jnp.float32) + got_kept[...].astype(jnp.float32)).astype(jnp.bfloat16)


def merge_call(rank, own, got, low, bit):
    count, tile, width = own.shape
    away, kept = (
        pl.BlockSpec((1, tile, width), lambda j, s, flip=flip: (block_at(j, low, (s[0] // bit + flip) % 2), 0, 0))
        for flip in (1, 0)
    )
    ospec = pl.BlockSpec((1, tile, width), lambda j, s: (j, 0, 0))
    return pl.pallas_call(
        merge_body,
        grid_spec=pltpu.PrefetchScalarGridSpec(
            num_scalar_prefetch=1,
            grid=(count // 2,),
            in_specs=[away, away, kept, kept],
            out_specs=[ospec] * 2,
        ),
        out_shape=[jax.ShapeDtypeStruct((count // 2, tile, width), jnp.bfloat16)] * 2,
        compiler_params=pltpu.CompilerParams(vmem_limit_bytes=40 << 20),
        cost_estimate=cost(flops=count * tile * width, bytes_accessed=6 * count * tile * width, transcendentals=0),
        name="merge",
    )(rank, own, got, own, got)


def product(lefts, weights):
    total = None
    for left, (w_ref, dims) in zip(lefts, weights):
        value = mm(left[...], w_ref[...], dims)
        total = value if total is None else total + value
    return total


def lay_together(parts, out_ref):
    @pl.when(pl.program_id(0) == 0)
    def _():
        gather_rows(parts, out_ref)


def project_body(terms, *refs):
    at, lefts, weights = 0, [], []
    for pieces, dims in terms:
        lefts.append(refs[at : at + pieces])
        weights.append((refs[at + pieces], dims))
        at += pieces + 1
    out_ref, scratch = refs[at], list(refs[at + 1 :])
    for index, left in enumerate(lefts):
        if len(left) > 1:
            lay_together(left, scratch[0])
            lefts[index] = scratch.pop(0)
        else:
            lefts[index] = left[0]
    out_ref[...] = product(lefts, weights).astype(out_ref.dtype)


def terms_of(terms):
    return [(left if isinstance(left, tuple) else (left,), w, NT if flip else NN) for left, w, flip in terms]


def term_specs(terms, tile):
    in_specs, args = [], []
    for left, w, dims in terms:
        depth = left[0].shape[1]
        in_specs += [whole(piece.shape) for piece in left]
        in_specs.append(
            pl.BlockSpec((tile, depth), lambda j: (j, 0)) if dims is NT else pl.BlockSpec((depth, tile), lambda j: (0, j))
        )
        args += [*left, w]
    return in_specs, args


def project(terms, dtype=jnp.bfloat16):
    terms = terms_of(terms)
    rows = sum(piece.shape[0] for piece in terms[0][0])
    width = terms[0][1].shape[0 if terms[0][2] is NT else 1]
    tile = min(512, width)
    in_specs, args = term_specs(terms, tile)
    return pl.pallas_call(
        functools.partial(project_body, [(len(left), dims) for left, _, dims in terms]),
        grid=(pl.cdiv(width, tile),),
        in_specs=in_specs,
        out_specs=pl.BlockSpec((rows, tile), lambda j: (0, j)),
        out_shape=jax.ShapeDtypeStruct((rows, width), dtype),
        scratch_shapes=[
            pltpu.VMEM((rows, left[0].shape[1]), jnp.bfloat16) for left, _, _ in terms if len(left) > 1
        ],
        compiler_params=pltpu.CompilerParams(vmem_limit_bytes=60 << 20),
        cost_estimate=cost(
            flops=2 * rows * width * sum(left[0].shape[1] for left, _, _ in terms),
            bytes_accessed=sum(2 * a.size for a in args) + 2 * rows * width,
            transcendentals=0,
        ),
        name="project",
    )(*args)


def pair_body(terms, steps, *refs):
    at, lefts, weights = 0, [], []
    for pieces, dims in terms:
        lefts.append(refs[at])
        weights.append((refs[at + pieces], dims))
        at += pieces + 1
    out_ref, mine_s, away_s, got_s, send_sem, recv_sem = refs[at:]
    rows = out_ref.shape[0]
    tile = mine_s.shape[2]
    step = pl.program_id(0)
    me = lax.axis_index("tensor")
    mate = {"tensor": me + 1 - 2 * (me % 2)}

    @pl.when(step == 0)
    def _():
        barrier = pltpu.get_barrier_semaphore()
        pl.semaphore_signal(barrier, inc=1, device_id=mate, device_id_type=pl.DeviceIdType.MESH)
        pl.semaphore_wait(barrier, 1)

    def copy(index):
        return pltpu.make_async_remote_copy(
            src_ref=away_s.at[index],
            dst_ref=got_s.at[index],
            send_sem=send_sem.at[index],
            recv_sem=recv_sem.at[index],
            device_id=mate,
            device_id_type=pl.DeviceIdType.MESH,
        )

    total = product(lefts, weights)
    away_s[step] = total[rows:, :].astype(jnp.bfloat16)
    copy(step).start()
    mine_s[step] = total[:rows, :]

    @pl.when(step == steps - 1)
    def _():
        for index in range(steps):
            copy(index).wait()
            both = mine_s[index] + got_s[index].astype(jnp.float32)
            out_ref[:, index * tile : (index + 1) * tile] = both.astype(out_ref.dtype)


def pair_sum(terms, ident, dtype):
    terms = terms_of(terms)
    rows = sum(piece.shape[0] for piece in terms[0][0]) // 2
    width = terms[0][1].shape[0 if terms[0][2] is NT else 1]
    tile = min(512, width)
    steps = width // tile
    in_specs, args = term_specs(terms, tile)
    return pl.pallas_call(
        functools.partial(pair_body, [(len(left), dims) for left, _, dims in terms], steps),
        grid=(steps,),
        in_specs=in_specs,
        out_specs=whole((rows, width)),
        out_shape=jax.ShapeDtypeStruct((rows, width), dtype),
        scratch_shapes=[
            pltpu.VMEM((steps, rows, tile), jnp.float32),
            pltpu.VMEM((steps, rows, tile), jnp.bfloat16),
            pltpu.VMEM((steps, rows, tile), jnp.bfloat16),
            pltpu.SemaphoreType.DMA((steps,)),
            pltpu.SemaphoreType.DMA((steps,)),
        ],
        compiler_params=pltpu.CompilerParams(vmem_limit_bytes=60 << 20, collective_id=ident),
        cost_estimate=cost(
            flops=4 * rows * width * sum(left[0].shape[1] for left, _, _ in terms),
            bytes_accessed=sum(2 * a.size for a in args) + 4 * rows * width,
            transcendentals=0,
        ),
        name="pair_sum",
    )(*args)


def partner(axis, bit):
    rank = lax.axis_index(axis)
    return {axis: rank + bit - 2 * bit * (rank // bit % 2)}


def last_body(ones, twos, threes, *refs):
    mats = ones + twos + threes
    away, kept, refs = refs[:mats], refs[mats : 2 * mats], refs[2 * mats :]
    ready_ref, got_ref, gains_ref, refs = refs[0], refs[1], refs[2], refs[3:]
    outs, done_ref, sums_ref, refs = refs[:mats], refs[mats], refs[mats + 1], refs[mats + 2 :]
    own, first, refs = refs[:mats], refs[mats : 2 * mats], refs[2 * mats :]
    held, to_z, from_z, refs = refs[:threes], refs[threes : 2 * threes], refs[2 * threes : 3 * threes], refs[3 * threes :]
    late = twos + threes
    to_last, from_last, total_s, refs = refs[:late], refs[late : 2 * late], refs[2 * late : 2 * late + twos], refs[2 * late + twos :]
    gain_in, gain_out, load_sem, send_sem, recv_sem = refs
    rank = lax.axis_index("dp")
    z1, z2 = rank // 2 % 2, rank // 4 % 2
    hops = [("tensor", 1), ("tensor", 2), ("dp", 1), ("dp", 2), ("dp", 4)]
    copies = []

    barrier = pltpu.get_barrier_semaphore()
    for axis, bit in hops:
        pl.semaphore_signal(barrier, inc=1, device_id=partner(axis, bit), device_id_type=pl.DeviceIdType.MESH)
    pl.semaphore_wait(barrier, len(hops))

    def send(src, dst, axis, bit):
        index = len(copies)
        copy = pltpu.make_async_remote_copy(
            src_ref=src,
            dst_ref=dst,
            send_sem=send_sem.at[index],
            recv_sem=recv_sem.at[index],
            device_id=partner(axis, bit),
            device_id_type=pl.DeviceIdType.MESH,
        )
        copy.start()
        copies.append(copy)
        return copy

    def side(bit, flip):
        return 1 - bit if flip else bit

    stage = {}
    gain_out[0] = gains_ref[...]
    stage["gains"] = send(gain_out.at[0], gain_in.at[0], *hops[0])

    def gain_hop(index):
        stage["gains"].wait_recv()
        total = gain_out[index] + gain_in[index]
        if index + 1 < len(hops):
            gain_out[index + 1] = total
            stage["gains"] = send(gain_out.at[index + 1], gain_in.at[index + 1], *hops[index + 1])
        else:
            sums_ref[...] = total

    for m in range(ones, ones + twos):
        for c in (1, 0):
            stage[m, "z", c] = send(away[m].at[side(z2, c)], first[m].at[c], "dp", 2)
    for m in range(ones):
        stage[m, "last"] = send(away[m], first[m], "dp", 4)

    def send_all(m):
        for a in (1, 0):
            for c in (1, 0):
                stage[m, a, c] = send(away[m].at[side(z1, a) + 2 * side(z2, c)], first[m].at[2 * a + c], "dp", 1)

    loads = [pltpu.make_async_copy(kept[m], own[m], load_sem.at[m]) for m in range(mats)]
    for load in loads:
        load.start()
    send_all(ones + twos)
    gain_hop(0)
    gain_hop(1)
    for m in range(ones + twos + 1, mats):
        send_all(m)
    for load in loads:
        load.wait()

    def wide(value):
        return value.astype(jnp.float32)

    def from_x(m, a, c):
        stage[m, a, c].wait_recv()
        total = wide(own[m][side(z1, a) + 2 * side(z2, c)]) + wide(first[m][2 * a + c])
        i = m - ones - twos
        if a:
            to_z[i][c] = total.astype(jnp.bfloat16)
            stage[m, "z", c] = send(to_z[i].at[c], from_z[i].at[c], "dp", 2)
        else:
            held[i][c] = total

    def from_near(m, c):
        stage[m, "z", c].wait_recv()
        if m < ones + twos:
            total = wide(own[m][side(z2, c)]) + wide(first[m][c])
            dst = total_s[m - ones]
        else:
            total = held[m - ones - twos][c] + wide(from_z[m - ones - twos][c])
            dst = outs[m]
        if c:
            to_last[m - ones][...] = total.astype(jnp.bfloat16)
            stage[m, "last"] = send(to_last[m - ones], from_last[m - ones], "dp", 4)
        else:
            dst[...] = total

    def finish(m):
        stage[m, "last"].wait_recv()
        if m < ones:
            outs[m][...] = wide(own[m][0]) + wide(first[m][0])
        elif m < ones + twos:
            outs[m][...] = (total_s[m - ones][...] + wide(from_last[m - ones][...])).T
        else:
            outs[m][...] += wide(from_last[m - ones][...])

    up, out, q, k, v = range(5)
    from_near(out, 1)
    from_x(q, 1, 1)
    from_x(q, 1, 0)
    from_near(out, 0)
    from_x(q, 0, 1)
    from_x(q, 0, 0)
    done_ref[...] = (wide(ready_ref[0]) + wide(got_ref[0])).T
    from_x(k, 1, 1)
    from_near(q, 1)
    from_x(k, 1, 0)
    from_near(q, 0)
    from_x(k, 0, 1)
    from_x(k, 0, 0)
    gain_hop(2)
    from_x(v, 1, 1)
    from_near(k, 1)
    from_x(v, 1, 0)
    from_near(k, 0)
    gain_hop(3)
    finish(up)
    from_x(v, 0, 1)
    from_x(v, 0, 0)
    finish(out)
    from_near(v, 1)
    from_near(v, 0)
    gain_hop(4)
    for m in (q, k, v):
        finish(m)
    for copy in copies:
        copy.wait_send()


def last_stages(ones, twos, threes, ready, gains):
    mats = [*ones, *twos, *threes]
    away, kept = [m[0] for m in mats], [m[1] for m in mats]
    shapes = [a.shape for a in away]
    low, wide = jnp.bfloat16, jnp.float32
    late, last = shapes[len(ones) + len(twos) :], shapes[len(ones) :]
    flat = [shape[1:] for shape in shapes]
    for m in range(len(ones), len(ones) + len(twos)):
        flat[m] = flat[m][::-1]
    any_space = pl.BlockSpec(memory_space=pl.ANY)
    inside = pl.BlockSpec(memory_space=pltpu.VMEM)
    count = len(ones) + 3 * len(twos) + 7 * len(threes) + 5
    result = pl.pallas_call(
        functools.partial(last_body, len(ones), len(twos), len(threes)),
        in_specs=[any_space] * (2 * len(mats)) + [inside] * 3,
        out_specs=[inside] * (len(mats) + 2),
        out_shape=[jax.ShapeDtypeStruct(shape, wide) for shape in flat]
        + [jax.ShapeDtypeStruct(ready[0].shape[:0:-1], wide), jax.ShapeDtypeStruct(gains.shape, wide)],
        scratch_shapes=[pltpu.VMEM(shape, low) for shape in shapes]
        + [pltpu.VMEM(shape, low) for shape in shapes]
        + [pltpu.VMEM((2,) + shape[1:], wide) for shape in late]
        + [pltpu.VMEM((2,) + shape[1:], low) for shape in late]
        + [pltpu.VMEM((2,) + shape[1:], low) for shape in late]
        + [pltpu.VMEM(shape[1:], low) for shape in last]
        + [pltpu.VMEM(shape[1:], low) for shape in last]
        + [pltpu.VMEM(shape[1:], wide) for shape in last[: len(twos)]]
        + [pltpu.VMEM((5,) + gains.shape, wide)] * 2
        + [pltpu.SemaphoreType.DMA((len(mats),)), pltpu.SemaphoreType.DMA((count,)), pltpu.SemaphoreType.DMA((count,))],
        compiler_params=pltpu.CompilerParams(vmem_limit_bytes=62 << 20, collective_id=8),
        cost_estimate=cost(flops=1 << 24, bytes_accessed=1 << 25, transcendentals=0),
        name="last_stages",
    )(*away, *kept, *ready, gains)
    return result[:-2], result[-2], result[-1]


def row_tables(length_row, group_row, mask_row):
    starts = jnp.cumsum(length_row) - length_row
    token = jnp.arange(ROWS, dtype=jnp.int32)
    doc_index = jnp.sum((token[:, None] >= starts[None, 1:]).astype(jnp.int32), axis=1)
    onehot = doc_index[:, None] == jnp.arange(DOCS, dtype=jnp.int32)[None, :]
    first = jnp.sum(jnp.where(onehot, starts[None, :], 0), axis=1)
    group_tok = jnp.sum(jnp.where(onehot, group_row[None, :], 0), axis=1)
    real = jnp.sum(jnp.where(onehot, mask_row[:, None], 0), axis=0)
    last_real = first + jnp.sum(jnp.where(onehot, real[None, :], 0), axis=1) - 1
    return (token - first, first, jnp.minimum(token, last_real), group_tok)


def rope_tables(inside):
    freq = rope_base ** (-jnp.arange(0, HEAD_DIM // 2, dtype=jnp.float32) * 2.0 / HEAD_DIM)
    angle = inside.astype(jnp.float32)[:, None] * freq[None, :]
    cosine, sine = jnp.cos(angle), jnp.sin(angle)
    return (
        jnp.concatenate([cosine, cosine], axis=-1),
        jnp.concatenate([-sine, sine], axis=-1),
        jnp.concatenate([sine, -sine], axis=-1),
    )


def rows_dot(left, right):
    return jnp.dot(left, right, preferred_element_type=jnp.float32)


def rows_dot_t(left, right):
    return lax.dot_general(left, right, NT, preferred_element_type=jnp.float32)


def exchange(values, axis, bit):
    size = lax.axis_size(axis)
    return lax.ppermute(values, axis, [(rank, rank ^ bit) for rank in range(size)])


def butterfly_sum(values, axis):
    size = lax.axis_size(axis)
    bit = 1
    while bit < size:
        values = values + exchange(values, axis, bit)
        bit *= 2
    return values


def tie(*values):
    return lax.optimization_barrier(values)


def scatter_small(values, axis):
    size = lax.axis_size(axis)
    rank = lax.axis_index(axis)
    kept = values
    bit = 1
    while bit < size:
        pairs = kept.reshape((kept.shape[0], kept.shape[1] // 2, 2) + kept.shape[2:])
        side = (rank // bit) % 2
        own = lax.dynamic_index_in_dim(pairs, side, axis=2, keepdims=False)
        away = lax.dynamic_index_in_dim(pairs, 1 - side, axis=2, keepdims=False)
        kept = own + exchange(away, axis, bit)
        bit *= 2
    return kept[:, 0]


class WeightGrad:
    def __init__(self, rank, pieces, mats, start=1):
        self.rank, self.pieces, self.mats, self.start = rank, pieces, mats, start
        self.size = lax.axis_size("dp")
        self.tile = pieces[0].shape[1] // self.size
        self.kernel = self.tile % 128 == 0

    def bits(self):
        return [2**i for i in range(self.size.bit_length() - 1)]

    def compute(self, *sides):
        if self.kernel:
            outs = grad_call(self.rank, self.pieces, self.mats, self.start, sides, self.tile)
        else:
            left = jnp.concatenate(self.pieces, axis=0)
            place = jnp.arange(self.size // 2, dtype=jnp.int32)
            bit = self.rank[0] // self.start % 2
            fulls = [
                lax.dot_general(left, jnp.concatenate(mat, axis=0), TN, preferred_element_type=jnp.float32)
                .astype(jnp.bfloat16)
                .reshape(self.size, self.tile, -1)
                for mat in self.mats
            ]
            outs = [
                jnp.take(full, block_at(place, self.start, (bit + side) % 2), axis=0) for side in sides for full in fulls
            ]
        return tuple(outs)


class Halving:
    def __init__(self, rank, own, start=1):
        self.rank, self.kept = rank, own
        self.size = lax.axis_size("dp")
        self.left = [2**i for i in range(self.size.bit_length() - 1) if 2**i != start]

    def merge(self, got, bit):
        low = 2 ** self.left.index(bit)
        self.left.remove(bit)
        if got.shape[1] % 128 == 0:
            away, self.kept = merge_call(self.rank, self.kept, got, low, bit)
            return away
        total = self.kept.astype(jnp.float32) + got.astype(jnp.float32)
        place = jnp.arange(total.shape[0] // 2, dtype=jnp.int32)
        side = self.rank[0] // bit % 2
        self.kept = jnp.take(total, block_at(place, low, side), axis=0)
        return jnp.take(total, block_at(place, low, 1 - side), axis=0).astype(jnp.bfloat16)

    def finish(self, got):
        while self.left:
            bit = self.left[0]
            got = exchange(self.merge(got, bit), "dp", bit)
        return (self.kept.astype(jnp.float32) + got.astype(jnp.float32))[0]


def hop(values, bit):
    return exchange(values, "dp", bit)


def shards(
    hidden_in,
    cotangent,
    gain_attn,
    w_query,
    w_key,
    w_value,
    w_out,
    gain_mlp,
    w_gate,
    w_up,
    w_down,
    doc_lengths,
    doc_groups,
    pad_mask,
):
    rows_local = hidden_in.shape[0]
    rank = lax.axis_index("tensor").astype(jnp.int32)
    rank_ref = rank[None]
    dp_rank = lax.axis_index("dp").astype(jnp.int32)[None]

    def to_far(values):
        return exchange(values, "tensor", 2)

    def to_mate(values):
        return exchange(values, "tensor", 1)

    x_f = hidden_in.astype(jnp.float32)
    inv_a = lax.rsqrt(jnp.mean(x_f * x_f, axis=-1, keepdims=True) + epsilon)
    a0 = (x_f * inv_a * gain_attn).astype(jnp.bfloat16)
    a2 = to_far(a0)
    a1 = to_mate(a0)
    a3 = to_mate(a2)

    inside, low, high, group_tok = row_tables(doc_lengths[0], doc_groups[0], pad_mask[0])
    low, high = low[None], high[None]
    real_tok = pad_mask[0].astype(jnp.float32)
    onehot_g = group_tok[:, None] == jnp.arange(GROUPS, dtype=jnp.int32)[None, :]
    counts = butterfly_sum(jnp.sum(jnp.where(onehot_g, real_tok[:, None], 0.0), axis=0), "dp")
    live = jnp.sum(counts)
    group_scale = jnp.sqrt(live / (GROUPS * jnp.maximum(counts, 1.0)))
    token_weight = real_tok * jnp.sum(jnp.where(onehot_g, group_scale[None, :], 0.0), axis=-1)
    weight_local = lax.dynamic_slice_in_dim(token_weight, rank * rows_local, rows_local)
    c0 = (cotangent.astype(jnp.float32) * weight_local[:, None]).astype(jnp.bfloat16)
    cosine, sine, back_sine = rope_tables(inside)

    near = qkv_pair(0, rank_ref, a0, a1, cosine, sine, w_query, w_key, w_value)
    a2, c0, *near = tie(a2, c0, *near)
    a3 = to_mate(a2)
    c2 = to_far(c0)
    c1 = to_mate(c0)
    far = qkv_pair(2, rank_ref, a2, a3, cosine, sine, w_query, w_key, w_value)
    qs, ks, vs = zip(near, far)
    heads_near, heads_far, lse = attend(rank_ref, qs, ks, vs, low, high)
    y1 = pair_sum([(heads_far, w_out, False)], 0, jnp.bfloat16)
    heads_n, c1, c2, y1 = tie(heads_near, c1, c2, y1)
    got = to_far(y1)
    c3 = to_mate(c2)
    mine = pair_sum([(heads_n, w_out, False)], 1, jnp.float32)
    dm_near = project([((c0, c1), w_down, True)], jnp.float32)
    dm_far = project([((c2, c3), w_down, True)], jnp.float32)
    got, dm_near, dm_far, mine = tie(got, dm_near, dm_far, mine)
    mid_h = x_f + mine + got.astype(jnp.float32)
    inv_b = lax.rsqrt(jnp.mean(mid_h * mid_h, axis=-1, keepdims=True) + epsilon)
    b0 = (mid_h * inv_b * gain_mlp).astype(jnp.bfloat16)
    b2 = to_far(b0)
    b1 = to_mate(b0)
    mid_near, dg_near, du_near = mlp_pair(b0, b1, dm_near, w_gate, w_up)
    mine8 = pair_sum([(mid_near, w_down, False)], 5, jnp.float32)
    b2, mid_near, dg_near, du_near, mine8 = tie(b2, mid_near, dg_near, du_near, mine8)
    b3 = to_mate(b2)
    mid_far, dg_far, du_far = mlp_pair(b2, b3, dm_far, w_gate, w_up)

    half = lax.axis_size("dp") // 2
    b_all, c_all = (b0, b1, b2, b3), (c0, c1, c2, c3)
    grad_down = WeightGrad(dp_rank, c_all, [(mid_near, mid_far)])
    grad_gate = WeightGrad(dp_rank, b_all, [(dg_near, dg_far)], 2)
    (down_send,) = grad_down.compute(1)
    dg_f, du_f, down_send = tie(dg_far, du_far, down_send)
    down_got = hop(down_send, 1)
    (gate_send,) = grad_gate.compute(1)
    gate_got = hop(gate_send, 2)
    y5 = pair_sum([(dg_f, w_gate, True), (du_f, w_up, True)], 2, jnp.bfloat16)
    dg_n, du_n, mid_n, y5 = tie(dg_near, du_near, mid_near, y5)
    got = to_far(y5)
    d_b = pair_sum([(dg_n, w_gate, True), (du_n, w_up, True)], 3, jnp.float32) + got.astype(jnp.float32)
    (up_send,) = WeightGrad(dp_rank, b_all, [(du_n, du_far)]).compute(1)
    (down_own,) = WeightGrad(dp_rank, c_all, [(mid_n, mid_far)]).compute(0)
    d_b, up_send, down_got, down_own = tie(d_b, up_send, down_got, down_own)
    up_got = hop(up_send, 1)
    down = Halving(dp_rank, down_own)
    down_got = hop(down.merge(down_got, 2), 2)

    n_b = mid_h * inv_b
    gain_mlp_part = jnp.sum(d_b * n_b, axis=0)
    e_b = d_b * gain_mlp
    weighted = cotangent.astype(jnp.float32) * weight_local[:, None]
    d_h = weighted + inv_b * (e_b - n_b * jnp.mean(e_b * n_b, axis=-1, keepdims=True))
    t0 = d_h.astype(jnp.bfloat16)
    t0, mid_f, dg_n, du_n = tie(t0, mid_far, dg_near, du_near)
    t2 = to_far(t0)
    t1 = to_mate(t0)
    gs_near = project([((t0, t1), w_out, True)])
    y8 = pair_sum([(mid_f, w_down, False)], 4, jnp.bfloat16)
    (gate_own,) = WeightGrad(dp_rank, b_all, [(dg_n, dg_far)], 2).compute(0)
    t2, gate_got, gs_near, y8, gate_own = tie(t2, gate_got, gs_near, y8, gate_own)

    got8 = to_far(y8)
    gate = Halving(dp_rank, gate_own, 2)
    t3 = to_mate(t2)
    gs_far = project([((t2, t3), w_out, True)])
    gate_got = hop(gate.merge(gate_got, 1), 1)
    (up_own,) = WeightGrad(dp_rank, b_all, [(du_n, du_far)]).compute(0)
    out_send, out_own = WeightGrad(dp_rank, (t0, t1, t2, t3), [(heads_near, heads_far)]).compute(1, 0)
    gs_far, up_got, down_got, up_own, out_send = tie(gs_far, up_got, down_got, up_own, out_send)
    up = Halving(dp_rank, up_own)
    up_got = hop(up.merge(up_got, 2), 2)
    down_got = hop(down.merge(down_got, half), half)
    dqn, dqf, dkn, dkf, dvn, dvf = attend_back(
        rank_ref, qs, ks, vs, (gs_near, gs_far), low, high, lse, cosine, back_sine
    )
    dqf, dkf, dvf, got8, out_send = tie(dqf, dkf, dvf, got8, out_send)

    out_got = hop(out_send, 1)
    y7 = pair_sum([(dqf, w_query, True), (dkf, w_key, True), (dvf, w_value, True)], 6, jnp.bfloat16)
    got = to_far(y7)
    dqn, dkn, dvn, y7, up_got, gate_got, down_got = tie(dqn, dkn, dvn, y7, up_got, gate_got, down_got)
    gate_got = hop(gate.merge(gate_got, half), half)
    up_away = up.merge(up_got, half)
    grad_qkv = WeightGrad(dp_rank, (a0, a1, a2, a3), [(dqn, dqf), (dkn, dkf), (dvn, dvf)])
    *sends, q_own, k_own, v_own = grad_qkv.compute(1, 0)
    d_a = pair_sum([(dqn, w_query, True), (dkn, w_key, True), (dvn, w_value, True)], 7, jnp.float32) + got.astype(jnp.float32)
    d_a, out_got, gate_got, up_away, *sends = tie(d_a, out_got, gate_got, up_away, *sends)

    out = Halving(dp_rank, out_own)
    out_away = out.merge(out_got, 2)
    output = (mid_h + mine8 + got8.astype(jnp.float32)).astype(jnp.bfloat16)
    n_a = x_f * inv_a
    gain_attn_part = jnp.sum(d_a * n_a, axis=0)
    e_a = d_a * gain_attn
    grad_input = d_h + inv_a * (e_a - n_a * jnp.mean(e_a * n_a, axis=-1, keepdims=True))
    gains = jnp.stack([gain_attn_part, gain_mlp_part])
    sum_gate = gate.finish(gate_got)
    if grad_qkv.kernel and half == 4:
        (sum_up, sum_out, *sums), sum_down, gains = last_stages(
            [(up_away, up.kept)],
            [(out_away, out.kept)],
            list(zip(sends, (q_own, k_own, v_own))),
            (down.kept, down_got),
            gains,
        )
        gains = lax.dynamic_slice_in_dim(gains, dp_rank[0] * grad_qkv.tile, grad_qkv.tile, 1)
    else:
        gains = butterfly_sum(scatter_small(gains.reshape(2, lax.axis_size("dp"), -1), "dp"), "tensor")
        sum_up = up.finish(hop(up_away, half))
        sum_out = out.finish(hop(out_away, 2)).T
        sum_down = down.finish(down_got).T
        sums = [Halving(dp_rank, own).finish(hop(send, 1)) for send, own in zip(sends, (q_own, k_own, v_own))]
    return (
        output,
        grad_input,
        gains[0],
        sums[0],
        sums[1],
        sums[2],
        sum_out,
        gains[1],
        sum_gate,
        sum_up,
        sum_down,
    )


def solution(mesh):
    rows, columns, split = P(("dp", "tensor"), None), P(None, "tensor"), P("tensor", None)
    in_specs = (
        rows,
        rows,
        P(),
        columns,
        columns,
        columns,
        split,
        P(),
        columns,
        columns,
        split,
        P("dp", None),
        P("dp", None),
        P("dp", None),
    )
    grads = P("dp", "tensor")
    grads_t = P("tensor", "dp")
    out_specs = (rows, rows, P("dp"), grads, grads, grads, grads_t, P("dp"), grads, grads, grads_t)
    return jax.shard_map(shards, mesh=mesh, in_specs=in_specs, out_specs=out_specs, check_vma=False)
```

```python
import functools

import jax
import jax.numpy as jnp
from jax import lax
from jax.experimental import pallas as pl
from jax.experimental.pallas import tpu as pltpu
from jax.sharding import PartitionSpec as P

HEAD_DIM = 128
ROWS = 1280
DOCS = 3
GROUPS = 8
QTILE = 256

epsilon = 1e-05
masked_score = -1e30
rope_base = 10000.0
COST = 1000


def cost(flops, bytes_accessed, transcendentals):
    return pl.CostEstimate(
        flops=flops // COST, bytes_accessed=bytes_accessed // COST, transcendentals=transcendentals // COST
    )


NT = (((1,), (1,)), ((), ()))
TN = (((0,), (0,)), ((), ()))
NN = (((1,), (0,)), ((), ()))


def mm(left, right, dims=NN):
    return lax.dot_general(left, right, dims, preferred_element_type=jnp.float32)


def whole(shape):
    return pl.BlockSpec(shape, lambda *_: (0,) * len(shape))


def turn(values, cosine, sine):
    return values * cosine + pltpu.roll(values, HEAD_DIM // 2, 1) * sine


def qkv_body(first, rank_ref, xa_ref, xb_ref, cos_ref, sin_ref, wq_ref, wk_ref, wv_ref, q_ref, k_ref, v_ref):
    rows = xa_ref.shape[0]
    for half, x_ref in enumerate((xa_ref, xb_ref)):
        span = pl.ds(half * rows, rows)
        x = x_ref[...]
        place = pl.ds(pl.multiple_of((rank_ref[0] ^ (first + half)) * rows, rows), rows)
        cosine, sine = cos_ref[place, :], sin_ref[place, :]
        for w_ref, out_ref in ((wq_ref, q_ref), (wk_ref, k_ref)):
            full = mm(x, w_ref[...])
            for head in range(full.shape[1] // HEAD_DIM):
                lanes = slice(head * HEAD_DIM, (head + 1) * HEAD_DIM)
                out_ref[span, lanes] = turn(full[:, lanes], cosine, sine).astype(jnp.bfloat16)
        v_ref[span, :] = mm(x, wv_ref[...]).astype(jnp.bfloat16)


def qkv_pair(first, rank, xa, xb, cosine, sine, wq, wk, wv):
    rows, depth = xa.shape
    width = wq.shape[1]
    tile = 256
    wspec = pl.BlockSpec((depth, tile), lambda j, *_: (0, j))
    ospec = pl.BlockSpec((2 * rows, tile), lambda j, *_: (0, j))
    out = jax.ShapeDtypeStruct((2 * rows, width), jnp.bfloat16)
    return pl.pallas_call(
        functools.partial(qkv_body, first),
        grid_spec=pltpu.PrefetchScalarGridSpec(
            num_scalar_prefetch=1,
            grid=(width // tile,),
            in_specs=[whole(xa.shape)] * 2 + [whole(cosine.shape)] * 2 + [wspec] * 3,
            out_specs=[ospec] * 3,
        ),
        out_shape=[out] * 3,
        compiler_params=pltpu.CompilerParams(vmem_limit_bytes=60 << 20),
        cost_estimate=cost(
            flops=12 * rows * depth * width, bytes_accessed=6 * depth * width + 4 * rows * depth, transcendentals=0
        ),
        name="qkv",
    )(rank, xa, xb, cosine, sine, wq, wk, wv)


def in_order(rank_ref, near_ref, far_ref, out_ref):
    piece = near_ref.shape[0] // 2
    for index in range(4):
        src = (near_ref, far_ref)[index // 2]
        at = pl.multiple_of((rank_ref[0] ^ index) * piece, piece)
        out_ref[pl.ds(at, piece), :] = src[pl.ds((index % 2) * piece, piece), :]


def out_of_order(rank_ref, src_ref, near_ref, far_ref):
    piece = near_ref.shape[0] // 2
    for index in range(4):
        dst = (near_ref, far_ref)[index // 2]
        at = pl.multiple_of((rank_ref[0] ^ index) * piece, piece)
        dst[pl.ds((index % 2) * piece, piece), :] = src_ref[pl.ds(at, piece), :].astype(dst.dtype)


def attend_body(rank_ref, qn, qf, kn, kf, vn, vf, low_ref, high_ref, on, of, lse_ref, q_s, k_s, v_s, o_s):
    in_order(rank_ref, qn, qf, q_s)
    in_order(rank_ref, kn, kf, k_s)
    in_order(rank_ref, vn, vf, v_s)
    scale = HEAD_DIM ** (-0.5)
    v_t = v_s[...].T
    for block in range(q_s.shape[0] // QTILE):
        span = pl.ds(block * QTILE, QTILE)
        end = (block + 1) * QTILE
        scores = mm(k_s[:end, :], q_s[span, :], NT)
        at = lax.broadcasted_iota(jnp.int32, scores.shape, 0)
        allowed = (at >= low_ref[:, span]) & (at <= high_ref[:, span])
        scores = jnp.where(allowed, scores * scale, masked_score)
        top = jnp.max(scores, axis=0, keepdims=True)
        prob = jnp.exp(scores - top)
        total = jnp.sum(prob, axis=0, keepdims=True)
        lse_ref[0, :, span] = top + jnp.log(total)
        out_t = mm(v_t[:, :end], prob.astype(jnp.bfloat16)) * (1.0 / total)
        o_s[span, :] = out_t.T
    out_of_order(rank_ref, o_s, on, of)


def attend(rank, qs, ks, vs, low, high):
    half, width = qs[0].shape
    rows = 2 * half
    heads = width // HEAD_DIM
    hspec = pl.BlockSpec((half, HEAD_DIM), lambda h, *_: (0, h))
    row = whole((1, rows))
    return pl.pallas_call(
        attend_body,
        grid_spec=pltpu.PrefetchScalarGridSpec(
            num_scalar_prefetch=1,
            grid=(heads,),
            in_specs=[hspec] * 6 + [row] * 2,
            out_specs=[hspec] * 2 + [pl.BlockSpec((1, 1, rows), lambda h, *_: (h, 0, 0))],
            scratch_shapes=[pltpu.VMEM((rows, HEAD_DIM), jnp.bfloat16)] * 3 + [pltpu.VMEM((rows, HEAD_DIM), jnp.float32)],
        ),
        out_shape=[jax.ShapeDtypeStruct((half, width), jnp.bfloat16)] * 2
        + [jax.ShapeDtypeStruct((heads, 1, rows), jnp.float32)],
        compiler_params=pltpu.CompilerParams(vmem_limit_bytes=60 << 20),
        cost_estimate=cost(
            flops=8 * rows * rows * width, bytes_accessed=8 * rows * width, transcendentals=heads * rows * rows // 2
        ),
        name="attend",
    )(rank, *qs, *ks, *vs, low, high)


def attend_back_body(
    rank_ref, qn, qf, kn, kf, vn, vf, gn, gf, low_ref, high_ref, lse_ref, cos_ref, sin_ref,
    dqn, dqf, dkn, dkf, dvn, dvf, q_s, k_s, v_s, g_s, dq_s, dk_s, dv_s,
):
    in_order(rank_ref, qn, qf, q_s)
    in_order(rank_ref, kn, kf, k_s)
    in_order(rank_ref, vn, vf, v_s)
    in_order(rank_ref, gn, gf, g_s)
    scale = HEAD_DIM ** (-0.5)
    k_t = k_s[...].T
    blocks = q_s.shape[0] // QTILE
    for block in reversed(range(blocks)):
        span = pl.ds(block * QTILE, QTILE)
        end = (block + 1) * QTILE
        query, grad = q_s[span, :], g_s[span, :]
        scores = mm(k_s[:end, :], query, NT) * scale
        at = lax.broadcasted_iota(jnp.int32, scores.shape, 0)
        allowed = (at >= low_ref[:, span]) & (at <= high_ref[:, span])
        prob = jnp.exp(jnp.where(allowed, scores, masked_score) - lse_ref[0, :, span])
        d_prob = mm(v_s[:end, :], grad, NT)
        dot = jnp.sum(prob * d_prob, axis=0, keepdims=True)
        d_score = (prob * (d_prob - dot) * scale).astype(jnp.bfloat16)
        dq_s[span, :] = mm(k_t[:, :end], d_score).T
        d_key = mm(d_score, query)
        d_value = mm(prob.astype(jnp.bfloat16), grad)
        if block == blocks - 1:
            dk_s[...] = d_key
            dv_s[...] = d_value
        else:
            dk_s[:end, :] += d_key
            dv_s[:end, :] += d_value
    dq_s[...] = turn(dq_s[...], cos_ref[...], sin_ref[...])
    dk_s[...] = turn(dk_s[...], cos_ref[...], sin_ref[...])
    out_of_order(rank_ref, dq_s, dqn, dqf)
    out_of_order(rank_ref, dk_s, dkn, dkf)
    out_of_order(rank_ref, dv_s, dvn, dvf)


def attend_back(rank, qs, ks, vs, gs, low, high, lse, cosine, back_sine):
    half, width = qs[0].shape
    rows = 2 * half
    heads = width // HEAD_DIM
    hspec = pl.BlockSpec((half, HEAD_DIM), lambda h, *_: (0, h))
    row = whole((1, rows))
    return pl.pallas_call(
        attend_back_body,
        grid_spec=pltpu.PrefetchScalarGridSpec(
            num_scalar_prefetch=1,
            grid=(heads,),
            in_specs=[hspec] * 8
            + [row] * 2
            + [pl.BlockSpec((1, 1, rows), lambda h, *_: (h, 0, 0))]
            + [whole((rows, HEAD_DIM))] * 2,
            out_specs=[hspec] * 6,
            scratch_shapes=[pltpu.VMEM((rows, HEAD_DIM), jnp.bfloat16)] * 4
            + [pltpu.VMEM((rows, HEAD_DIM), jnp.float32)] * 3,
        ),
        out_shape=[jax.ShapeDtypeStruct((half, width), jnp.bfloat16)] * 6,
        compiler_params=pltpu.CompilerParams(vmem_limit_bytes=60 << 20),
        cost_estimate=cost(
            flops=20 * rows * rows * width, bytes_accessed=16 * rows * width, transcendentals=heads * rows * rows // 2
        ),
        name="attend_back",
    )(rank, *qs, *ks, *vs, *gs, low, high, lse, cosine, back_sine)


def mlp_body(xa_ref, xb_ref, dm_ref, wg_ref, wu_ref, mid_ref, dg_ref, du_ref):
    rows = xa_ref.shape[0]
    for half, x_ref in enumerate((xa_ref, xb_ref)):
        span = pl.ds(half * rows, rows)
        x = x_ref[...]
        gate = mm(x, wg_ref[...])
        up = mm(x, wu_ref[...])
        d_mid = dm_ref[span, :]
        sigma = 1.0 / (1.0 + jnp.exp(-gate))
        active = gate * sigma
        mid_ref[span, :] = (active * up).astype(jnp.bfloat16)
        dg_ref[span, :] = (d_mid * up * sigma * (1.0 + gate * (1.0 - sigma))).astype(jnp.bfloat16)
        du_ref[span, :] = (d_mid * active).astype(jnp.bfloat16)


def mlp_pair(xa, xb, d_mid, wg, wu):
    rows, depth = xa.shape
    width = wg.shape[1]
    tile = 256
    wspec = pl.BlockSpec((depth, tile), lambda j: (0, j))
    ospec = pl.BlockSpec((2 * rows, tile), lambda j: (0, j))
    return pl.pallas_call(
        mlp_body,
        grid=(pl.cdiv(width, tile),),
        in_specs=[whole(xa.shape)] * 2 + [ospec] + [wspec] * 2,
        out_specs=[ospec] * 3,
        out_shape=[jax.ShapeDtypeStruct((2 * rows, width), jnp.bfloat16)] * 3,
        compiler_params=pltpu.CompilerParams(vmem_limit_bytes=60 << 20),
        cost_estimate=cost(
            flops=8 * rows * depth * width,
            bytes_accessed=4 * depth * width + 4 * rows * depth + 20 * rows * width,
            transcendentals=2 * rows * width,
        ),
        name="mlp",
    )(xa, xb, d_mid, wg, wu)


def gather_rows(parts, out_ref):
    at = 0
    for part in parts:
        out_ref[at : at + part.shape[0], :] = part[...]
        at += part.shape[0]


def gather_sides(rights, out_ref):
    at = 0
    for near, far in zip(rights[::2], rights[1::2]):
        rows, width = near.shape
        out_ref[:rows, at : at + width] = near[...]
        out_ref[rows:, at : at + width] = far[...]
        at += width


def block_at(place, low, side):
    return place // low * (2 * low) + place % low + low * side


def filled(step, low, side):
    group, half = step // (2 * low), step // low % 2
    here = jnp.where(half == side, step % low, jnp.where(half > side, low - 1, -1))
    return jnp.maximum(group * low + here, 0)


def grad_body(pieces, widths, low, sides, rank_ref, *refs):
    left, rights = refs[:pieces], refs[pieces : pieces + 2 * len(widths)]
    outs, (left_s, right_s) = refs[pieces + 2 * len(widths) : -2], refs[-2:]
    step = pl.program_id(0)

    @pl.when(step == 0)
    def _():
        gather_sides(rights, right_s)

    gather_rows(left, left_s)
    total = mm(left_s[...], right_s[...], TN).astype(jnp.bfloat16)

    def store(refs):
        at = 0
        for ref, width in zip(refs, widths):
            ref[0] = total[:, at : at + width]
            at += width

    if len(sides) == 1:
        store(outs)
    else:
        sent = step // low % 2 != rank_ref[0] // low % 2
        pl.when(sent)(lambda: store(outs[: len(widths)]))
        pl.when(jnp.logical_not(sent))(lambda: store(outs[len(widths) :]))


def grad_call(rank, pieces, mats, low, sides, tile):
    rows, depth = pieces[0].shape[0] * len(pieces), pieces[0].shape[1]
    widths = [near.shape[1] for near, _ in mats]
    width, half = sum(widths), depth // tile // 2
    count = half * len(sides)

    def own(s, side):
        bit = s[0] // low % 2
        return 1 - bit if side else bit

    if len(sides) == 1:
        lspec = pl.BlockSpec((pieces[0].shape[0], tile), lambda j, s: (0, block_at(j, low, own(s, sides[0]))))
    else:
        lspec = pl.BlockSpec((pieces[0].shape[0], tile), lambda j, s: (0, j))
    out_specs = []
    for side in sides:
        for w in widths:
            if len(sides) == 1:
                out_specs.append(pl.BlockSpec((1, tile, w), lambda j, s: (j, 0, 0)))
            else:
                out_specs.append(pl.BlockSpec((1, tile, w), lambda j, s, side=side: (filled(j, low, own(s, side)), 0, 0)))
    rights = [part for mat in mats for part in mat]
    return pl.pallas_call(
        functools.partial(grad_body, len(pieces), widths, low, sides),
        grid_spec=pltpu.PrefetchScalarGridSpec(
            num_scalar_prefetch=1,
            grid=(count,),
            in_specs=[lspec] * len(pieces) + [whole(r.shape) for r in rights],
            out_specs=out_specs,
            scratch_shapes=[pltpu.VMEM((rows, tile), jnp.bfloat16), pltpu.VMEM((rows, width), jnp.bfloat16)],
        ),
        out_shape=[jax.ShapeDtypeStruct((half, tile, w), jnp.bfloat16) for _ in sides for w in widths],
        compiler_params=pltpu.CompilerParams(vmem_limit_bytes=60 << 20),
        cost_estimate=cost(
            flops=2 * rows * tile * count * width,
            bytes_accessed=2 * rows * (tile * count + width) + 2 * tile * count * width,
            transcendentals=0,
        ),
        name="weight_grad",
    )(rank, *pieces, *rights)


def merge_body(_, own_away, got_away, own_kept, got_kept, away_ref, kept_ref):
    away_ref[...] = (own_away[...].astype(jnp.float32) + got_away[...].astype(jnp.float32)).astype(jnp.bfloat16)
    kept_ref[...] = (own_kept[...].astype(jnp.float32) + got_kept[...].astype(jnp.float32)).astype(jnp.bfloat16)


def merge_call(rank, own, got, low, bit):
    count, tile, width = own.shape
    away, kept = (
        pl.BlockSpec((1, tile, width), lambda j, s, flip=flip: (block_at(j, low, (s[0] // bit + flip) % 2), 0, 0))
        for flip in (1, 0)
    )
    ospec = pl.BlockSpec((1, tile, width), lambda j, s: (j, 0, 0))
    return pl.pallas_call(
        merge_body,
        grid_spec=pltpu.PrefetchScalarGridSpec(
            num_scalar_prefetch=1,
            grid=(count // 2,),
            in_specs=[away, away, kept, kept],
            out_specs=[ospec] * 2,
        ),
        out_shape=[jax.ShapeDtypeStruct((count // 2, tile, width), jnp.bfloat16)] * 2,
        compiler_params=pltpu.CompilerParams(vmem_limit_bytes=40 << 20),
        cost_estimate=cost(flops=count * tile * width, bytes_accessed=6 * count * tile * width, transcendentals=0),
        name="merge",
    )(rank, own, got, own, got)


def product(lefts, weights, half, rows):
    total = None
    for left, (w_ref, dims) in zip(lefts, weights):
        value = mm(left[half][...] if len(left) == 2 else left[0][pl.ds(half * rows, rows), :], w_ref[...], dims)
        total = value if total is None else total + value
    return total


def project_body(terms, *refs):
    at, lefts, weights = 0, [], []
    for pieces, dims in terms:
        lefts.append(refs[at : at + pieces])
        weights.append((refs[at + pieces], dims))
        at += pieces + 1
    out_ref = refs[at]
    rows = out_ref.shape[0] // 2
    for half in range(2):
        span = pl.ds(half * rows, rows)
        out_ref[span, :] = product(lefts, weights, half, rows).astype(out_ref.dtype)


def terms_of(terms):
    return [(left if isinstance(left, tuple) else (left,), w, NT if flip else NN) for left, w, flip in terms]


def term_specs(terms, tile):
    in_specs, args = [], []
    for left, w, dims in terms:
        depth = left[0].shape[1]
        in_specs += [whole(piece.shape) for piece in left]
        in_specs.append(
            pl.BlockSpec((tile, depth), lambda j: (j, 0)) if dims is NT else pl.BlockSpec((depth, tile), lambda j: (0, j))
        )
        args += [*left, w]
    return in_specs, args


def project(terms, dtype=jnp.bfloat16):
    terms = terms_of(terms)
    rows = sum(piece.shape[0] for piece in terms[0][0])
    width = terms[0][1].shape[0 if terms[0][2] is NT else 1]
    tile = min(512, width)
    in_specs, args = term_specs(terms, tile)
    return pl.pallas_call(
        functools.partial(project_body, [(len(left), dims) for left, _, dims in terms]),
        grid=(pl.cdiv(width, tile),),
        in_specs=in_specs,
        out_specs=pl.BlockSpec((rows, tile), lambda j: (0, j)),
        out_shape=jax.ShapeDtypeStruct((rows, width), dtype),
        compiler_params=pltpu.CompilerParams(vmem_limit_bytes=60 << 20),
        cost_estimate=cost(
            flops=2 * rows * width * sum(left[0].shape[1] for left, _, _ in terms),
            bytes_accessed=sum(2 * a.size for a in args) + 2 * rows * width,
            transcendentals=0,
        ),
        name="project",
    )(*args)


def pair_body(terms, steps, *refs):
    at, lefts, weights = 0, [], []
    for pieces, dims in terms:
        lefts.append(refs[at : at + pieces])
        weights.append((refs[at + pieces], dims))
        at += pieces + 1
    out_ref, mine_s, away_s, got_s, send_sem, recv_sem = refs[at:]
    rows = out_ref.shape[0]
    tile = mine_s.shape[2]
    step = pl.program_id(0)
    me = lax.axis_index("tensor")
    mate = {"tensor": me + 1 - 2 * (me % 2)}

    @pl.when(step == 0)
    def _():
        barrier = pltpu.get_barrier_semaphore()
        pl.semaphore_signal(barrier, inc=1, device_id=mate, device_id_type=pl.DeviceIdType.MESH)
        pl.semaphore_wait(barrier, 1)

    def copy(index):
        return pltpu.make_async_remote_copy(
            src_ref=away_s.at[index],
            dst_ref=got_s.at[index],
            send_sem=send_sem.at[index],
            recv_sem=recv_sem.at[index],
            device_id=mate,
            device_id_type=pl.DeviceIdType.MESH,
        )

    away_s[step] = product(lefts, weights, 1, rows).astype(jnp.bfloat16)
    copy(step).start()
    mine_s[step] = product(lefts, weights, 0, rows)

    @pl.when(step == steps - 1)
    def _():
        for index in range(steps):
            copy(index).wait()
            total = mine_s[index] + got_s[index].astype(jnp.float32)
            out_ref[:, index * tile : (index + 1) * tile] = total.astype(out_ref.dtype)


def pair_sum(terms, ident, dtype):
    terms = terms_of(terms)
    rows = sum(piece.shape[0] for piece in terms[0][0]) // 2
    width = terms[0][1].shape[0 if terms[0][2] is NT else 1]
    tile = min(512, width)
    steps = width // tile
    in_specs, args = term_specs(terms, tile)
    return pl.pallas_call(
        functools.partial(pair_body, [(len(left), dims) for left, _, dims in terms], steps),
        grid=(steps,),
        in_specs=in_specs,
        out_specs=whole((rows, width)),
        out_shape=jax.ShapeDtypeStruct((rows, width), dtype),
        scratch_shapes=[
            pltpu.VMEM((steps, rows, tile), jnp.float32),
            pltpu.VMEM((steps, rows, tile), jnp.bfloat16),
            pltpu.VMEM((steps, rows, tile), jnp.bfloat16),
            pltpu.SemaphoreType.DMA((steps,)),
            pltpu.SemaphoreType.DMA((steps,)),
        ],
        compiler_params=pltpu.CompilerParams(vmem_limit_bytes=60 << 20, collective_id=ident),
        cost_estimate=cost(
            flops=4 * rows * width * sum(left[0].shape[1] for left, _, _ in terms),
            bytes_accessed=sum(2 * a.size for a in args) + 4 * rows * width,
            transcendentals=0,
        ),
        name="pair_sum",
    )(*args)


def partner(axis, bit):
    rank = lax.axis_index(axis)
    return {axis: rank + bit - 2 * bit * (rank // bit % 2)}


def last_body(flips, twos, threes, *refs):
    ones = len(flips)
    mats = ones + twos + threes
    away, kept, refs = refs[:mats], refs[mats : 2 * mats], refs[2 * mats :]
    ready_ref, got_ref, gains_ref, refs = refs[0], refs[1], refs[2], refs[3:]
    outs, done_ref, sums_ref, refs = refs[:mats], refs[mats], refs[mats + 1], refs[mats + 2 :]
    own, first, refs = refs[:mats], refs[mats : 2 * mats], refs[2 * mats :]
    held, to_z, from_z, refs = refs[:threes], refs[threes : 2 * threes], refs[2 * threes : 3 * threes], refs[3 * threes :]
    late = twos + threes
    to_last, from_last, refs = refs[:late], refs[late : 2 * late], refs[2 * late :]
    gain_in, gain_out, load_sem, send_sem, recv_sem = refs
    rank = lax.axis_index("dp")
    z1, z2 = rank // 2 % 2, rank // 4 % 2
    hops = [("tensor", 1), ("tensor", 2), ("dp", 1), ("dp", 2), ("dp", 4)]
    copies = []

    barrier = pltpu.get_barrier_semaphore()
    for axis, bit in hops:
        pl.semaphore_signal(barrier, inc=1, device_id=partner(axis, bit), device_id_type=pl.DeviceIdType.MESH)
    pl.semaphore_wait(barrier, len(hops))

    def send(src, dst, axis, bit):
        index = len(copies)
        copy = pltpu.make_async_remote_copy(
            src_ref=src,
            dst_ref=dst,
            send_sem=send_sem.at[index],
            recv_sem=recv_sem.at[index],
            device_id=partner(axis, bit),
            device_id_type=pl.DeviceIdType.MESH,
        )
        copy.start()
        copies.append(copy)
        return copy

    def side(bit, flip):
        return 1 - bit if flip else bit

    stage = {}
    gain_out[0] = gains_ref[...]
    stage["gains"] = send(gain_out.at[0], gain_in.at[0], *hops[0])

    def gain_hop(index):
        stage["gains"].wait_recv()
        total = gain_out[index] + gain_in[index]
        if index + 1 < len(hops):
            gain_out[index + 1] = total
            stage["gains"] = send(gain_out.at[index + 1], gain_in.at[index + 1], *hops[index + 1])
        else:
            sums_ref[...] = total

    for m in range(ones, ones + twos):
        for c in (1, 0):
            stage[m, "z", c] = send(away[m].at[side(z2, c)], first[m].at[c], "dp", 2)
    for m in reversed(range(ones)):
        stage[m, "last"] = send(away[m], first[m], "dp", 4)

    def send_all(m):
        for a in (1, 0):
            for c in (1, 0):
                stage[m, a, c] = send(away[m].at[side(z1, a) + 2 * side(z2, c)], first[m].at[2 * a + c], "dp", 1)

    loads = [pltpu.make_async_copy(kept[m], own[m], load_sem.at[m]) for m in range(mats)]
    for load in loads:
        load.start()
    send_all(ones + twos)
    gain_hop(0)
    gain_hop(1)
    for m in range(ones + twos + 1, mats):
        send_all(m)
    for load in loads:
        load.wait()

    def wide(value):
        return value.astype(jnp.float32)

    def from_x(m, a, c):
        stage[m, a, c].wait_recv()
        total = wide(own[m][side(z1, a) + 2 * side(z2, c)]) + wide(first[m][2 * a + c])
        i = m - ones - twos
        if a:
            to_z[i][c] = total.astype(jnp.bfloat16)
            stage[m, "z", c] = send(to_z[i].at[c], from_z[i].at[c], "dp", 2)
        else:
            held[i][c] = total

    def from_near(m, c):
        stage[m, "z", c].wait_recv()
        if m < ones + twos:
            total = wide(own[m][side(z2, c)]) + wide(first[m][c])
        else:
            total = held[m - ones - twos][c] + wide(from_z[m - ones - twos][c])
        if c:
            to_last[m - ones][...] = total.astype(jnp.bfloat16)
            stage[m, "last"] = send(to_last[m - ones], from_last[m - ones], "dp", 4)
        else:
            outs[m][...] = total

    def finish(m):
        stage[m, "last"].wait_recv()
        if m < ones:
            total = wide(own[m][0]) + wide(first[m][0])
            outs[m][...] = total.T if flips[m] else total
        else:
            outs[m][...] += wide(from_last[m - ones][...])

    up, out, q, k, v = range(5)
    done_ref[...] = (wide(ready_ref[0]) + wide(got_ref[0])).T
    from_near(q, 1)
    from_x(k, 1, 1)
    from_x(k, 1, 0)
    from_near(q, 0)
    from_x(k, 0, 1)
    from_x(k, 0, 0)
    gain_hop(2)
    finish(out)
    from_x(v, 1, 1)
    from_near(k, 1)
    from_x(v, 1, 0)
    from_near(k, 0)
    from_x(v, 0, 1)
    from_x(v, 0, 0)
    finish(up)
    gain_hop(3)
    from_near(v, 1)
    from_near(v, 0)
    finish(q)
    gain_hop(4)
    finish(k)
    finish(v)
    for copy in copies:
        copy.wait_send()


def last_stages(ones, twos, threes, ready, gains):
    mats = [*ones, *twos, *threes]
    away, kept = [m[0] for m in mats], [m[1] for m in mats]
    shapes = [a.shape for a in away]
    low, wide = jnp.bfloat16, jnp.float32
    late, last = shapes[len(ones) + len(twos) :], shapes[len(ones) :]
    flat = [shape[1:] for shape in shapes]
    flat = [shape[::-1] if m < len(ones) and ones[m][2] else shape for m, shape in enumerate(flat)]
    any_space = pl.BlockSpec(memory_space=pl.ANY)
    inside = pl.BlockSpec(memory_space=pltpu.VMEM)
    count = len(ones) + 3 * len(twos) + 7 * len(threes) + 5
    result = pl.pallas_call(
        functools.partial(last_body, [m[2] for m in ones], len(twos), len(threes)),
        in_specs=[any_space] * (2 * len(mats)) + [inside] * 3,
        out_specs=[inside] * (len(mats) + 2),
        out_shape=[jax.ShapeDtypeStruct(shape, wide) for shape in flat]
        + [jax.ShapeDtypeStruct(ready[0].shape[:0:-1], wide), jax.ShapeDtypeStruct(gains.shape, wide)],
        scratch_shapes=[pltpu.VMEM(shape, low) for shape in shapes]
        + [pltpu.VMEM(shape, low) for shape in shapes]
        + [pltpu.VMEM((2,) + shape[1:], wide) for shape in late]
        + [pltpu.VMEM((2,) + shape[1:], low) for shape in late]
        + [pltpu.VMEM((2,) + shape[1:], low) for shape in late]
        + [pltpu.VMEM(shape[1:], low) for shape in last]
        + [pltpu.VMEM(shape[1:], low) for shape in last]
        + [pltpu.VMEM((5,) + gains.shape, wide)] * 2
        + [pltpu.SemaphoreType.DMA((len(mats),)), pltpu.SemaphoreType.DMA((count,)), pltpu.SemaphoreType.DMA((count,))],
        compiler_params=pltpu.CompilerParams(vmem_limit_bytes=62 << 20, collective_id=8),
        cost_estimate=cost(flops=1 << 24, bytes_accessed=1 << 25, transcendentals=0),
        name="last_stages",
    )(*away, *kept, *ready, gains)
    return result[:-2], result[-2], result[-1]


def row_tables(length_row, group_row, mask_row):
    starts = jnp.cumsum(length_row) - length_row
    token = jnp.arange(ROWS, dtype=jnp.int32)
    doc_index = jnp.sum((token[:, None] >= starts[None, 1:]).astype(jnp.int32), axis=1)
    onehot = doc_index[:, None] == jnp.arange(DOCS, dtype=jnp.int32)[None, :]
    first = jnp.sum(jnp.where(onehot, starts[None, :], 0), axis=1)
    group_tok = jnp.sum(jnp.where(onehot, group_row[None, :], 0), axis=1)
    real = jnp.sum(jnp.where(onehot, mask_row[:, None], 0), axis=0)
    last_real = first + jnp.sum(jnp.where(onehot, real[None, :], 0), axis=1) - 1
    return (token - first, first, jnp.minimum(token, last_real), group_tok)


def rope_tables(inside):
    freq = rope_base ** (-jnp.arange(0, HEAD_DIM // 2, dtype=jnp.float32) * 2.0 / HEAD_DIM)
    angle = inside.astype(jnp.float32)[:, None] * freq[None, :]
    cosine, sine = jnp.cos(angle), jnp.sin(angle)
    return (
        jnp.concatenate([cosine, cosine], axis=-1),
        jnp.concatenate([-sine, sine], axis=-1),
        jnp.concatenate([sine, -sine], axis=-1),
    )


def rows_dot(left, right):
    return jnp.dot(left, right, preferred_element_type=jnp.float32)


def rows_dot_t(left, right):
    return lax.dot_general(left, right, NT, preferred_element_type=jnp.float32)


def exchange(values, axis, bit):
    size = lax.axis_size(axis)
    return lax.ppermute(values, axis, [(rank, rank ^ bit) for rank in range(size)])


def butterfly_sum(values, axis):
    size = lax.axis_size(axis)
    bit = 1
    while bit < size:
        values = values + exchange(values, axis, bit)
        bit *= 2
    return values


def tie(*values):
    return lax.optimization_barrier(values)


def scatter_small(values, axis):
    size = lax.axis_size(axis)
    rank = lax.axis_index(axis)
    kept = values
    bit = 1
    while bit < size:
        pairs = kept.reshape((kept.shape[0], kept.shape[1] // 2, 2) + kept.shape[2:])
        side = (rank // bit) % 2
        own = lax.dynamic_index_in_dim(pairs, side, axis=2, keepdims=False)
        away = lax.dynamic_index_in_dim(pairs, 1 - side, axis=2, keepdims=False)
        kept = own + exchange(away, axis, bit)
        bit *= 2
    return kept[:, 0]


class WeightGrad:
    def __init__(self, rank, pieces, mats, start=1):
        self.rank, self.pieces, self.mats, self.start = rank, pieces, mats, start
        self.size = lax.axis_size("dp")
        self.tile = pieces[0].shape[1] // self.size
        self.kernel = self.tile % 128 == 0

    def bits(self):
        return [2**i for i in range(self.size.bit_length() - 1)]

    def compute(self, *sides):
        if self.kernel:
            outs = grad_call(self.rank, self.pieces, self.mats, self.start, sides, self.tile)
        else:
            left = jnp.concatenate(self.pieces, axis=0)
            place = jnp.arange(self.size // 2, dtype=jnp.int32)
            bit = self.rank[0] // self.start % 2
            fulls = [
                lax.dot_general(left, jnp.concatenate(mat, axis=0), TN, preferred_element_type=jnp.float32)
                .astype(jnp.bfloat16)
                .reshape(self.size, self.tile, -1)
                for mat in self.mats
            ]
            outs = [
                jnp.take(full, block_at(place, self.start, (bit + side) % 2), axis=0) for side in sides for full in fulls
            ]
        return tuple(outs)


class Halving:
    def __init__(self, rank, own, start=1):
        self.rank, self.kept = rank, own
        self.size = lax.axis_size("dp")
        self.left = [2**i for i in range(self.size.bit_length() - 1) if 2**i != start]

    def merge(self, got, bit):
        low = 2 ** self.left.index(bit)
        self.left.remove(bit)
        if got.shape[1] % 128 == 0:
            away, self.kept = merge_call(self.rank, self.kept, got, low, bit)
            return away
        total = self.kept.astype(jnp.float32) + got.astype(jnp.float32)
        place = jnp.arange(total.shape[0] // 2, dtype=jnp.int32)
        side = self.rank[0] // bit % 2
        self.kept = jnp.take(total, block_at(place, low, side), axis=0)
        return jnp.take(total, block_at(place, low, 1 - side), axis=0).astype(jnp.bfloat16)

    def finish(self, got):
        while self.left:
            bit = self.left[0]
            got = exchange(self.merge(got, bit), "dp", bit)
        return (self.kept.astype(jnp.float32) + got.astype(jnp.float32))[0]


def hop(values, bit):
    return exchange(values, "dp", bit)


def shards(
    hidden_in,
    cotangent,
    gain_attn,
    w_query,
    w_key,
    w_value,
    w_out,
    gain_mlp,
    w_gate,
    w_up,
    w_down,
    doc_lengths,
    doc_groups,
    pad_mask,
):
    rows_local = hidden_in.shape[0]
    rank = lax.axis_index("tensor").astype(jnp.int32)
    rank_ref = rank[None]
    dp_rank = lax.axis_index("dp").astype(jnp.int32)[None]

    def to_far(values):
        return exchange(values, "tensor", 2)

    def to_mate(values):
        return exchange(values, "tensor", 1)

    x_f = hidden_in.astype(jnp.float32)
    inv_a = lax.rsqrt(jnp.mean(x_f * x_f, axis=-1, keepdims=True) + epsilon)
    a0 = (x_f * inv_a * gain_attn).astype(jnp.bfloat16)
    a2 = to_far(a0)
    a1 = to_mate(a0)
    a3 = to_mate(a2)

    inside, low, high, group_tok = row_tables(doc_lengths[0], doc_groups[0], pad_mask[0])
    low, high = low[None], high[None]
    real_tok = pad_mask[0].astype(jnp.float32)
    onehot_g = group_tok[:, None] == jnp.arange(GROUPS, dtype=jnp.int32)[None, :]
    counts = butterfly_sum(jnp.sum(jnp.where(onehot_g, real_tok[:, None], 0.0), axis=0), "dp")
    live = jnp.sum(counts)
    group_scale = jnp.sqrt(live / (GROUPS * jnp.maximum(counts, 1.0)))
    token_weight = real_tok * jnp.sum(jnp.where(onehot_g, group_scale[None, :], 0.0), axis=-1)
    weight_local = lax.dynamic_slice_in_dim(token_weight, rank * rows_local, rows_local)
    c0 = (cotangent.astype(jnp.float32) * weight_local[:, None]).astype(jnp.bfloat16)
    cosine, sine, back_sine = rope_tables(inside)

    near = qkv_pair(0, rank_ref, a0, a1, cosine, sine, w_query, w_key, w_value)
    a2, c0, *near = tie(a2, c0, *near)
    a3 = to_mate(a2)
    c2 = to_far(c0)
    c1 = to_mate(c0)
    far = qkv_pair(2, rank_ref, a2, a3, cosine, sine, w_query, w_key, w_value)
    qs, ks, vs = zip(near, far)
    heads_near, heads_far, lse = attend(rank_ref, qs, ks, vs, low, high)
    y1 = pair_sum([(heads_far, w_out, False)], 0, jnp.bfloat16)
    heads_n, c1, c2, y1 = tie(heads_near, c1, c2, y1)
    got = to_far(y1)
    c3 = to_mate(c2)
    mine = pair_sum([(heads_n, w_out, False)], 1, jnp.float32)
    dm_near = project([((c0, c1), w_down, True)], jnp.float32)
    dm_far = project([((c2, c3), w_down, True)], jnp.float32)
    got, dm_near, dm_far, mine = tie(got, dm_near, dm_far, mine)
    mid_h = x_f + mine + got.astype(jnp.float32)
    inv_b = lax.rsqrt(jnp.mean(mid_h * mid_h, axis=-1, keepdims=True) + epsilon)
    b0 = (mid_h * inv_b * gain_mlp).astype(jnp.bfloat16)
    b2 = to_far(b0)
    b1 = to_mate(b0)
    mid_near, dg_near, du_near = mlp_pair(b0, b1, dm_near, w_gate, w_up)
    mine8 = pair_sum([(mid_near, w_down, False)], 5, jnp.float32)
    b2, mid_near, dg_near, du_near, mine8 = tie(b2, mid_near, dg_near, du_near, mine8)
    b3 = to_mate(b2)
    mid_far, dg_far, du_far = mlp_pair(b2, b3, dm_far, w_gate, w_up)

    half = lax.axis_size("dp") // 2
    b_all, c_all = (b0, b1, b2, b3), (c0, c1, c2, c3)
    grad_down = WeightGrad(dp_rank, c_all, [(mid_near, mid_far)])
    grad_gate = WeightGrad(dp_rank, b_all, [(dg_near, dg_far)], 2)
    (down_send,) = grad_down.compute(1)
    dg_f, du_f, down_send = tie(dg_far, du_far, down_send)
    down_got = hop(down_send, 1)
    (gate_send,) = grad_gate.compute(1)
    gate_got = hop(gate_send, 2)
    y5 = pair_sum([(dg_f, w_gate, True), (du_f, w_up, True)], 2, jnp.bfloat16)
    dg_n, du_n, mid_n, y5 = tie(dg_near, du_near, mid_near, y5)
    got = to_far(y5)
    d_b = pair_sum([(dg_n, w_gate, True), (du_n, w_up, True)], 3, jnp.float32) + got.astype(jnp.float32)
    (up_send,) = WeightGrad(dp_rank, b_all, [(du_n, du_far)]).compute(1)
    (down_own,) = WeightGrad(dp_rank, c_all, [(mid_n, mid_far)]).compute(0)
    d_b, up_send, down_got, down_own = tie(d_b, up_send, down_got, down_own)
    up_got = hop(up_send, 1)
    down = Halving(dp_rank, down_own)
    down_got = hop(down.merge(down_got, 2), 2)

    n_b = mid_h * inv_b
    gain_mlp_part = jnp.sum(d_b * n_b, axis=0)
    e_b = d_b * gain_mlp
    weighted = cotangent.astype(jnp.float32) * weight_local[:, None]
    d_h = weighted + inv_b * (e_b - n_b * jnp.mean(e_b * n_b, axis=-1, keepdims=True))
    t0 = d_h.astype(jnp.bfloat16)
    t0, mid_f, dg_n, du_n = tie(t0, mid_far, dg_near, du_near)
    t2 = to_far(t0)
    t1 = to_mate(t0)
    gs_near = project([((t0, t1), w_out, True)])
    y8 = pair_sum([(mid_f, w_down, False)], 4, jnp.bfloat16)
    (gate_own,) = WeightGrad(dp_rank, b_all, [(dg_n, dg_far)], 2).compute(0)
    t2, gate_got, gs_near, y8, gate_own = tie(t2, gate_got, gs_near, y8, gate_own)

    got8 = to_far(y8)
    gate = Halving(dp_rank, gate_own, 2)
    t3 = to_mate(t2)
    gs_far = project([((t2, t3), w_out, True)])
    gate_got = hop(gate.merge(gate_got, 1), 1)
    (up_own,) = WeightGrad(dp_rank, b_all, [(du_n, du_far)]).compute(0)
    out_send, out_own = WeightGrad(dp_rank, (t0, t1, t2, t3), [(heads_near, heads_far)]).compute(1, 0)
    gs_far, up_got, down_got, up_own, out_send = tie(gs_far, up_got, down_got, up_own, out_send)
    up = Halving(dp_rank, up_own)
    up_got = hop(up.merge(up_got, 2), 2)
    down_got = hop(down.merge(down_got, half), half)
    dqn, dqf, dkn, dkf, dvn, dvf = attend_back(
        rank_ref, qs, ks, vs, (gs_near, gs_far), low, high, lse, cosine, back_sine
    )
    dqf, dkf, dvf, got8, out_send = tie(dqf, dkf, dvf, got8, out_send)

    out_got = hop(out_send, 1)
    grad_qkv = WeightGrad(dp_rank, (a0, a1, a2, a3), [(dqn, dqf), (dkn, dkf), (dvn, dvf)])
    *sends, q_own, k_own, v_own = grad_qkv.compute(1, 0)
    dqf, dkf, dvf, down_got, *sends = tie(dqf, dkf, dvf, down_got, *sends)
    q_got = hop(sends[0], 1)
    y7 = pair_sum([(dqf, w_query, True), (dkf, w_key, True), (dvf, w_value, True)], 6, jnp.bfloat16)
    got = to_far(y7)
    dqn, dkn, dvn, y7, up_got, gate_got, out_got = tie(dqn, dkn, dvn, y7, up_got, gate_got, out_got)
    out = Halving(dp_rank, out_own)
    out_got = hop(out.merge(out_got, 2), 2)
    gate_got = hop(gate.merge(gate_got, half), half)
    up_away = up.merge(up_got, half)
    d_a = pair_sum([(dqn, w_query, True), (dkn, w_key, True), (dvn, w_value, True)], 7, jnp.float32) + got.astype(jnp.float32)
    d_a, out_got, gate_got, q_got, up_away = tie(d_a, out_got, gate_got, q_got, up_away)

    q = Halving(dp_rank, q_own)
    q_away, out_away = q.merge(q_got, 2), out.merge(out_got, half)
    output = (mid_h + mine8 + got8.astype(jnp.float32)).astype(jnp.bfloat16)
    n_a = x_f * inv_a
    gain_attn_part = jnp.sum(d_a * n_a, axis=0)
    e_a = d_a * gain_attn
    grad_input = d_h + inv_a * (e_a - n_a * jnp.mean(e_a * n_a, axis=-1, keepdims=True))
    gains = jnp.stack([gain_attn_part, gain_mlp_part])
    sum_gate = gate.finish(gate_got)
    if grad_qkv.kernel and half == 4:
        (sum_up, sum_out, *sums), sum_down, gains = last_stages(
            [(up_away, up.kept, False), (out_away, out.kept, True)],
            [(q_away, q.kept)],
            [(sends[1], k_own), (sends[2], v_own)],
            (down.kept, down_got),
            gains,
        )
        gains = lax.dynamic_slice_in_dim(gains, dp_rank[0] * grad_qkv.tile, grad_qkv.tile, 1)
    else:
        gains = butterfly_sum(scatter_small(gains.reshape(2, lax.axis_size("dp"), -1), "dp"), "tensor")
        sum_up = up.finish(hop(up_away, half))
        sum_out = out.finish(hop(out_away, half)).T
        sum_down = down.finish(down_got).T
        sums = [q.finish(hop(q_away, 2))]
        sums += [Halving(dp_rank, own).finish(hop(send, 1)) for send, own in zip(sends[1:], (k_own, v_own))]
    return (
        output,
        grad_input,
        gains[0],
        sums[0],
        sums[1],
        sums[2],
        sum_out,
        gains[1],
        sum_gate,
        sum_up,
        sum_down,
    )


def solution(mesh):
    rows, columns, split = P(("dp", "tensor"), None), P(None, "tensor"), P("tensor", None)
    in_specs = (
        rows,
        rows,
        P(),
        columns,
        columns,
        columns,
        split,
        P(),
        columns,
        columns,
        split,
        P("dp", None),
        P("dp", None),
        P("dp", None),
    )
    grads = P("dp", "tensor")
    grads_t = P("tensor", "dp")
    out_specs = (rows, rows, P("dp"), grads, grads, grads, grads_t, P("dp"), grads, grads, grads_t)
    return jax.shard_map(shards, mesh=mesh, in_specs=in_specs, out_specs=out_specs, check_vma=False)
```

```python
import functools

import jax
import jax.numpy as jnp
from jax import lax
from jax.experimental import pallas as pl
from jax.experimental.pallas import tpu as pltpu
from jax.sharding import PartitionSpec as P

HEAD_DIM = 128
ROWS = 1280
DOCS = 3
GROUPS = 8
QTILE = 256

epsilon = 1e-05
masked_score = -1e30
rope_base = 10000.0
COST = 1000


def cost(flops, bytes_accessed, transcendentals):
    return pl.CostEstimate(
        flops=flops // COST, bytes_accessed=bytes_accessed // COST, transcendentals=transcendentals // COST
    )


NT = (((1,), (1,)), ((), ()))
TN = (((0,), (0,)), ((), ()))
NN = (((1,), (0,)), ((), ()))


def mm(left, right, dims=NN):
    return lax.dot_general(left, right, dims, preferred_element_type=jnp.float32)


def whole(shape):
    return pl.BlockSpec(shape, lambda *_: (0,) * len(shape))


def turn(values, cosine, sine):
    return values * cosine + pltpu.roll(values, HEAD_DIM // 2, 1) * sine


def qkv_body(first, rank_ref, xa_ref, xb_ref, cos_ref, sin_ref, wq_ref, wk_ref, wv_ref, q_ref, k_ref, v_ref):
    rows = xa_ref.shape[0]
    for half, x_ref in enumerate((xa_ref, xb_ref)):
        span = pl.ds(half * rows, rows)
        x = x_ref[...]
        place = pl.ds(pl.multiple_of((rank_ref[0] ^ (first + half)) * rows, rows), rows)
        cosine, sine = cos_ref[place, :], sin_ref[place, :]
        for w_ref, out_ref in ((wq_ref, q_ref), (wk_ref, k_ref)):
            full = mm(x, w_ref[...])
            for head in range(full.shape[1] // HEAD_DIM):
                lanes = slice(head * HEAD_DIM, (head + 1) * HEAD_DIM)
                out_ref[span, lanes] = turn(full[:, lanes], cosine, sine).astype(jnp.bfloat16)
        v_ref[span, :] = mm(x, wv_ref[...]).astype(jnp.bfloat16)


def qkv_pair(first, rank, xa, xb, cosine, sine, wq, wk, wv):
    rows, depth = xa.shape
    width = wq.shape[1]
    tile = 256
    wspec = pl.BlockSpec((depth, tile), lambda j, *_: (0, j))
    ospec = pl.BlockSpec((2 * rows, tile), lambda j, *_: (0, j))
    out = jax.ShapeDtypeStruct((2 * rows, width), jnp.bfloat16)
    return pl.pallas_call(
        functools.partial(qkv_body, first),
        grid_spec=pltpu.PrefetchScalarGridSpec(
            num_scalar_prefetch=1,
            grid=(width // tile,),
            in_specs=[whole(xa.shape)] * 2 + [whole(cosine.shape)] * 2 + [wspec] * 3,
            out_specs=[ospec] * 3,
        ),
        out_shape=[out] * 3,
        compiler_params=pltpu.CompilerParams(vmem_limit_bytes=60 << 20),
        cost_estimate=cost(
            flops=12 * rows * depth * width, bytes_accessed=6 * depth * width + 4 * rows * depth, transcendentals=0
        ),
        name="qkv",
    )(rank, xa, xb, cosine, sine, wq, wk, wv)


def in_order(rank_ref, near_ref, far_ref, out_ref):
    piece = near_ref.shape[0] // 2
    for index in range(4):
        src = (near_ref, far_ref)[index // 2]
        at = pl.multiple_of((rank_ref[0] ^ index) * piece, piece)
        out_ref[pl.ds(at, piece), :] = src[pl.ds((index % 2) * piece, piece), :]


def out_of_order(rank_ref, src_ref, near_ref, far_ref):
    piece = near_ref.shape[0] // 2
    for index in range(4):
        dst = (near_ref, far_ref)[index // 2]
        at = pl.multiple_of((rank_ref[0] ^ index) * piece, piece)
        dst[pl.ds((index % 2) * piece, piece), :] = src_ref[pl.ds(at, piece), :].astype(dst.dtype)


def attend_body(rank_ref, qn, qf, kn, kf, vn, vf, low_ref, high_ref, on, of, lse_ref, q_s, k_s, v_s, o_s):
    in_order(rank_ref, qn, qf, q_s)
    in_order(rank_ref, kn, kf, k_s)
    in_order(rank_ref, vn, vf, v_s)
    scale = HEAD_DIM ** (-0.5)
    v_t = v_s[...].T
    for block in range(q_s.shape[0] // QTILE):
        span = pl.ds(block * QTILE, QTILE)
        end = (block + 1) * QTILE
        scores = mm(k_s[:end, :], q_s[span, :], NT)
        at = lax.broadcasted_iota(jnp.int32, scores.shape, 0)
        allowed = (at >= low_ref[:, span]) & (at <= high_ref[:, span])
        scores = jnp.where(allowed, scores * scale, masked_score)
        top = jnp.max(scores, axis=0, keepdims=True)
        prob = jnp.exp(scores - top)
        total = jnp.sum(prob, axis=0, keepdims=True)
        lse_ref[0, :, span] = top + jnp.log(total)
        out_t = mm(v_t[:, :end], prob.astype(jnp.bfloat16)) * (1.0 / total)
        o_s[span, :] = out_t.T
    out_of_order(rank_ref, o_s, on, of)


def attend(rank, qs, ks, vs, low, high):
    half, width = qs[0].shape
    rows = 2 * half
    heads = width // HEAD_DIM
    hspec = pl.BlockSpec((half, HEAD_DIM), lambda h, *_: (0, h))
    row = whole((1, rows))
    return pl.pallas_call(
        attend_body,
        grid_spec=pltpu.PrefetchScalarGridSpec(
            num_scalar_prefetch=1,
            grid=(heads,),
            in_specs=[hspec] * 6 + [row] * 2,
            out_specs=[hspec] * 2 + [pl.BlockSpec((1, 1, rows), lambda h, *_: (h, 0, 0))],
            scratch_shapes=[pltpu.VMEM((rows, HEAD_DIM), jnp.bfloat16)] * 3 + [pltpu.VMEM((rows, HEAD_DIM), jnp.float32)],
        ),
        out_shape=[jax.ShapeDtypeStruct((half, width), jnp.bfloat16)] * 2
        + [jax.ShapeDtypeStruct((heads, 1, rows), jnp.float32)],
        compiler_params=pltpu.CompilerParams(vmem_limit_bytes=60 << 20),
        cost_estimate=cost(
            flops=8 * rows * rows * width, bytes_accessed=8 * rows * width, transcendentals=heads * rows * rows // 2
        ),
        name="attend",
    )(rank, *qs, *ks, *vs, low, high)


def attend_back_body(
    rank_ref, qn, qf, kn, kf, vn, vf, gn, gf, low_ref, high_ref, lse_ref, cos_ref, sin_ref,
    dqn, dqf, dkn, dkf, dvn, dvf, q_s, k_s, v_s, g_s, dq_s, dk_s, dv_s,
):
    in_order(rank_ref, qn, qf, q_s)
    in_order(rank_ref, kn, kf, k_s)
    in_order(rank_ref, vn, vf, v_s)
    in_order(rank_ref, gn, gf, g_s)
    scale = HEAD_DIM ** (-0.5)
    k_t = k_s[...].T
    blocks = q_s.shape[0] // QTILE
    for block in reversed(range(blocks)):
        span = pl.ds(block * QTILE, QTILE)
        end = (block + 1) * QTILE
        query, grad = q_s[span, :], g_s[span, :]
        scores = mm(k_s[:end, :], query, NT) * scale
        at = lax.broadcasted_iota(jnp.int32, scores.shape, 0)
        allowed = (at >= low_ref[:, span]) & (at <= high_ref[:, span])
        prob = jnp.exp(jnp.where(allowed, scores, masked_score) - lse_ref[0, :, span])
        d_prob = mm(v_s[:end, :], grad, NT)
        dot = jnp.sum(prob * d_prob, axis=0, keepdims=True)
        d_score = (prob * (d_prob - dot) * scale).astype(jnp.bfloat16)
        dq_s[span, :] = mm(k_t[:, :end], d_score).T
        d_key = mm(d_score, query)
        d_value = mm(prob.astype(jnp.bfloat16), grad)
        if block == blocks - 1:
            dk_s[...] = d_key
            dv_s[...] = d_value
        else:
            dk_s[:end, :] += d_key
            dv_s[:end, :] += d_value
    dq_s[...] = turn(dq_s[...], cos_ref[...], sin_ref[...])
    dk_s[...] = turn(dk_s[...], cos_ref[...], sin_ref[...])
    out_of_order(rank_ref, dq_s, dqn, dqf)
    out_of_order(rank_ref, dk_s, dkn, dkf)
    out_of_order(rank_ref, dv_s, dvn, dvf)


def attend_back(rank, qs, ks, vs, gs, low, high, lse, cosine, back_sine):
    half, width = qs[0].shape
    rows = 2 * half
    heads = width // HEAD_DIM
    hspec = pl.BlockSpec((half, HEAD_DIM), lambda h, *_: (0, h))
    row = whole((1, rows))
    return pl.pallas_call(
        attend_back_body,
        grid_spec=pltpu.PrefetchScalarGridSpec(
            num_scalar_prefetch=1,
            grid=(heads,),
            in_specs=[hspec] * 8
            + [row] * 2
            + [pl.BlockSpec((1, 1, rows), lambda h, *_: (h, 0, 0))]
            + [whole((rows, HEAD_DIM))] * 2,
            out_specs=[hspec] * 6,
            scratch_shapes=[pltpu.VMEM((rows, HEAD_DIM), jnp.bfloat16)] * 4
            + [pltpu.VMEM((rows, HEAD_DIM), jnp.float32)] * 3,
        ),
        out_shape=[jax.ShapeDtypeStruct((half, width), jnp.bfloat16)] * 6,
        compiler_params=pltpu.CompilerParams(vmem_limit_bytes=60 << 20),
        cost_estimate=cost(
            flops=20 * rows * rows * width, bytes_accessed=16 * rows * width, transcendentals=heads * rows * rows // 2
        ),
        name="attend_back",
    )(rank, *qs, *ks, *vs, *gs, low, high, lse, cosine, back_sine)


def mlp_body(xa_ref, xb_ref, dm_ref, wg_ref, wu_ref, mid_ref, dg_ref, du_ref):
    rows = xa_ref.shape[0]
    for half, x_ref in enumerate((xa_ref, xb_ref)):
        span = pl.ds(half * rows, rows)
        x = x_ref[...]
        gate = mm(x, wg_ref[...])
        up = mm(x, wu_ref[...])
        d_mid = dm_ref[span, :]
        sigma = 1.0 / (1.0 + jnp.exp(-gate))
        active = gate * sigma
        mid_ref[span, :] = (active * up).astype(jnp.bfloat16)
        dg_ref[span, :] = (d_mid * up * sigma * (1.0 + gate * (1.0 - sigma))).astype(jnp.bfloat16)
        du_ref[span, :] = (d_mid * active).astype(jnp.bfloat16)


def mlp_pair(xa, xb, d_mid, wg, wu):
    rows, depth = xa.shape
    width = wg.shape[1]
    tile = 256
    wspec = pl.BlockSpec((depth, tile), lambda j: (0, j))
    ospec = pl.BlockSpec((2 * rows, tile), lambda j: (0, j))
    return pl.pallas_call(
        mlp_body,
        grid=(pl.cdiv(width, tile),),
        in_specs=[whole(xa.shape)] * 2 + [ospec] + [wspec] * 2,
        out_specs=[ospec] * 3,
        out_shape=[jax.ShapeDtypeStruct((2 * rows, width), jnp.bfloat16)] * 3,
        compiler_params=pltpu.CompilerParams(vmem_limit_bytes=60 << 20),
        cost_estimate=cost(
            flops=8 * rows * depth * width,
            bytes_accessed=4 * depth * width + 4 * rows * depth + 20 * rows * width,
            transcendentals=2 * rows * width,
        ),
        name="mlp",
    )(xa, xb, d_mid, wg, wu)


def gather_rows(parts, out_ref):
    at = 0
    for part in parts:
        out_ref[at : at + part.shape[0], :] = part[...]
        at += part.shape[0]


def gather_sides(rights, out_ref):
    at = 0
    for near, far in zip(rights[::2], rights[1::2]):
        rows, width = near.shape
        out_ref[:rows, at : at + width] = near[...]
        out_ref[rows:, at : at + width] = far[...]
        at += width


def block_at(place, low, side):
    return place // low * (2 * low) + place % low + low * side


def filled(step, low, side):
    group, half = step // (2 * low), step // low % 2
    here = jnp.where(half == side, step % low, jnp.where(half > side, low - 1, -1))
    return jnp.maximum(group * low + here, 0)


def grad_body(pieces, widths, low, sides, rank_ref, *refs):
    left, rights = refs[:pieces], refs[pieces : pieces + 2 * len(widths)]
    outs, (left_s, right_s) = refs[pieces + 2 * len(widths) : -2], refs[-2:]
    step = pl.program_id(0)

    @pl.when(step == 0)
    def _():
        gather_sides(rights, right_s)

    gather_rows(left, left_s)
    total = mm(left_s[...], right_s[...], TN).astype(jnp.bfloat16)

    def store(refs):
        at = 0
        for ref, width in zip(refs, widths):
            ref[0] = total[:, at : at + width]
            at += width

    if len(sides) == 1:
        store(outs)
    else:
        sent = step // low % 2 != rank_ref[0] // low % 2
        pl.when(sent)(lambda: store(outs[: len(widths)]))
        pl.when(jnp.logical_not(sent))(lambda: store(outs[len(widths) :]))


def grad_call(rank, pieces, mats, low, sides, tile):
    rows, depth = pieces[0].shape[0] * len(pieces), pieces[0].shape[1]
    widths = [near.shape[1] for near, _ in mats]
    width, half = sum(widths), depth // tile // 2
    count = half * len(sides)

    def own(s, side):
        bit = s[0] // low % 2
        return 1 - bit if side else bit

    if len(sides) == 1:
        lspec = pl.BlockSpec((pieces[0].shape[0], tile), lambda j, s: (0, block_at(j, low, own(s, sides[0]))))
    else:
        lspec = pl.BlockSpec((pieces[0].shape[0], tile), lambda j, s: (0, j))
    out_specs = []
    for side in sides:
        for w in widths:
            if len(sides) == 1:
                out_specs.append(pl.BlockSpec((1, tile, w), lambda j, s: (j, 0, 0)))
            else:
                out_specs.append(pl.BlockSpec((1, tile, w), lambda j, s, side=side: (filled(j, low, own(s, side)), 0, 0)))
    rights = [part for mat in mats for part in mat]
    return pl.pallas_call(
        functools.partial(grad_body, len(pieces), widths, low, sides),
        grid_spec=pltpu.PrefetchScalarGridSpec(
            num_scalar_prefetch=1,
            grid=(count,),
            in_specs=[lspec] * len(pieces) + [whole(r.shape) for r in rights],
            out_specs=out_specs,
            scratch_shapes=[pltpu.VMEM((rows, tile), jnp.bfloat16), pltpu.VMEM((rows, width), jnp.bfloat16)],
        ),
        out_shape=[jax.ShapeDtypeStruct((half, tile, w), jnp.bfloat16) for _ in sides for w in widths],
        compiler_params=pltpu.CompilerParams(vmem_limit_bytes=60 << 20),
        cost_estimate=cost(
            flops=2 * rows * tile * count * width,
            bytes_accessed=2 * rows * (tile * count + width) + 2 * tile * count * width,
            transcendentals=0,
        ),
        name="weight_grad",
    )(rank, *pieces, *rights)


def merge_body(_, own_away, got_away, own_kept, got_kept, away_ref, kept_ref):
    away_ref[...] = (own_away[...].astype(jnp.float32) + got_away[...].astype(jnp.float32)).astype(jnp.bfloat16)
    kept_ref[...] = (own_kept[...].astype(jnp.float32) + got_kept[...].astype(jnp.float32)).astype(jnp.bfloat16)


def merge_call(rank, own, got, low, bit):
    count, tile, width = own.shape
    away, kept = (
        pl.BlockSpec((1, tile, width), lambda j, s, flip=flip: (block_at(j, low, (s[0] // bit + flip) % 2), 0, 0))
        for flip in (1, 0)
    )
    ospec = pl.BlockSpec((1, tile, width), lambda j, s: (j, 0, 0))
    return pl.pallas_call(
        merge_body,
        grid_spec=pltpu.PrefetchScalarGridSpec(
            num_scalar_prefetch=1,
            grid=(count // 2,),
            in_specs=[away, away, kept, kept],
            out_specs=[ospec] * 2,
        ),
        out_shape=[jax.ShapeDtypeStruct((count // 2, tile, width), jnp.bfloat16)] * 2,
        compiler_params=pltpu.CompilerParams(vmem_limit_bytes=40 << 20),
        cost_estimate=cost(flops=count * tile * width, bytes_accessed=6 * count * tile * width, transcendentals=0),
        name="merge",
    )(rank, own, got, own, got)


def product(lefts, weights, half, rows):
    total = None
    for left, (w_ref, dims) in zip(lefts, weights):
        value = mm(left[half][...] if len(left) == 2 else left[0][pl.ds(half * rows, rows), :], w_ref[...], dims)
        total = value if total is None else total + value
    return total


def project_body(terms, *refs):
    at, lefts, weights = 0, [], []
    for pieces, dims in terms:
        lefts.append(refs[at : at + pieces])
        weights.append((refs[at + pieces], dims))
        at += pieces + 1
    out_ref = refs[at]
    rows = out_ref.shape[0] // 2
    for half in range(2):
        span = pl.ds(half * rows, rows)
        out_ref[span, :] = product(lefts, weights, half, rows).astype(out_ref.dtype)


def terms_of(terms):
    return [(left if isinstance(left, tuple) else (left,), w, NT if flip else NN) for left, w, flip in terms]


def term_specs(terms, tile):
    in_specs, args = [], []
    for left, w, dims in terms:
        depth = left[0].shape[1]
        in_specs += [whole(piece.shape) for piece in left]
        in_specs.append(
            pl.BlockSpec((tile, depth), lambda j: (j, 0)) if dims is NT else pl.BlockSpec((depth, tile), lambda j: (0, j))
        )
        args += [*left, w]
    return in_specs, args


def project(terms, dtype=jnp.bfloat16):
    terms = terms_of(terms)
    rows = sum(piece.shape[0] for piece in terms[0][0])
    width = terms[0][1].shape[0 if terms[0][2] is NT else 1]
    tile = min(512, width)
    in_specs, args = term_specs(terms, tile)
    return pl.pallas_call(
        functools.partial(project_body, [(len(left), dims) for left, _, dims in terms]),
        grid=(pl.cdiv(width, tile),),
        in_specs=in_specs,
        out_specs=pl.BlockSpec((rows, tile), lambda j: (0, j)),
        out_shape=jax.ShapeDtypeStruct((rows, width), dtype),
        compiler_params=pltpu.CompilerParams(vmem_limit_bytes=60 << 20),
        cost_estimate=cost(
            flops=2 * rows * width * sum(left[0].shape[1] for left, _, _ in terms),
            bytes_accessed=sum(2 * a.size for a in args) + 2 * rows * width,
            transcendentals=0,
        ),
        name="project",
    )(*args)


def pair_body(terms, steps, *refs):
    at, lefts, weights = 0, [], []
    for pieces, dims in terms:
        lefts.append(refs[at : at + pieces])
        weights.append((refs[at + pieces], dims))
        at += pieces + 1
    out_ref, mine_s, away_s, got_s, send_sem, recv_sem = refs[at:]
    rows = out_ref.shape[0]
    tile = mine_s.shape[2]
    step = pl.program_id(0)
    me = lax.axis_index("tensor")
    mate = {"tensor": me + 1 - 2 * (me % 2)}

    @pl.when(step == 0)
    def _():
        barrier = pltpu.get_barrier_semaphore()
        pl.semaphore_signal(barrier, inc=1, device_id=mate, device_id_type=pl.DeviceIdType.MESH)
        pl.semaphore_wait(barrier, 1)

    def copy(index):
        return pltpu.make_async_remote_copy(
            src_ref=away_s.at[index],
            dst_ref=got_s.at[index],
            send_sem=send_sem.at[index],
            recv_sem=recv_sem.at[index],
            device_id=mate,
            device_id_type=pl.DeviceIdType.MESH,
        )

    away_s[step] = product(lefts, weights, 1, rows).astype(jnp.bfloat16)
    copy(step).start()
    mine_s[step] = product(lefts, weights, 0, rows)

    @pl.when(step == steps - 1)
    def _():
        for index in range(steps):
            copy(index).wait()
            total = mine_s[index] + got_s[index].astype(jnp.float32)
            out_ref[:, index * tile : (index + 1) * tile] = total.astype(out_ref.dtype)


def pair_sum(terms, ident, dtype):
    terms = terms_of(terms)
    rows = sum(piece.shape[0] for piece in terms[0][0]) // 2
    width = terms[0][1].shape[0 if terms[0][2] is NT else 1]
    tile = min(512, width)
    steps = width // tile
    in_specs, args = term_specs(terms, tile)
    return pl.pallas_call(
        functools.partial(pair_body, [(len(left), dims) for left, _, dims in terms], steps),
        grid=(steps,),
        in_specs=in_specs,
        out_specs=whole((rows, width)),
        out_shape=jax.ShapeDtypeStruct((rows, width), dtype),
        scratch_shapes=[
            pltpu.VMEM((steps, rows, tile), jnp.float32),
            pltpu.VMEM((steps, rows, tile), jnp.bfloat16),
            pltpu.VMEM((steps, rows, tile), jnp.bfloat16),
            pltpu.SemaphoreType.DMA((steps,)),
            pltpu.SemaphoreType.DMA((steps,)),
        ],
        compiler_params=pltpu.CompilerParams(vmem_limit_bytes=60 << 20, collective_id=ident),
        cost_estimate=cost(
            flops=4 * rows * width * sum(left[0].shape[1] for left, _, _ in terms),
            bytes_accessed=sum(2 * a.size for a in args) + 4 * rows * width,
            transcendentals=0,
        ),
        name="pair_sum",
    )(*args)


def partner(axis, bit):
    rank = lax.axis_index(axis)
    return {axis: rank + bit - 2 * bit * (rank // bit % 2)}


def last_body(ones, twos, threes, *refs):
    mats = ones + twos + threes
    away, kept, refs = refs[:mats], refs[mats : 2 * mats], refs[2 * mats :]
    ready_ref, got_ref, gains_ref, refs = refs[0], refs[1], refs[2], refs[3:]
    outs, done_ref, sums_ref, refs = refs[:mats], refs[mats], refs[mats + 1], refs[mats + 2 :]
    own, first, refs = refs[:mats], refs[mats : 2 * mats], refs[2 * mats :]
    held, to_z, from_z, refs = refs[:threes], refs[threes : 2 * threes], refs[2 * threes : 3 * threes], refs[3 * threes :]
    late = twos + threes
    to_last, from_last, total_s, refs = refs[:late], refs[late : 2 * late], refs[2 * late : 2 * late + twos], refs[2 * late + twos :]
    gain_in, gain_out, load_sem, send_sem, recv_sem = refs
    rank = lax.axis_index("dp")
    z1, z2 = rank // 2 % 2, rank // 4 % 2
    hops = [("tensor", 1), ("tensor", 2), ("dp", 1), ("dp", 2), ("dp", 4)]
    copies = []

    barrier = pltpu.get_barrier_semaphore()
    for axis, bit in hops:
        pl.semaphore_signal(barrier, inc=1, device_id=partner(axis, bit), device_id_type=pl.DeviceIdType.MESH)
    pl.semaphore_wait(barrier, len(hops))

    def send(src, dst, axis, bit):
        index = len(copies)
        copy = pltpu.make_async_remote_copy(
            src_ref=src,
            dst_ref=dst,
            send_sem=send_sem.at[index],
            recv_sem=recv_sem.at[index],
            device_id=partner(axis, bit),
            device_id_type=pl.DeviceIdType.MESH,
        )
        copy.start()
        copies.append(copy)
        return copy

    def side(bit, flip):
        return 1 - bit if flip else bit

    stage = {}
    gain_out[0] = gains_ref[...]
    stage["gains"] = send(gain_out.at[0], gain_in.at[0], *hops[0])

    def gain_hop(index):
        stage["gains"].wait_recv()
        total = gain_out[index] + gain_in[index]
        if index + 1 < len(hops):
            gain_out[index + 1] = total
            stage["gains"] = send(gain_out.at[index + 1], gain_in.at[index + 1], *hops[index + 1])
        else:
            sums_ref[...] = total

    for m in range(ones, ones + twos):
        for c in (1, 0):
            stage[m, "z", c] = send(away[m].at[side(z2, c)], first[m].at[c], "dp", 2)
    pieces = 4
    tile = own[0].shape[1] // pieces

    def send_piece(m, index):
        rows = pl.ds(index * tile, tile)
        stage[m, "piece", index] = send(away[m].at[0, rows, :], first[m].at[0, rows, :], "dp", 4)

    send_piece(0, 0)

    def send_all(m):
        for a in (1, 0):
            for c in (1, 0):
                stage[m, a, c] = send(away[m].at[side(z1, a) + 2 * side(z2, c)], first[m].at[2 * a + c], "dp", 1)

    loads = [pltpu.make_async_copy(kept[m], own[m], load_sem.at[m]) for m in range(mats)]
    for load in loads:
        load.start()
    send_all(ones + twos)
    gain_hop(0)
    gain_hop(1)
    for m in range(ones + twos + 1, mats):
        send_all(m)
    for load in loads:
        load.wait()

    def wide(value):
        return value.astype(jnp.float32)

    def from_x(m, a, c):
        stage[m, a, c].wait_recv()
        total = wide(own[m][side(z1, a) + 2 * side(z2, c)]) + wide(first[m][2 * a + c])
        i = m - ones - twos
        if a:
            to_z[i][c] = total.astype(jnp.bfloat16)
            stage[m, "z", c] = send(to_z[i].at[c], from_z[i].at[c], "dp", 2)
        else:
            held[i][c] = total

    def from_near(m, c):
        stage[m, "z", c].wait_recv()
        if m < ones + twos:
            total = wide(own[m][side(z2, c)]) + wide(first[m][c])
            dst = total_s[m - ones]
        else:
            total = held[m - ones - twos][c] + wide(from_z[m - ones - twos][c])
            dst = outs[m]
        if c:
            to_last[m - ones][...] = total.astype(jnp.bfloat16)
            stage[m, "last"] = send(to_last[m - ones], from_last[m - ones], "dp", 4)
        else:
            dst[...] = total

    def finish(m):
        if m < ones:
            for index in range(pieces):
                stage[m, "piece", index].wait_recv()
        else:
            stage[m, "last"].wait_recv()
        if m < ones:
            outs[m][...] = wide(own[m][0]) + wide(first[m][0])
        elif m < ones + twos:
            outs[m][...] = (total_s[m - ones][...] + wide(from_last[m - ones][...])).T
        else:
            outs[m][...] += wide(from_last[m - ones][...])

    up, out, q, k, v = range(5)
    from_near(out, 1)
    from_x(q, 1, 1)
    from_x(q, 1, 0)
    from_near(out, 0)
    send_piece(up, 1)
    from_x(q, 0, 1)
    from_x(q, 0, 0)
    done_ref[...] = (wide(ready_ref[0]) + wide(got_ref[0])).T
    from_x(k, 1, 1)
    from_near(q, 1)
    from_x(k, 1, 0)
    from_near(q, 0)
    send_piece(up, 2)
    from_x(k, 0, 1)
    from_x(k, 0, 0)
    gain_hop(2)
    from_x(v, 1, 1)
    from_near(k, 1)
    send_piece(up, 3)
    from_x(v, 1, 0)
    from_near(k, 0)
    gain_hop(3)
    finish(up)
    from_x(v, 0, 1)
    from_x(v, 0, 0)
    finish(out)
    from_near(v, 1)
    from_near(v, 0)
    gain_hop(4)
    for m in (q, k, v):
        finish(m)
    for copy in copies:
        copy.wait_send()


def last_stages(ones, twos, threes, ready, gains):
    mats = [*ones, *twos, *threes]
    away, kept = [m[0] for m in mats], [m[1] for m in mats]
    shapes = [a.shape for a in away]
    low, wide = jnp.bfloat16, jnp.float32
    late, last = shapes[len(ones) + len(twos) :], shapes[len(ones) :]
    flat = [shape[1:] for shape in shapes]
    for m in range(len(ones), len(ones) + len(twos)):
        flat[m] = flat[m][::-1]
    any_space = pl.BlockSpec(memory_space=pl.ANY)
    inside = pl.BlockSpec(memory_space=pltpu.VMEM)
    count = 4 * len(ones) + 3 * len(twos) + 7 * len(threes) + 5
    result = pl.pallas_call(
        functools.partial(last_body, len(ones), len(twos), len(threes)),
        in_specs=[any_space] * (2 * len(mats)) + [inside] * 3,
        out_specs=[inside] * (len(mats) + 2),
        out_shape=[jax.ShapeDtypeStruct(shape, wide) for shape in flat]
        + [jax.ShapeDtypeStruct(ready[0].shape[:0:-1], wide), jax.ShapeDtypeStruct(gains.shape, wide)],
        scratch_shapes=[pltpu.VMEM(shape, low) for shape in shapes]
        + [pltpu.VMEM(shape, low) for shape in shapes]
        + [pltpu.VMEM((2,) + shape[1:], wide) for shape in late]
        + [pltpu.VMEM((2,) + shape[1:], low) for shape in late]
        + [pltpu.VMEM((2,) + shape[1:], low) for shape in late]
        + [pltpu.VMEM(shape[1:], low) for shape in last]
        + [pltpu.VMEM(shape[1:], low) for shape in last]
        + [pltpu.VMEM(shape[1:], wide) for shape in last[: len(twos)]]
        + [pltpu.VMEM((5,) + gains.shape, wide)] * 2
        + [pltpu.SemaphoreType.DMA((len(mats),)), pltpu.SemaphoreType.DMA((count,)), pltpu.SemaphoreType.DMA((count,))],
        compiler_params=pltpu.CompilerParams(vmem_limit_bytes=62 << 20, collective_id=8),
        cost_estimate=cost(flops=1 << 24, bytes_accessed=1 << 25, transcendentals=0),
        name="last_stages",
    )(*away, *kept, *ready, gains)
    return result[:-2], result[-2], result[-1]


def row_tables(length_row, group_row, mask_row):
    starts = jnp.cumsum(length_row) - length_row
    token = jnp.arange(ROWS, dtype=jnp.int32)
    doc_index = jnp.sum((token[:, None] >= starts[None, 1:]).astype(jnp.int32), axis=1)
    onehot = doc_index[:, None] == jnp.arange(DOCS, dtype=jnp.int32)[None, :]
    first = jnp.sum(jnp.where(onehot, starts[None, :], 0), axis=1)
    group_tok = jnp.sum(jnp.where(onehot, group_row[None, :], 0), axis=1)
    real = jnp.sum(jnp.where(onehot, mask_row[:, None], 0), axis=0)
    last_real = first + jnp.sum(jnp.where(onehot, real[None, :], 0), axis=1) - 1
    return (token - first, first, jnp.minimum(token, last_real), group_tok)


def rope_tables(inside):
    freq = rope_base ** (-jnp.arange(0, HEAD_DIM // 2, dtype=jnp.float32) * 2.0 / HEAD_DIM)
    angle = inside.astype(jnp.float32)[:, None] * freq[None, :]
    cosine, sine = jnp.cos(angle), jnp.sin(angle)
    return (
        jnp.concatenate([cosine, cosine], axis=-1),
        jnp.concatenate([-sine, sine], axis=-1),
        jnp.concatenate([sine, -sine], axis=-1),
    )


def rows_dot(left, right):
    return jnp.dot(left, right, preferred_element_type=jnp.float32)


def rows_dot_t(left, right):
    return lax.dot_general(left, right, NT, preferred_element_type=jnp.float32)


def exchange(values, axis, bit):
    size = lax.axis_size(axis)
    return lax.ppermute(values, axis, [(rank, rank ^ bit) for rank in range(size)])


def butterfly_sum(values, axis):
    size = lax.axis_size(axis)
    bit = 1
    while bit < size:
        values = values + exchange(values, axis, bit)
        bit *= 2
    return values


def tie(*values):
    return lax.optimization_barrier(values)


def scatter_small(values, axis):
    size = lax.axis_size(axis)
    rank = lax.axis_index(axis)
    kept = values
    bit = 1
    while bit < size:
        pairs = kept.reshape((kept.shape[0], kept.shape[1] // 2, 2) + kept.shape[2:])
        side = (rank // bit) % 2
        own = lax.dynamic_index_in_dim(pairs, side, axis=2, keepdims=False)
        away = lax.dynamic_index_in_dim(pairs, 1 - side, axis=2, keepdims=False)
        kept = own + exchange(away, axis, bit)
        bit *= 2
    return kept[:, 0]


class WeightGrad:
    def __init__(self, rank, pieces, mats, start=1):
        self.rank, self.pieces, self.mats, self.start = rank, pieces, mats, start
        self.size = lax.axis_size("dp")
        self.tile = pieces[0].shape[1] // self.size
        self.kernel = self.tile % 128 == 0

    def bits(self):
        return [2**i for i in range(self.size.bit_length() - 1)]

    def compute(self, *sides):
        if self.kernel:
            outs = grad_call(self.rank, self.pieces, self.mats, self.start, sides, self.tile)
        else:
            left = jnp.concatenate(self.pieces, axis=0)
            place = jnp.arange(self.size // 2, dtype=jnp.int32)
            bit = self.rank[0] // self.start % 2
            fulls = [
                lax.dot_general(left, jnp.concatenate(mat, axis=0), TN, preferred_element_type=jnp.float32)
                .astype(jnp.bfloat16)
                .reshape(self.size, self.tile, -1)
                for mat in self.mats
            ]
            outs = [
                jnp.take(full, block_at(place, self.start, (bit + side) % 2), axis=0) for side in sides for full in fulls
            ]
        return tuple(outs)


class Halving:
    def __init__(self, rank, own, start=1):
        self.rank, self.kept = rank, own
        self.size = lax.axis_size("dp")
        self.left = [2**i for i in range(self.size.bit_length() - 1) if 2**i != start]

    def merge(self, got, bit):
        low = 2 ** self.left.index(bit)
        self.left.remove(bit)
        if got.shape[1] % 128 == 0:
            away, self.kept = merge_call(self.rank, self.kept, got, low, bit)
            return away
        total = self.kept.astype(jnp.float32) + got.astype(jnp.float32)
        place = jnp.arange(total.shape[0] // 2, dtype=jnp.int32)
        side = self.rank[0] // bit % 2
        self.kept = jnp.take(total, block_at(place, low, side), axis=0)
        return jnp.take(total, block_at(place, low, 1 - side), axis=0).astype(jnp.bfloat16)

    def finish(self, got):
        while self.left:
            bit = self.left[0]
            got = exchange(self.merge(got, bit), "dp", bit)
        return (self.kept.astype(jnp.float32) + got.astype(jnp.float32))[0]


def hop(values, bit):
    return exchange(values, "dp", bit)


def shards(
    hidden_in,
    cotangent,
    gain_attn,
    w_query,
    w_key,
    w_value,
    w_out,
    gain_mlp,
    w_gate,
    w_up,
    w_down,
    doc_lengths,
    doc_groups,
    pad_mask,
):
    rows_local = hidden_in.shape[0]
    rank = lax.axis_index("tensor").astype(jnp.int32)
    rank_ref = rank[None]
    dp_rank = lax.axis_index("dp").astype(jnp.int32)[None]

    def to_far(values):
        return exchange(values, "tensor", 2)

    def to_mate(values):
        return exchange(values, "tensor", 1)

    x_f = hidden_in.astype(jnp.float32)
    inv_a = lax.rsqrt(jnp.mean(x_f * x_f, axis=-1, keepdims=True) + epsilon)
    a0 = (x_f * inv_a * gain_attn).astype(jnp.bfloat16)
    a2 = to_far(a0)
    a1 = to_mate(a0)
    a3 = to_mate(a2)

    inside, low, high, group_tok = row_tables(doc_lengths[0], doc_groups[0], pad_mask[0])
    low, high = low[None], high[None]
    real_tok = pad_mask[0].astype(jnp.float32)
    onehot_g = group_tok[:, None] == jnp.arange(GROUPS, dtype=jnp.int32)[None, :]
    counts = butterfly_sum(jnp.sum(jnp.where(onehot_g, real_tok[:, None], 0.0), axis=0), "dp")
    live = jnp.sum(counts)
    group_scale = jnp.sqrt(live / (GROUPS * jnp.maximum(counts, 1.0)))
    token_weight = real_tok * jnp.sum(jnp.where(onehot_g, group_scale[None, :], 0.0), axis=-1)
    weight_local = lax.dynamic_slice_in_dim(token_weight, rank * rows_local, rows_local)
    c0 = (cotangent.astype(jnp.float32) * weight_local[:, None]).astype(jnp.bfloat16)
    cosine, sine, back_sine = rope_tables(inside)

    near = qkv_pair(0, rank_ref, a0, a1, cosine, sine, w_query, w_key, w_value)
    a2, c0, *near = tie(a2, c0, *near)
    a3 = to_mate(a2)
    c2 = to_far(c0)
    c1 = to_mate(c0)
    far = qkv_pair(2, rank_ref, a2, a3, cosine, sine, w_query, w_key, w_value)
    qs, ks, vs = zip(near, far)
    heads_near, heads_far, lse = attend(rank_ref, qs, ks, vs, low, high)
    y1 = pair_sum([(heads_far, w_out, False)], 0, jnp.bfloat16)
    heads_n, c1, c2, y1 = tie(heads_near, c1, c2, y1)
    got = to_far(y1)
    c3 = to_mate(c2)
    mine = pair_sum([(heads_n, w_out, False)], 1, jnp.float32)
    dm_near = project([((c0, c1), w_down, True)], jnp.float32)
    dm_far = project([((c2, c3), w_down, True)], jnp.float32)
    got, dm_near, dm_far, mine = tie(got, dm_near, dm_far, mine)
    mid_h = x_f + mine + got.astype(jnp.float32)
    inv_b = lax.rsqrt(jnp.mean(mid_h * mid_h, axis=-1, keepdims=True) + epsilon)
    b0 = (mid_h * inv_b * gain_mlp).astype(jnp.bfloat16)
    b2 = to_far(b0)
    b1 = to_mate(b0)
    mid_near, dg_near, du_near = mlp_pair(b0, b1, dm_near, w_gate, w_up)
    mine8 = pair_sum([(mid_near, w_down, False)], 5, jnp.float32)
    b2, mid_near, dg_near, du_near, mine8 = tie(b2, mid_near, dg_near, du_near, mine8)
    b3 = to_mate(b2)
    mid_far, dg_far, du_far = mlp_pair(b2, b3, dm_far, w_gate, w_up)

    half = lax.axis_size("dp") // 2
    b_all, c_all = (b0, b1, b2, b3), (c0, c1, c2, c3)
    grad_down = WeightGrad(dp_rank, c_all, [(mid_near, mid_far)])
    grad_gate = WeightGrad(dp_rank, b_all, [(dg_near, dg_far)], 2)
    (down_send,) = grad_down.compute(1)
    dg_f, du_f, down_send = tie(dg_far, du_far, down_send)
    down_got = hop(down_send, 1)
    (gate_send,) = grad_gate.compute(1)
    gate_got = hop(gate_send, 2)
    y5 = pair_sum([(dg_f, w_gate, True), (du_f, w_up, True)], 2, jnp.bfloat16)
    dg_n, du_n, mid_n, y5 = tie(dg_near, du_near, mid_near, y5)
    got = to_far(y5)
    d_b = pair_sum([(dg_n, w_gate, True), (du_n, w_up, True)], 3, jnp.float32) + got.astype(jnp.float32)
    (up_send,) = WeightGrad(dp_rank, b_all, [(du_n, du_far)]).compute(1)
    (down_own,) = WeightGrad(dp_rank, c_all, [(mid_n, mid_far)]).compute(0)
    d_b, up_send, down_got, down_own = tie(d_b, up_send, down_got, down_own)
    up_got = hop(up_send, 1)
    down = Halving(dp_rank, down_own)
    down_got = hop(down.merge(down_got, 2), 2)

    n_b = mid_h * inv_b
    gain_mlp_part = jnp.sum(d_b * n_b, axis=0)
    e_b = d_b * gain_mlp
    weighted = cotangent.astype(jnp.float32) * weight_local[:, None]
    d_h = weighted + inv_b * (e_b - n_b * jnp.mean(e_b * n_b, axis=-1, keepdims=True))
    t0 = d_h.astype(jnp.bfloat16)
    t0, mid_f, dg_n, du_n = tie(t0, mid_far, dg_near, du_near)
    t2 = to_far(t0)
    t1 = to_mate(t0)
    gs_near = project([((t0, t1), w_out, True)])
    y8 = pair_sum([(mid_f, w_down, False)], 4, jnp.bfloat16)
    (gate_own,) = WeightGrad(dp_rank, b_all, [(dg_n, dg_far)], 2).compute(0)
    t2, gate_got, gs_near, y8, gate_own = tie(t2, gate_got, gs_near, y8, gate_own)

    got8 = to_far(y8)
    gate = Halving(dp_rank, gate_own, 2)
    t3 = to_mate(t2)
    gs_far = project([((t2, t3), w_out, True)])
    gate_got = hop(gate.merge(gate_got, 1), 1)
    (up_own,) = WeightGrad(dp_rank, b_all, [(du_n, du_far)]).compute(0)
    out_send, out_own = WeightGrad(dp_rank, (t0, t1, t2, t3), [(heads_near, heads_far)]).compute(1, 0)
    gs_far, up_got, down_got, up_own, out_send = tie(gs_far, up_got, down_got, up_own, out_send)
    up = Halving(dp_rank, up_own)
    up_got = hop(up.merge(up_got, 2), 2)
    down_got = hop(down.merge(down_got, half), half)
    dqn, dqf, dkn, dkf, dvn, dvf = attend_back(
        rank_ref, qs, ks, vs, (gs_near, gs_far), low, high, lse, cosine, back_sine
    )
    dqf, dkf, dvf, got8, out_send = tie(dqf, dkf, dvf, got8, out_send)

    out_got = hop(out_send, 1)
    y7 = pair_sum([(dqf, w_query, True), (dkf, w_key, True), (dvf, w_value, True)], 6, jnp.bfloat16)
    got = to_far(y7)
    dqn, dkn, dvn, y7, up_got, gate_got, down_got = tie(dqn, dkn, dvn, y7, up_got, gate_got, down_got)
    gate_got = hop(gate.merge(gate_got, half), half)
    up_away = up.merge(up_got, half)
    grad_qkv = WeightGrad(dp_rank, (a0, a1, a2, a3), [(dqn, dqf), (dkn, dkf), (dvn, dvf)])
    *sends, q_own, k_own, v_own = grad_qkv.compute(1, 0)
    d_a = pair_sum([(dqn, w_query, True), (dkn, w_key, True), (dvn, w_value, True)], 7, jnp.float32) + got.astype(jnp.float32)
    d_a, out_got, gate_got, up_away, *sends = tie(d_a, out_got, gate_got, up_away, *sends)

    out = Halving(dp_rank, out_own)
    out_away = out.merge(out_got, 2)
    output = (mid_h + mine8 + got8.astype(jnp.float32)).astype(jnp.bfloat16)
    n_a = x_f * inv_a
    gain_attn_part = jnp.sum(d_a * n_a, axis=0)
    e_a = d_a * gain_attn
    grad_input = d_h + inv_a * (e_a - n_a * jnp.mean(e_a * n_a, axis=-1, keepdims=True))
    gains = jnp.stack([gain_attn_part, gain_mlp_part])
    sum_gate = gate.finish(gate_got)
    if grad_qkv.kernel and half == 4:
        (sum_up, sum_out, *sums), sum_down, gains = last_stages(
            [(up_away, up.kept)],
            [(out_away, out.kept)],
            list(zip(sends, (q_own, k_own, v_own))),
            (down.kept, down_got),
            gains,
        )
        gains = lax.dynamic_slice_in_dim(gains, dp_rank[0] * grad_qkv.tile, grad_qkv.tile, 1)
    else:
        gains = butterfly_sum(scatter_small(gains.reshape(2, lax.axis_size("dp"), -1), "dp"), "tensor")
        sum_up = up.finish(hop(up_away, half))
        sum_out = out.finish(hop(out_away, 2)).T
        sum_down = down.finish(down_got).T
        sums = [Halving(dp_rank, own).finish(hop(send, 1)) for send, own in zip(sends, (q_own, k_own, v_own))]
    return (
        output,
        grad_input,
        gains[0],
        sums[0],
        sums[1],
        sums[2],
        sum_out,
        gains[1],
        sum_gate,
        sum_up,
        sum_down,
    )


def solution(mesh):
    rows, columns, split = P(("dp", "tensor"), None), P(None, "tensor"), P("tensor", None)
    in_specs = (
        rows,
        rows,
        P(),
        columns,
        columns,
        columns,
        split,
        P(),
        columns,
        columns,
        split,
        P("dp", None),
        P("dp", None),
        P("dp", None),
    )
    grads = P("dp", "tensor")
    grads_t = P("tensor", "dp")
    out_specs = (rows, rows, P("dp"), grads, grads, grads, grads_t, P("dp"), grads, grads, grads_t)
    return jax.shard_map(shards, mesh=mesh, in_specs=in_specs, out_specs=out_specs, check_vma=False)
```
